128 devices in a mesh: dp: 64 (over z, y, x), tensor: 2 (over core).
Axes of the slice: x: 4, y: 4, z: 4, core: 2. Of those that a mesh axis runs over, the one named last changes fastest.
Arguments:
- tokens: bfloat16 [49152, 768], P(('dp', 'tensor')), may hold values from -6 to 6
- skip_tokens: bfloat16 [49152, 768], P(('dp', 'tensor')), may hold values from -6 to 6
- cot_back: bfloat16 [49152, 768], P(('dp', 'tensor')), may hold values from -6 to 6
- cot_head: bfloat16 [49152, 768], P(('dp', 'tensor')), may hold values from -6 to 6
- one_span: int32 [192], P('dp'), may hold values 0 or 1
- lower_qkv: bfloat16 [3, 768, 768], P(None, None, 'tensor'), may hold values from -0.21875 to 0.21875
- lower_proj: bfloat16 [768, 768], P('tensor'), may hold values from -1.75 to 1.75
- lower_gain_attn: float32 [768], replicated, may hold values from 0.1 to 1.9
- lower_shift_attn: float32 [768], replicated, may hold values from -1.5 to 1.5
- lower_w_in: bfloat16 [768, 3072], P(None, 'tensor'), may hold values from -0.21875 to 0.21875
- lower_w_out: bfloat16 [3072, 768], P('tensor'), may hold values from -0.15625 to 0.15625
- lower_gain_ffn: float32 [768], replicated, may hold values from 0.1 to 1.9
- lower_shift_ffn: float32 [768], replicated, may hold values from -1.5 to 1.5
- upper_qkv: bfloat16 [3, 768, 768], P(None, None, 'tensor'), may hold values from -0.21875 to 0.21875
- upper_proj: bfloat16 [768, 768], P('tensor'), may hold values from -1.75 to 1.75
- upper_gain_attn: float32 [768], replicated, may hold values from 0.1 to 1.9
- upper_shift_attn: float32 [768], replicated, may hold values from -1.5 to 1.5
- upper_w_in: bfloat16 [768, 3072], P(None, 'tensor'), may hold values from -0.21875 to 0.21875
- upper_w_out: bfloat16 [3072, 768], P('tensor'), may hold values from -0.15625 to 0.15625
- upper_gain_ffn: float32 [768], replicated, may hold values from 0.1 to 1.9
- upper_shift_ffn: float32 [768], replicated, may hold values from -1.5 to 1.5
Outputs:
- back_out: bfloat16 [49152, 768], P(('dp', 'tensor'))
- head_out: bfloat16 [49152, 768], P(('dp', 'tensor'))
- grad_tokens: float32 [49152, 768], P(('dp', 'tensor'))
- grad_skip: float32 [49152, 768], P(('dp', 'tensor'))
- grad_lower_qkv: float32 [3, 768, 768], P(None, None, 'tensor')
- grad_lower_proj: float32 [768, 768], P('tensor')
- grad_lower_gain_attn: float32 [768], replicated
- grad_lower_shift_attn: float32 [768], replicated
- grad_lower_w_in: float32 [768, 3072], P(None, 'tensor')
- grad_lower_w_out: float32 [3072, 768], P('tensor')
- grad_lower_gain_ffn: float32 [768], replicated
- grad_lower_shift_ffn: float32 [768], replicated
- grad_upper_qkv: float32 [3, 768, 768], P(None, None, 'tensor')
- grad_upper_proj: float32 [768, 768], P('tensor')
- grad_upper_gain_attn: float32 [768], replicated
- grad_upper_shift_attn: float32 [768], replicated
- grad_upper_w_in: float32 [768, 3072], P(None, 'tensor')
- grad_upper_w_out: float32 [3072, 768], P('tensor')
- grad_upper_gain_ffn: float32 [768], replicated
- grad_upper_shift_ffn: float32 [768], replicated
The draws below stay inside these ranges and needn't reach their ends.
Inputs may be any that keep to these rules, and one draw needn't show every extreme that they name: `one_span`: 1 marks a document whose second span is padding: masked as keys, and zero in both outputs.
All inputs are finite; a program needn't handle non-finite values. No bound on the sum of `one_span` on one device may be relied on, other than what follows from the above.
Results may differ from the reference program's by a relative error of at most 0.02.
Values may be sent and summed in bfloat16 or wider, within the bound.
No kernel may reach another device: no remote copies, remote signals or barrier semaphores. Data moves between devices by JAX's collectives and lax.ppermute only.
A program may use at most 192 MiB of HBM per device.

```python
import math
import jax
import jax.numpy as jnp
from jax import lax

D = 768
HEADS = 12
HEAD_DIM = 64
FF = 3072
SPAN = 128
DOCS = 192
TOKENS = 49152


def set_ends(result, stream_key, least, high):
    longest = result.shape.index(max(result.shape))
    spots = []
    for shift in (0, 1):
        where = [jax.random.randint(jax.random.fold_in(stream_key, axis), (), 0, length) for axis, length in enumerate(result.shape)]
        where[longest] = (where[longest] + shift) % result.shape[longest]
        spots.append(tuple(where))
    return result.at[spots[0]].set(least).at[spots[1]].set(high)


def block_scale(stream_key, shape, cuts, low, top_value):
    level = 1.0
    for dim, shards_of in cuts:
        draws = jax.random.uniform(jax.random.fold_in(jax.random.fold_in(stream_key, 6), dim), (shards_of,), jnp.float32, low / len(cuts), top_value / len(cuts))
        level = level * jnp.repeat(jnp.exp(draws), shape[dim] // shards_of).reshape((-1,) + (1,) * (len(shape) - 1 - dim))
    return level


def centred(own_key, extent, deviation, limit, pieces=(), held_as=jnp.bfloat16):
    loudness = block_scale(own_key, extent, pieces, -0.22, 0.18) if pieces else 1.0
    drawn = jax.random.normal(own_key, extent, jnp.float32) * deviation * loudness
    return jnp.minimum(jnp.maximum(drawn, -limit), limit).astype(held_as)


def setup_inputs(seed: int = 0) -> dict:
    splits = jax.random.split(jax.random.key(seed), 22)
    return {
        "tokens": centred(splits[0], (TOKENS, D), 1.0, 6.0, ((0, 128),)),
        "skip_tokens": centred(splits[1], (TOKENS, D), 1.0, 6.0, ((0, 128),)),
        "cot_back": centred(splits[2], (TOKENS, D), 1.0, 6.0, ((0, 128),)),
        "cot_head": centred(splits[3], (TOKENS, D), 1.0, 6.0, ((0, 128),)),
        "one_span": set_ends((jax.random.randint(splits[4], (DOCS,), 0, 2) < 1).astype(jnp.int32), jax.random.fold_in(splits[4], 1), 0, 1),
        "lower_qkv": centred(splits[5], (3, D, D), D ** -0.5, 0.21875, ((2, 2),)),
        "lower_proj": centred(splits[6], (D, D), (D // 64) ** -0.5, 1.75, ((0, 2),)),
        "lower_gain_attn": jnp.clip(1.0 + 0.18 * jax.random.normal(splits[7], (D,), jnp.float32), 0.1, 1.9),
        "lower_shift_attn": centred(splits[8], (D,), 0.3, 1.5, (), jnp.float32),
        "lower_w_in": centred(splits[9], (D, FF), D ** -0.5, 0.21875, ((1, 2),)),
        "lower_w_out": centred(splits[10], (FF, D), (FF // 2) ** -0.5, 0.15625, ((0, 2),)),
        "lower_gain_ffn": jnp.clip(1.0 + 0.18 * jax.random.normal(splits[11], (D,), jnp.float32), 0.1, 1.9),
        "lower_shift_ffn": centred(splits[12], (D,), 0.3, 1.5, (), jnp.float32),
        "upper_qkv": centred(splits[13], (3, D, D), D ** -0.5, 0.21875, ((2, 2),)),
        "upper_proj": centred(splits[14], (D, D), (D // 64) ** -0.5, 1.75, ((0, 2),)),
        "upper_gain_attn": jnp.clip(1.0 + 0.18 * jax.random.normal(splits[15], (D,), jnp.float32), 0.1, 1.9),
        "upper_shift_attn": centred(splits[16], (D,), 0.3, 1.5, (), jnp.float32),
        "upper_w_in": centred(splits[17], (D, FF), D ** -0.5, 0.21875, ((1, 2),)),
        "upper_w_out": centred(splits[18], (FF, D), (FF // 2) ** -0.5, 0.15625, ((0, 2),)),
        "upper_gain_ffn": jnp.clip(1.0 + 0.18 * jax.random.normal(splits[19], (D,), jnp.float32), 0.1, 1.9),
        "upper_shift_ffn": centred(splits[20], (D,), 0.3, 1.5, (), jnp.float32),
    }


EPS = 1e-06
SCALE = 0.125
NEG = -1000000000.0
HIGH = lax.Precision.HIGHEST

@jax.custom_vjp
def low(v):
    return lax.optimization_barrier(v.astype(jnp.bfloat16)).astype(jnp.float32)

@jax.custom_vjp
def low_back(v):
    return v

def low_keep(v):
    return (low(v), None)

def low_pass(kept, grad):
    return (grad,)

def back_keep(v):
    return (v, None)

def back_low(kept, grad):
    return (low(grad),)
low.defvjp(low_keep, low_pass)
low_back.defvjp(back_keep, back_low)

def layer_norm(resid, gain, shift):
    mean = lax.optimization_barrier(jnp.mean(resid, axis=-1, keepdims=True))
    centered = resid - mean
    var = lax.optimization_barrier(jnp.mean(centered * centered, axis=-1, keepdims=True))
    return centered * lax.rsqrt(var + EPS) * gain + shift

def block(rows, weights, key_ok):
    qkv_w, proj_w, gain_a, shift_a, in_w, out_w, gain_f, shift_f = weights
    inputs = low(rows)
    qkv = jnp.einsum('bsd,cdj->bscj', inputs, qkv_w, precision=HIGH)
    shape = rows.shape[:2] + (HEADS, HEAD_DIM)
    query = low_back(low(qkv[:, :, 0])).reshape(shape)
    keys = low_back(low(qkv[:, :, 1])).reshape(shape)
    values = low_back(low(qkv[:, :, 2])).reshape(shape)
    scores = low_back(jnp.einsum('bqhe,bkhe->bhqk', query, keys, precision=HIGH) * SCALE)
    scores = jnp.where(key_ok[:, None, None, :], scores, NEG)
    prob = low(jax.nn.softmax(scores, axis=-1))
    mixed = jnp.einsum('bhqk,bkhe->bqhe', prob, values, precision=HIGH).reshape(rows.shape)
    context = low_back(low(mixed))
    attn = low_back(jnp.einsum('bsd,de->bse', context, proj_w, precision=HIGH))
    first = layer_norm(rows + attn, gain_a, shift_a)
    pre = low_back(jnp.einsum('bsd,df->bsf', low(first), in_w, precision=HIGH))
    act = low(jax.nn.gelu(pre, approximate=False))
    ffn = low_back(jnp.einsum('bsf,fd->bsd', act, out_w, precision=HIGH))
    return layer_norm(first + ffn, gain_f, shift_f)

def reference(tokens, skip_tokens, cot_back, cot_head, one_span, lower_qkv, lower_proj, lower_gain_attn, lower_shift_attn, lower_w_in, lower_w_out, lower_gain_ffn, lower_shift_ffn, upper_qkv, upper_proj, upper_gain_attn, upper_shift_attn, upper_w_in, upper_w_out, upper_gain_ffn, upper_shift_ffn):
    docs = one_span.shape[0]
    rows2 = 2 * SPAN
    batch = math.gcd(docs, 16)
    groups = docs // batch
    position = jnp.arange(rows2)
    key_ok = (position[None, :] < SPAN) | (one_span[:, None] == 0)
    valid = key_ok.astype(jnp.float32)[:, :, None]
    is_cls = (position % SPAN == 0)[None, :, None]

    def split(a):
        return a.astype(jnp.float32).reshape(groups, batch, rows2, D)
    lower = tuple((w.astype(jnp.float32) for w in (lower_qkv, lower_proj, lower_gain_attn, lower_shift_attn, lower_w_in, lower_w_out, lower_gain_ffn, lower_shift_ffn)))
    upper = tuple((w.astype(jnp.float32) for w in (upper_qkv, upper_proj, upper_gain_attn, upper_shift_attn, upper_w_in, upper_w_out, upper_gain_ffn, upper_shift_ffn)))
    ok_groups = key_ok.reshape(groups, batch, rows2)
    keep_groups = valid.reshape(groups, batch, rows2, 1)

    def forward(lower_w, upper_w, inputs, skipped):

        def one_group(item):
            rows, skip_rows, okay, keep = item
            back = block(rows, lower_w, okay)
            head = block(jnp.where(is_cls, back, skip_rows), upper_w, okay)
            return (back * keep, head * keep)
        return lax.map(jax.checkpoint(one_group), (inputs, skipped, ok_groups, keep_groups))
    outputs, pullback = jax.vjp(forward, lower, upper, split(tokens), split(skip_tokens))
    grad_low, grad_up, grad_tok, grad_skp = pullback((split(cot_back), split(cot_head)))

    def flat(a):
        return a.reshape(docs * rows2, D)
    return (flat(outputs[0]).astype(jnp.bfloat16), flat(outputs[1]).astype(jnp.bfloat16), flat(grad_tok), flat(grad_skp), grad_low[0], grad_low[1], grad_low[2], grad_low[3], grad_low[4], grad_low[5], grad_low[6], grad_low[7], grad_up[0], grad_up[1], grad_up[2], grad_up[3], grad_up[4], grad_up[5], grad_up[6], grad_up[7])
```

```python
import jax
import jax.numpy as jnp
from jax import lax
from jax.sharding import PartitionSpec as P

HEAD_DIM = 64
SPAN = 128


EPS = 1e-06
SCALE = 0.125
NEG = -1000000000.0


def norm_forward(resid, gain, shift):
    mean = jnp.mean(resid, axis=-1, keepdims=True)
    centered = resid - mean
    var = jnp.mean(centered * centered, axis=-1, keepdims=True)
    inv_std = lax.rsqrt(var + EPS)
    normed = centered * inv_std
    return (normed * gain + shift, normed, inv_std)


def norm_backward(grad_out, normed, inv_std, gain):
    grad_normed = grad_out * gain
    first_mean = jnp.mean(grad_normed, axis=-1, keepdims=True)
    second_mean = jnp.mean(grad_normed * normed, axis=-1, keepdims=True)
    grad_resid = inv_std * (grad_normed - first_mean - normed * second_mean)
    return (grad_resid, jnp.sum(grad_out * normed, axis=0), jnp.sum(grad_out, axis=0))


def gelu_slope(value):
    return (
        0.5 * (1.0 + jax.scipy.special.erf(value * 0.7071067811865476))
        + value * jnp.exp(-0.5 * value * value) * 0.3989422804014327
    )


def contract_last(left, right):
    return lax.dot_general(
        left, right, (((1,), (1,)), ((), ())), preferred_element_type=jnp.float32
    )


def contract_rows(left, right):
    return lax.dot_general(
        left, right, (((0,), (0,)), ((), ())), preferred_element_type=jnp.float32
    )


SWAP = [(0, 1), (1, 0)]


def gather_rows(rows_low):
    other = lax.ppermute(rows_low, "tensor", SWAP)
    first = lax.axis_index("tensor") == 0
    return jnp.concatenate(
        [jnp.where(first, rows_low, other), jnp.where(first, other, rows_low)], axis=0
    )


def gather_grad(rows_low):
    return gather_rows(rows_low)


def scatter_sum(full):
    count = full.shape[0] // 2
    side = lax.axis_index("tensor")
    away = lax.dynamic_slice_in_dim(full, (1 - side) * count, count, 0).astype(jnp.bfloat16)
    keep = lax.dynamic_slice_in_dim(full, side * count, count, 0)
    return keep + lax.ppermute(away, "tensor", SWAP).astype(jnp.float32)


BLOCK = (48, 384)


def coord_bits(chip):
    x, y, z = chip % 4, chip // 4 % 4, chip // 16
    low = [(p ^ (p >> 1)) & 1 for p in (x, y, z)]
    high = [p >> 1 for p in (x, y, z)]
    return low, high


def flip(chip, core, stage, mask):
    pos = [chip % 4, chip // 4 % 4, chip // 16]
    for axis in range(3):
        if mask >> axis & 1:
            low = (core == 0) == (stage == 0)
            pos[axis] = pos[axis] ^ 1 if low else 3 - pos[axis]
    return pos[0] + 4 * pos[1] + 16 * pos[2]


def exchange(value, stage, mask):
    pairs = [
        (2 * chip + core, 2 * flip(chip, core, stage, mask) + core)
        for chip in range(64)
        for core in range(2)
    ]
    return lax.ppermute(value, ("dp", "tensor"), pairs)


def my_bits():
    low, high = coord_bits(lax.axis_index("dp"))
    core = lax.axis_index("tensor")
    first = [jnp.where(core == 0, a, b) for a, b in zip(low, high)]
    second = [jnp.where(core == 0, b, a) for a, b in zip(low, high)]
    near = first[0] + 2 * first[1] + 4 * first[2]
    far = second[0] + 2 * second[1] + 4 * second[2]
    return near, far


def total(terms):
    out = terms[0].astype(jnp.float32)
    for term in terms[1:]:
        out = out + term.astype(jnp.float32)
    return out


def sum_over_chips(blocks, turn, order):
    rel = jnp.take(blocks, order, axis=0).reshape((2, 2, 2, 8) + BLOCK)
    axes = [2 - (turn + j) % 3 for j in range(3)]
    terms = [rel]
    for axis in axes:
        send = total([lax.slice_in_dim(t, 1, 2, axis=axis) for t in terms]).astype(jnp.bfloat16)
        terms = [lax.slice_in_dim(t, 0, 1, axis=axis) for t in terms]
        terms.append(exchange(send, 0, 1 << (2 - axis)))
    terms = [t.reshape((8,) + BLOCK) for t in terms]
    own = [total([t[0] for t in terms])]
    for mask in range(1, 8):
        own.append(exchange(total([t[mask] for t in terms]).astype(jnp.bfloat16), 1, mask))
    mine = total(own).astype(jnp.bfloat16)
    parts = [mine] + [exchange(mine, 1, mask) for mask in range(1, 8)]
    held = jnp.stack(parts).reshape((1, 1, 1, 8) + BLOCK)
    for axis in reversed(axes):
        held = jnp.concatenate([held, exchange(held, 0, 1 << (2 - axis))], axis=axis)
    return jnp.take(held.reshape((64,) + BLOCK), order, axis=0)


def to_blocks(grad):
    rows, columns = grad.shape
    out = grad.astype(jnp.bfloat16).reshape(rows // 48, 48, columns // 384, 384)
    return out.transpose(0, 2, 1, 3).reshape((-1,) + BLOCK)


def from_blocks(blocks, shape):
    rows, columns = shape
    out = blocks.reshape(rows // 48, columns // 384, 48, 384).transpose(0, 2, 1, 3)
    return out.reshape(shape).astype(jnp.float32)


def sum_weights(grads, order):
    qkv, proj, w_in, w_out = grads
    attn = jnp.concatenate([to_blocks(qkv.reshape(-1, qkv.shape[-1])), to_blocks(proj)])
    sum_out = sum_over_chips(to_blocks(w_out), 0, order)
    sum_in = sum_over_chips(to_blocks(w_in), 1, order)
    sum_attn = sum_over_chips(attn, 2, order)
    return (
        from_blocks(sum_attn[:48], (qkv.shape[0] * qkv.shape[1], qkv.shape[2])).reshape(qkv.shape),
        from_blocks(sum_attn[48:], proj.shape),
        from_blocks(sum_in, w_in.shape),
        from_blocks(sum_out, w_out.shape),
    )


def sum_norms(norms):
    value = jnp.stack(norms)
    value = value + lax.ppermute(value, "tensor", SWAP)
    for stage in range(2):
        for axis in range(3):
            value = value + exchange(value, stage, 1 << axis)
    return [value[i] for i in range(8)]


def sum_rows(full, weight, count):

    def term(start, size):
        return jnp.dot(full, weight, preferred_element_type=jnp.float32)

    return scatter_sum(term(jnp.int32(0), count * lax.axis_size("tensor")))


def sum_back(term, count):
    return scatter_sum(term(jnp.int32(0), count * lax.axis_size("tensor")))


def split_heads(full_qkv, index, docs):
    rows, _, width = full_qkv.shape
    return full_qkv[:, index].reshape(docs, 2 * SPAN, width // HEAD_DIM, HEAD_DIM)


def attend(qkv, key_ok):
    docs = key_ok.shape[0]
    rows, _, width = qkv.shape
    query = split_heads(qkv, 0, docs).astype(jnp.bfloat16)
    keys = split_heads(qkv, 1, docs).astype(jnp.bfloat16)
    values = split_heads(qkv, 2, docs).astype(jnp.bfloat16)
    scores = jnp.einsum("nqhe,nkhe->nhqk", query, keys, preferred_element_type=jnp.float32) * SCALE
    scores = jnp.where(key_ok[:, None, None, :], scores, NEG)
    largest = jnp.max(scores, axis=-1, keepdims=True)
    raised = jnp.exp(scores - largest)
    total = jnp.sum(raised, axis=-1, keepdims=True)
    log_total = largest + jnp.log(total)
    prob_low = (raised / total).astype(jnp.bfloat16)
    mixed = jnp.einsum("nhqk,nkhe->nqhe", prob_low, values, preferred_element_type=jnp.float32)
    context = mixed.reshape(rows, width).astype(jnp.bfloat16)
    return (context, (query, keys, values, log_total))


def attend_back(grad_ctx, kept, key_ok):
    query, keys, values, log_total = kept
    docs, length, heads, size = query.shape
    scores = jnp.einsum("nqhe,nkhe->nhqk", query, keys, preferred_element_type=jnp.float32) * SCALE
    scores = jnp.where(key_ok[:, None, None, :], scores, NEG)
    prob = jnp.exp(scores - log_total)
    prob_low = prob.astype(jnp.bfloat16)
    grad_mix = grad_ctx.reshape(docs, length, heads, size)
    grad_values = jnp.einsum(
        "nhqk,nqhe->nkhe", prob_low, grad_mix, preferred_element_type=jnp.float32
    )
    grad_prob = jnp.einsum("nqhe,nkhe->nhqk", grad_mix, values, preferred_element_type=jnp.float32)
    grad_scores = prob * (grad_prob - jnp.sum(grad_prob * prob, axis=-1, keepdims=True))
    grad_scores = grad_scores.astype(jnp.bfloat16)
    grad_query = (
        jnp.einsum("nhqk,nkhe->nqhe", grad_scores, keys, preferred_element_type=jnp.float32) * SCALE
    )
    grad_keys = (
        jnp.einsum("nhqk,nqhe->nkhe", grad_scores, query, preferred_element_type=jnp.float32)
        * SCALE
    )
    rows = docs * length
    width = heads * size
    stacked = jnp.stack(
        [
            grad_query.reshape(rows, width),
            grad_keys.reshape(rows, width),
            grad_values.reshape(rows, width),
        ],
        axis=1,
    )
    return stacked.astype(jnp.bfloat16)


def block_forward(rows, weights, key_ok, count):
    qkv_w, proj_w, gain_a, shift_a, in_w, out_w, gain_f, shift_f = weights
    full = gather_rows(rows.astype(jnp.bfloat16))
    qkv = jnp.einsum("rd,cdj->rcj", full, qkv_w, preferred_element_type=jnp.float32)
    context, att_kept = attend(qkv, key_ok)
    attn = sum_rows(context, proj_w, count)
    first, normed_a, inv_a = norm_forward(rows + attn, gain_a, shift_a)
    full_first = gather_rows(first.astype(jnp.bfloat16))
    pre = jnp.dot(full_first, in_w, preferred_element_type=jnp.float32)
    act = jax.nn.gelu(pre, approximate=False).astype(jnp.bfloat16)
    ffn = sum_rows(act, out_w, count)
    result, normed_f, inv_f = norm_forward(first + ffn, gain_f, shift_f)
    return (
        result,
        (full, att_kept, context, normed_a, inv_a, full_first, pre, act, normed_f, inv_f),
    )


def block_backward(grad_out, weights, key_ok, count, kept):
    qkv_w, proj_w, gain_a, shift_a, in_w, out_w, gain_f, shift_f = weights
    full, att_kept, context, normed_a, inv_a, full_first, pre, act, normed_f, inv_f = kept
    grad_second, grad_gain_f, grad_shift_f = norm_backward(grad_out, normed_f, inv_f, gain_f)
    full_grad_ffn = gather_grad(grad_second.astype(jnp.bfloat16))
    grad_act = contract_last(full_grad_ffn, out_w)
    grad_out_w = contract_rows(act, full_grad_ffn)
    grad_pre = (grad_act * gelu_slope(pre)).astype(jnp.bfloat16)
    grad_in_w = contract_rows(full_first, grad_pre)

    def ffn_term(start, size):
        return contract_last(grad_pre, in_w)

    grad_first = grad_second + sum_back(ffn_term, count)
    grad_resid, grad_gain_a, grad_shift_a = norm_backward(grad_first, normed_a, inv_a, gain_a)
    full_grad_attn = gather_grad(grad_resid.astype(jnp.bfloat16))
    grad_ctx = contract_last(full_grad_attn, proj_w).astype(jnp.bfloat16)
    grad_proj = contract_rows(context, full_grad_attn)
    grad_qkv = attend_back(grad_ctx, att_kept, key_ok)
    grad_qkv_w = jnp.einsum("rd,rcj->cdj", full, grad_qkv, preferred_element_type=jnp.float32)

    def attn_term(start, size):
        return jnp.einsum("rcj,cdj->rd", grad_qkv, qkv_w, preferred_element_type=jnp.float32)

    grad_rows = grad_resid + sum_back(attn_term, count)
    return (
        grad_rows,
        (grad_qkv_w, grad_proj, grad_in_w, grad_out_w),
        (grad_gain_a, grad_shift_a, grad_gain_f, grad_shift_f),
    )


def on_device(
    tokens,
    skip_tokens,
    cot_back,
    cot_head,
    one_span,
    lower_qkv,
    lower_proj,
    lower_gain_attn,
    lower_shift_attn,
    lower_w_in,
    lower_w_out,
    lower_gain_ffn,
    lower_shift_ffn,
    upper_qkv,
    upper_proj,
    upper_gain_attn,
    upper_shift_attn,
    upper_w_in,
    upper_w_out,
    upper_gain_ffn,
    upper_shift_ffn,
):
    count = tokens.shape[0]
    docs_local = one_span.shape[0]
    position = jnp.arange(2 * SPAN)
    key_ok = (position[None, :] < SPAN) | (one_span[:, None] == 0)
    row_index = lax.axis_index("tensor") * count + jnp.arange(count)
    doc_index = row_index // (2 * SPAN)
    doc_flag = jnp.sum(
        jnp.where(doc_index[:, None] == jnp.arange(docs_local)[None, :], one_span[None, :], 0),
        axis=1,
    )
    row_ok = (row_index // SPAN % 2 == 0) | (doc_flag == 0)
    valid = row_ok[:, None].astype(jnp.float32)
    is_cls = (row_index % SPAN == 0)[:, None]
    lower = (
        lower_qkv,
        lower_proj,
        lower_gain_attn,
        lower_shift_attn,
        lower_w_in,
        lower_w_out,
        lower_gain_ffn,
        lower_shift_ffn,
    )
    upper = (
        upper_qkv,
        upper_proj,
        upper_gain_attn,
        upper_shift_attn,
        upper_w_in,
        upper_w_out,
        upper_gain_ffn,
        upper_shift_ffn,
    )
    back, kept_lower = block_forward(tokens.astype(jnp.float32), lower, key_ok, count)
    head_in = jnp.where(is_cls, back, skip_tokens.astype(jnp.float32))
    head, kept_upper = block_forward(head_in, upper, key_ok, count)
    grad_head_in, weights_upper, norms_upper = block_backward(
        cot_head.astype(jnp.float32) * valid, upper, key_ok, count, kept_upper
    )
    grad_skip = jnp.where(is_cls, 0.0, grad_head_in)
    grad_back = cot_back.astype(jnp.float32) * valid + jnp.where(is_cls, grad_head_in, 0.0)
    grad_tokens, weights_lower, norms_lower = block_backward(
        grad_back, lower, key_ok, count, kept_lower
    )
    near, far = my_bits()
    slots = jnp.arange(64)
    order = (slots // 8 ^ near) * 8 + (slots % 8 ^ far)
    weights_upper = sum_weights(weights_upper, order)
    weights_lower = sum_weights(weights_lower, order)
    norms = sum_norms(norms_lower + norms_upper)
    return (
        (back * valid).astype(jnp.bfloat16),
        (head * valid).astype(jnp.bfloat16),
        grad_tokens,
        grad_skip,
        weights_lower[0],
        weights_lower[1],
        norms[0],
        norms[1],
        weights_lower[2],
        weights_lower[3],
        norms[2],
        norms[3],
        weights_upper[0],
        weights_upper[1],
        norms[4],
        norms[5],
        weights_upper[2],
        weights_upper[3],
        norms[6],
        norms[7],
    )


def solution(mesh):
    return jax.shard_map(
        on_device,
        mesh=mesh,
        in_specs=(
            P(("dp", "tensor"), None),
            P(("dp", "tensor"), None),
            P(("dp", "tensor"), None),
            P(("dp", "tensor"), None),
            P("dp"),
            P(None, None, "tensor"),
            P("tensor", None),
            P(),
            P(),
            P(None, "tensor"),
            P("tensor", None),
            P(),
            P(),
            P(None, None, "tensor"),
            P("tensor", None),
            P(),
            P(),
            P(None, "tensor"),
            P("tensor", None),
            P(),
            P(),
        ),
        out_specs=(
            P(("dp", "tensor"), None),
            P(("dp", "tensor"), None),
            P(("dp", "tensor"), None),
            P(("dp", "tensor"), None),
            P(None, None, "tensor"),
            P("tensor", None),
            P(),
            P(),
            P(None, "tensor"),
            P("tensor", None),
            P(),
            P(),
            P(None, None, "tensor"),
            P("tensor", None),
            P(),
            P(),
            P(None, "tensor"),
            P("tensor", None),
            P(),
            P(),
        ),
        check_vma=False,
    )
```

```python
import functools

import jax
import jax.numpy as jnp
from jax import lax
from jax.experimental import pallas as pl
from jax.experimental.pallas import tpu as pltpu
from jax.sharding import PartitionSpec as P

SPAN = 128
EPS = 1e-06
SCALE = 0.125
NEG = -1000000000.0

D = 768
ROWS = 768
HALF = ROWS // 2
HIDDEN = 1536
PIECE = 384
PAIR = 128
BLOCK = (48, 384)
F32 = jnp.float32
BF16 = jnp.bfloat16

SWAP = [(0, 1), (1, 0)]


def dot_nn(left, right):
    return lax.dot_general(left, right, (((1,), (0,)), ((), ())), preferred_element_type=F32)


def dot_nt(left, right):
    return lax.dot_general(left, right, (((1,), (1,)), ((), ())), preferred_element_type=F32)


def dot_tn(left, right):
    return lax.dot_general(left, right, (((0,), (0,)), ((), ())), preferred_element_type=F32)


def normalize(resid):
    mean = jnp.mean(resid, axis=-1, keepdims=True)
    centered = resid - mean
    var = jnp.mean(centered * centered, axis=-1, keepdims=True)
    inv = lax.rsqrt(var + EPS)
    return centered * inv, inv


def norm_grad(grad_out, normed, inv, gain):
    grad = grad_out * gain
    first = jnp.mean(grad, axis=-1, keepdims=True)
    second = jnp.mean(grad * normed, axis=-1, keepdims=True)
    return inv * (grad - first - normed * second)


def fold(value):
    return jnp.sum(value.reshape(-1, 8, value.shape[-1]), axis=0)

DOC = 2 * SPAN
DOCS = ROWS // DOC


def doc_rows(doc):
    return slice(doc * DOC, (doc + 1) * DOC)


def half_rows(index):
    return pl.ds(pl.multiple_of(index * HALF, HALF), HALF)


def join_halves(side, own_ref, other_ref, full_ref):
    full_ref[half_rows(side), :] = own_ref[...]
    full_ref[half_rows(1 - side), :] = other_ref[...]


def doc_masks(spans_ref, doc):
    row = lax.broadcasted_iota(jnp.int32, (DOC, 1), 0)
    keep = jnp.where((row < SPAN) | (spans_ref[doc] == 0), 1.0, 0.0)
    return keep, (row & (SPAN - 1)) == 0


def spread(column):
    return jnp.broadcast_to(column, (column.shape[0], 128))


def head_masks():
    lane = lax.broadcasted_iota(jnp.int32, (1, PAIR), 1)
    return lane < 64


def both_heads(value, left):
    zero = jnp.zeros_like(value)
    return jnp.concatenate([jnp.where(left, value, zero), jnp.where(left, zero, value)], axis=0)


def attend(spans_ref, x_ref, qkv_w_ref, proj_ref, qkv_ref, prob_ref, ctx_ref, part_ref, wide):
    for index in range(3):
        wide[:, index * 384:(index + 1) * 384] = qkv_w_ref[index]
    for doc in range(DOCS):
        at = doc_rows(doc)
        out = dot_nn(x_ref[at, :], wide[...])
        qkv_ref[at, :384] = (out[:, :384] * SCALE).astype(BF16)
        qkv_ref[at, 384:] = out[:, 384:].astype(BF16)
    left = head_masks()
    col = lax.broadcasted_iota(jnp.int32, (1, 2 * DOC), 1) & (DOC - 1)
    for doc in range(DOCS):
        at = doc_rows(doc)
        key_ok = (col < SPAN) | (spans_ref[doc] == 0)
        scores = []
        for pair in range(3):
            query = qkv_ref[at, pair * PAIR:(pair + 1) * PAIR]
            keys = qkv_ref[at, 384 + pair * PAIR:384 + (pair + 1) * PAIR]
            scores.append(jnp.where(key_ok, dot_nt(query, both_heads(keys, left)), NEG))
        for pair in range(3):
            probs = []
            for head in range(2):
                score = scores[pair][:, head * DOC:(head + 1) * DOC]
                raised = jnp.exp(score - jnp.max(score, axis=-1, keepdims=True))
                probs.append(
                    (raised * (1.0 / jnp.sum(raised, axis=-1, keepdims=True))).astype(BF16)
                )
            prob = jnp.concatenate(probs, axis=1)
            prob_ref[doc, pair] = prob
            values = qkv_ref[at, 768 + pair * PAIR:768 + (pair + 1) * PAIR]
            mixed = dot_nn(prob, both_heads(values, left))
            ctx_ref[at, pair * PAIR:(pair + 1) * PAIR] = mixed.astype(BF16)
    for doc in range(DOCS):
        at = doc_rows(doc)
        part_ref[at, :] = dot_nn(ctx_ref[at, :], proj_ref[...]).astype(BF16)


def attend_first_kernel(
    side_ref, spans_ref, own_ref, other_ref, qkv_w_ref, proj_ref,
    x_ref, qkv_ref, prob_ref, ctx_ref, part_ref, wide,
):
    join_halves(side_ref[0], own_ref, other_ref, x_ref)
    attend(spans_ref, x_ref, qkv_w_ref, proj_ref, qkv_ref, prob_ref, ctx_ref, part_ref, wide)


def attend_second_kernel(
    side_ref, spans_ref, first_ref, mine_ref, theirs_ref, gain_ref, shift_ref, own_ref, other_ref,
    qkv_w_ref, proj_ref,
    x_ref, normed_ref, inv_ref, out_ref, qkv_ref, prob_ref, ctx_ref, part_ref, wide, full,
):
    side = side_ref[0]
    join_halves(side, own_ref, other_ref, x_ref)
    for doc in range(DOCS):
        at = doc_rows(doc)
        keep, cls = doc_masks(spans_ref, doc)
        resid = first_ref[at, :] + mine_ref[at, :].astype(F32) + theirs_ref[at, :].astype(F32)
        normed, inv = normalize(resid)
        back = normed * gain_ref[...] + shift_ref[...]
        normed_ref[at, :] = normed.astype(BF16)
        inv_ref[at, :] = spread(inv)
        x_ref[at, :] = jnp.where(cls, back, x_ref[at, :].astype(F32)).astype(BF16)
        full[at, :] = (back * keep).astype(BF16)
    out_ref[...] = full[half_rows(side), :]
    attend(spans_ref, x_ref, qkv_w_ref, proj_ref, qkv_ref, prob_ref, ctx_ref, part_ref, wide)


def feed_kernel(
    x_ref, mine_ref, theirs_ref, gain_ref, shift_ref, in_ref, out_w_ref,
    first_ref, low_ref, normed_ref, inv_ref, act_ref, slope_ref, part_ref,
):
    for doc in range(DOCS):
        at = doc_rows(doc)
        resid = x_ref[at, :].astype(F32) + mine_ref[at, :].astype(F32) + theirs_ref[at, :].astype(F32)
        normed, inv = normalize(resid)
        first = normed * gain_ref[...] + shift_ref[...]
        normed_ref[at, :] = normed.astype(BF16)
        inv_ref[at, :] = spread(inv)
        first_ref[at, :] = first
        low_ref[at, :] = first.astype(BF16)
    for doc in range(DOCS):
        at = doc_rows(doc)
        for piece in range(3):
            cut = slice(piece * 512, (piece + 1) * 512)
            pre = dot_nn(low_ref[at, :], in_ref[:, cut])
            share = 0.5 * (1.0 + lax.erf(pre * 0.7071067811865476))
            density = jnp.exp(-0.5 * pre * pre) * 0.3989422804014327
            act_ref[at, cut] = (pre * share).astype(BF16)
            slope_ref[at, cut] = (share + pre * density).astype(BF16)
    for doc in range(DOCS):
        at = doc_rows(doc)
        part_ref[at, :] = dot_nn(act_ref[at, :], out_w_ref[...]).astype(BF16)


def feed_back(gs_low_ref, slope_ref, in_ref, out_w_ref, grad_pre_ref, part_ref):
    for doc in range(DOCS):
        at = doc_rows(doc)
        for piece in range(3):
            cut = slice(piece * 512, (piece + 1) * 512)
            grad_act = dot_nt(gs_low_ref[at, :], out_w_ref[cut, :])
            grad_pre_ref[at, cut] = (grad_act * slope_ref[at, cut].astype(F32)).astype(BF16)
    for doc in range(DOCS):
        at = doc_rows(doc)
        part_ref[at, :] = dot_nt(grad_pre_ref[at, :], in_ref[...]).astype(BF16)


def put_norm_grads(norms_ref, sums):
    gain, shift = sums
    norms_ref[...] = jnp.zeros_like(norms_ref)
    norms_ref[0:1, :] = jnp.sum(gain, axis=0, keepdims=True)
    norms_ref[1:2, :] = jnp.sum(shift, axis=0, keepdims=True)


def add_sums(sums, grad_out, normed):
    new = (fold(grad_out * normed), fold(grad_out))
    return new if sums is None else (sums[0] + new[0], sums[1] + new[1])


def feed_back_second_kernel(
    side_ref, spans_ref, first_ref, mine_ref, theirs_ref, gain_ref, shift_ref, own_ref, other_ref,
    slope_ref, in_ref, out_w_ref,
    head_ref, gs_ref, gs_low_ref, norms_ref, grad_pre_ref, part_ref, cot, full,
):
    side = side_ref[0]
    join_halves(side, own_ref, other_ref, cot)
    sums = None
    for doc in range(DOCS):
        at = doc_rows(doc)
        keep, _ = doc_masks(spans_ref, doc)
        resid = first_ref[at, :] + mine_ref[at, :].astype(F32) + theirs_ref[at, :].astype(F32)
        normed, inv = normalize(resid)
        head = normed * gain_ref[...] + shift_ref[...]
        full[at, :] = (head * keep).astype(BF16)
        grad_out = cot[at, :].astype(F32) * keep
        grad = norm_grad(grad_out, normed, inv, gain_ref[...])
        gs_ref[at, :] = grad
        gs_low_ref[at, :] = grad.astype(BF16)
        sums = add_sums(sums, grad_out, normed)
    head_ref[...] = full[half_rows(side), :]
    put_norm_grads(norms_ref, sums)
    feed_back(gs_low_ref, slope_ref, in_ref, out_w_ref, grad_pre_ref, part_ref)


def feed_back_first_kernel(
    side_ref, spans_ref, normed_ref, inv_ref, gain_ref, own_ref, other_ref,
    resid_ref, mine_ref, theirs_ref, slope_ref, in_ref, out_w_ref,
    skip_ref, gs_ref, gs_low_ref, norms_ref, grad_pre_ref, part_ref, cot, full,
):
    side = side_ref[0]
    join_halves(side, own_ref, other_ref, cot)
    sums = None
    for doc in range(DOCS):
        at = doc_rows(doc)
        keep, cls = doc_masks(spans_ref, doc)
        above = resid_ref[at, :] + mine_ref[at, :].astype(F32) + theirs_ref[at, :].astype(F32)
        full[at, :] = jnp.where(cls, 0.0, above)
        normed = normed_ref[at, :].astype(F32)
        grad_out = cot[at, :].astype(F32) * keep + jnp.where(cls, above, 0.0)
        grad = norm_grad(grad_out, normed, inv_ref[at, 0:1], gain_ref[...])
        gs_ref[at, :] = grad
        gs_low_ref[at, :] = grad.astype(BF16)
        sums = add_sums(sums, grad_out, normed)
    skip_ref[...] = full[half_rows(side), :]
    put_norm_grads(norms_ref, sums)
    feed_back(gs_low_ref, slope_ref, in_ref, out_w_ref, grad_pre_ref, part_ref)


def attend_back_kernel(
    gs_ref, mine_ref, theirs_ref, normed_ref, inv_ref, gain_ref, qkv_ref, prob_ref,
    qkv_w_ref, proj_ref,
    resid_ref, low_ref, norms_ref, grad_qkv_ref, part_ref, grad_ctx, wide,
):
    for index in range(3):
        wide[:, index * 384:(index + 1) * 384] = qkv_w_ref[index]
    sums = None
    for doc in range(DOCS):
        at = doc_rows(doc)
        grad_out = gs_ref[at, :] + mine_ref[at, :].astype(F32) + theirs_ref[at, :].astype(F32)
        normed = normed_ref[at, :].astype(F32)
        grad = norm_grad(grad_out, normed, inv_ref[at, 0:1], gain_ref[...])
        resid_ref[at, :] = grad
        low_ref[at, :] = grad.astype(BF16)
        sums = add_sums(sums, grad_out, normed)
    put_norm_grads(norms_ref, sums)
    for doc in range(DOCS):
        at = doc_rows(doc)
        grad_ctx[at, :] = dot_nt(low_ref[at, :], proj_ref[...]).astype(BF16)
    left = head_masks()
    for doc in range(DOCS):
        at = doc_rows(doc)
        pairs = [slice(pair * PAIR, (pair + 1) * PAIR) for pair in range(3)]
        grad_probs = []
        for pair in range(3):
            values = qkv_ref[at, 768 + pair * PAIR:768 + (pair + 1) * PAIR]
            grad_probs.append(dot_nt(grad_ctx[at, pairs[pair]], both_heads(values, left)))
        for pair in range(3):
            prob_low = prob_ref[doc, pair]
            scored = []
            for head in range(2):
                cut = slice(head * DOC, (head + 1) * DOC)
                prob = prob_low[:, cut].astype(F32)
                grad_prob = grad_probs[pair][:, cut]
                inner = jnp.sum(grad_prob * prob, axis=-1, keepdims=True)
                scored.append((prob * (grad_prob - inner)).astype(BF16))
            grad_scores = jnp.concatenate(scored, axis=1)
            query = qkv_ref[at, pairs[pair]]
            keys = qkv_ref[at, 384 + pair * PAIR:384 + (pair + 1) * PAIR]
            grad_query = dot_nn(grad_scores, both_heads(keys, left)) * SCALE
            grad_keys = dot_tn(grad_scores, query)
            grad_values = dot_tn(prob_low, grad_ctx[at, pairs[pair]])
            grad_qkv_ref[at, pair * PAIR:(pair + 1) * PAIR] = grad_query.astype(BF16)
            for index, grad in ((1, grad_keys), (2, grad_values)):
                cut = slice(index * 384 + pair * PAIR, index * 384 + (pair + 1) * PAIR)
                grad_qkv_ref[at, cut] = jnp.where(left, grad[:DOC], grad[DOC:]).astype(BF16)
    for doc in range(DOCS):
        at = doc_rows(doc)
        part_ref[at, :] = dot_nt(grad_qkv_ref[at, :], wide[...]).astype(BF16)


def cut_wide(value, blocks, piece):
    for half in range(2):
        for k in range(8):
            blocks[piece, half, k] = value[k * 48:(k + 1) * 48, half * 384:(half + 1) * 384]


def cut_tall(value, blocks, piece):
    for half in range(2):
        for k in range(8):
            at = half * 384 + k * 48
            blocks[piece, half, k] = value[at:at + 48, :]


def put_blocks(order_ref, blocks, send_ref, keep_ref):
    first, second, third, outer = [order_ref[i] for i in range(4)]
    for rel, ref in ((1, send_ref), (0, keep_ref)):
        for b in range(2):
            piece = 2 * (rel ^ first) + (b ^ second)
            for e in range(2):
                for k in range(8):
                    ref[b, e, k] = blocks[piece, e ^ third, k ^ outer]


def out_grad_kernel(order_ref, act_ref, gs_ref, send_ref, keep_ref, blocks):
    for p in range(2):
        value = dot_tn(act_ref[:, p * 768:(p + 1) * 768], gs_ref[...]).astype(BF16)
        cut_wide(value[:384], blocks, 2 * p)
        cut_wide(value[384:], blocks, 2 * p + 1)
    put_blocks(order_ref, blocks, send_ref, keep_ref)


def in_grad_kernel(order_ref, low_ref, grad_ref, send_ref, keep_ref, blocks):
    for p in range(2):
        value = dot_tn(low_ref[...], grad_ref[:, p * 768:(p + 1) * 768]).astype(BF16)
        cut_tall(value[:, :384], blocks, 2 * p)
        cut_tall(value[:, 384:], blocks, 2 * p + 1)
    put_blocks(order_ref, blocks, send_ref, keep_ref)


def attend_grad_kernel(order_ref, x_ref, grad_ref, ctx_ref, low_ref, send_ref, keep_ref, blocks):
    value = dot_tn(x_ref[...], grad_ref[...]).astype(BF16)
    for piece in range(3):
        cut_tall(value[:, piece * 384:(piece + 1) * 384], blocks, piece)
    cut_wide(dot_tn(ctx_ref[...], low_ref[...]).astype(BF16), blocks, 3)
    put_blocks(order_ref, blocks, send_ref, keep_ref)


def take_wide(ref, block, low, far, out_ref):
    for half in range(2):
        for k in range(8):
            at = (slice(k * 48, (k + 1) * 48), slice(half * 384, (half + 1) * 384))
            out_ref[at] = ref[block, half ^ low, k ^ far].astype(F32)


def take_tall(ref, block, low, far, out_ref):
    for half in range(2):
        for k in range(8):
            at = half * 384 + k * 48
            out_ref[at:at + 48, :] = ref[block, half ^ low, k ^ far].astype(F32)


def take_step(take, piece, order_ref, held_ref, got_ref, out_ref):
    first, second, third, outer = [order_ref[i] for i in range(4)]
    block = (piece & 1) ^ second

    @pl.when((piece >> 1) == first)
    def _():
        take(held_ref, block, third, outer, out_ref)

    @pl.when((piece >> 1) != first)
    def _():
        take(got_ref, block, third, outer, out_ref)


def out_place_kernel(order_ref, held_ref, got_ref, out_ref):
    take_step(take_wide, pl.program_id(0), order_ref, held_ref, got_ref, out_ref)


def in_place_kernel(order_ref, held_ref, got_ref, out_ref):
    take_step(take_tall, pl.program_id(0), order_ref, held_ref, got_ref, out_ref)


def attend_place_kernel(order_ref, held_ref, got_ref, qkv_ref, proj_ref):
    which = pl.program_id(0)

    @pl.when(which < 3)
    def _():
        take_step(take_tall, which, order_ref, held_ref, got_ref, qkv_ref.at[0])

    @pl.when(which == 3)
    def _():
        take_step(take_wide, which, order_ref, held_ref, got_ref, proj_ref)


def sds(*shape, dtype=BF16):
    return jax.ShapeDtypeStruct(shape, dtype)


SCALARS = pl.BlockSpec(memory_space=pltpu.SMEM)
LOCAL = pl.BlockSpec(memory_space=pltpu.VMEM)


def cost(flops, arrays, outs):
    moved = sum(a.size * a.dtype.itemsize for a in list(arrays) + list(outs))
    return pl.CostEstimate(flops=flops, bytes_accessed=moved, transcendentals=0)


def run(kernel, scalars, arrays, outs, scratch, flops, limit=20):
    return pl.pallas_call(
        kernel,
        out_shape=list(outs),
        in_specs=[SCALARS] * len(scalars) + [LOCAL] * len(arrays),
        out_specs=[LOCAL] * len(outs),
        scratch_shapes=scratch,
        compiler_params=pltpu.CompilerParams(vmem_limit_bytes=limit * 2**20),
        cost_estimate=cost(flops, arrays, outs),
        name=kernel.__name__,
    )(*scalars, *arrays)


STATS = sds(ROWS, 128, dtype=F32)
ATTEND_OUTS = [sds(ROWS, 1152), sds(3, 3, DOC, 2 * DOC), sds(ROWS, PIECE), sds(ROWS, D)]
WIDE = pltpu.VMEM((D, 1152), BF16)


def attend_first(side, spans, own, other, weights):
    return run(
        attend_first_kernel, [side, spans], [own, other, weights[0], weights[1]],
        [sds(ROWS, D)] + ATTEND_OUTS, [WIDE], 2_400_000_000,
    )


def attend_second(side, spans, first, mine, theirs, gain, shift, own, other, weights):
    return run(
        attend_second_kernel, [side, spans],
        [first, mine, theirs, gain, shift, own, other, weights[0], weights[1]],
        [sds(ROWS, D), sds(ROWS, D), STATS, sds(HALF, D)] + ATTEND_OUTS,
        [WIDE, pltpu.VMEM((ROWS, D), BF16)], 2_400_000_000,
    )


def feed(x, mine, theirs, weights):
    return run(
        feed_kernel, [], [x, mine, theirs, weights[2], weights[3], weights[4], weights[5]],
        [sds(ROWS, D, dtype=F32), sds(ROWS, D), sds(ROWS, D), STATS,
         sds(ROWS, HIDDEN), sds(ROWS, HIDDEN), sds(ROWS, D)],
        [], 3_600_000_000,
    )


FEED_BACK_OUTS = [
    sds(ROWS, D, dtype=F32), sds(ROWS, D), sds(8, D, dtype=F32), sds(ROWS, HIDDEN), sds(ROWS, D),
]


def feed_back_second(side, spans, first, mine, theirs, own, other, slope, weights):
    return run(
        feed_back_second_kernel, [side, spans],
        [first, mine, theirs, weights[6], weights[7], own, other, slope, weights[4], weights[5]],
        [sds(HALF, D)] + FEED_BACK_OUTS,
        [pltpu.VMEM((ROWS, D), BF16), pltpu.VMEM((ROWS, D), BF16)], 3_600_000_000,
    )


def feed_back_first(side, spans, normed, inv, own, other, resid, mine, theirs, slope, weights):
    return run(
        feed_back_first_kernel, [side, spans],
        [normed, inv, weights[6], own, other, resid, mine, theirs, slope, weights[4], weights[5]],
        [sds(HALF, D, dtype=F32)] + FEED_BACK_OUTS,
        [pltpu.VMEM((ROWS, D), BF16), pltpu.VMEM((ROWS, D), F32)], 3_600_000_000,
    )


def attend_back(gs, mine, theirs, normed, inv, qkv, prob, weights):
    return run(
        attend_back_kernel, [],
        [gs, mine, theirs, normed, inv, weights[2], qkv, prob, weights[0], weights[1]],
        [sds(ROWS, D, dtype=F32), sds(ROWS, D), sds(8, D, dtype=F32), sds(ROWS, 1152), sds(ROWS, D)],
        [pltpu.VMEM((ROWS, PIECE), BF16), WIDE], 2_800_000_000,
    )


SPLIT_OUTS = [sds(2, 2, 8, *BLOCK), sds(2, 2, 8, *BLOCK)]
BLOCKS = pltpu.VMEM((4, 2, 8) + BLOCK, BF16)


def out_grad(order, act, gs_low):
    return run(out_grad_kernel, [order], [act, gs_low], SPLIT_OUTS, [BLOCKS], 1_800_000_000)


def in_grad(order, low, grad_pre):
    return run(in_grad_kernel, [order], [low, grad_pre], SPLIT_OUTS, [BLOCKS], 1_800_000_000)


def attend_grad(order, x, grad_qkv, ctx, low):
    return run(
        attend_grad_kernel, [order], [x, grad_qkv, ctx, low], SPLIT_OUTS, [BLOCKS], 1_800_000_000
    )


HELD = pl.BlockSpec((2, 2, 8) + BLOCK, lambda s, o: (0, 0, 0, 0, 0))


def place(kernel, order, held, got, outs):
    shapes, specs = zip(*outs)
    return pl.pallas_call(
        kernel,
        out_shape=list(shapes),
        grid_spec=pltpu.PrefetchScalarGridSpec(
            num_scalar_prefetch=1,
            grid=(4,),
            in_specs=[HELD, HELD],
            out_specs=list(specs),
        ),
        compiler_params=pltpu.CompilerParams(
            dimension_semantics=("arbitrary",), vmem_limit_bytes=20 * 2**20
        ),
        cost_estimate=cost(1_000_000, [held, got], shapes),
        name=kernel.__name__,
    )(order, held, got)


def place_out(order, held, got):
    spec = pl.BlockSpec((PIECE, D), lambda s, o: (s, 0))
    return place(out_place_kernel, order, held, got, [(sds(HIDDEN, D, dtype=F32), spec)])[0]


def place_in(order, held, got):
    spec = pl.BlockSpec((D, PIECE), lambda s, o: (0, s))
    return place(in_place_kernel, order, held, got, [(sds(D, HIDDEN, dtype=F32), spec)])[0]


def place_attend(order, held, got):
    qkv = pl.BlockSpec((1, D, PIECE), lambda s, o: (jnp.minimum(s, 2), 0, 0))
    proj = pl.BlockSpec((PIECE, D), lambda s, o: (0, 0))
    return place(
        attend_place_kernel, order, held, got,
        [(sds(3, D, PIECE, dtype=F32), qkv), (sds(PIECE, D, dtype=F32), proj)],
    )


def swap(value):
    return lax.ppermute(value, "tensor", SWAP)


def flip(chip, core, stage, axis):
    pos = [chip % 4, chip // 4 % 4, chip // 16]
    low = (core == 0) == (stage == 0)
    pos[axis] = pos[axis] ^ 1 if low else 3 - pos[axis]
    return pos[0] + 4 * pos[1] + 16 * pos[2]


def exchange(value, stage, axis):
    pairs = [
        (2 * chip + core, 2 * flip(chip, core, stage, axis) + core)
        for chip in range(64)
        for core in range(2)
    ]
    return lax.ppermute(value, ("dp", "tensor"), pairs)


def my_orders():
    chip = lax.axis_index("dp")
    core = lax.axis_index("tensor")
    pos = [chip % 4, chip // 4 % 4, chip // 16]
    low = [(p ^ (p >> 1)) & 1 for p in pos]
    high = [p >> 1 for p in pos]
    near = [jnp.where(core == 0, a, b) for a, b in zip(low, high)]
    far = [jnp.where(core == 0, b, a) for a, b in zip(low, high)]
    outer = 4 * far[0] + 2 * far[1] + far[2]
    orders = []
    for turn in range(3):
        first, second, third = [near[(turn + j) % 3] for j in range(3)]
        orders.append(jnp.stack([first, second, third, outer]).astype(jnp.int32))
    return orders


def total(terms):
    out = terms[0].astype(F32)
    for term in terms[1:]:
        out = out + term.astype(F32)
    return out


def reduce_near(send, keep, turn):
    terms = [keep, exchange(send, 0, turn % 3)]
    for j in (1, 2):
        out = total([t[1] for t in terms]).astype(BF16)
        terms = [t[0] for t in terms] + [exchange(out, 0, (turn + j) % 3)]
    return terms


def reduce_far(chunks):
    groups = [[t.reshape((2, 2, 2) + BLOCK) for t in terms] for terms in chunks]
    for axis in range(3):
        out = jnp.stack([total([t[1] for t in terms]).astype(BF16) for terms in groups])
        got = exchange(out, 1, axis)
        groups = [[t[0] for t in terms] + [got[i]] for i, terms in enumerate(groups)]
    held = jnp.stack([total(terms).astype(BF16) for terms in groups])
    shape = held.shape
    held = held.reshape((shape[0], 1) + BLOCK)
    for axis in (2, 1, 0):
        held = jnp.concatenate([held, exchange(held, 1, axis)], axis=1)
    return [held[i] for i in range(shape[0])]


def spread_near(held, turn):
    for j in (2, 1):
        held = jnp.stack([held, exchange(held, 0, (turn + j) % 3)])
    return held, exchange(held, 0, turn % 3)


def sum_norms(value):
    for stage in range(2):
        for axis in range(3):
            value = value + exchange(value, stage, axis)
    return value


def on_device(
    tokens,
    skip_tokens,
    cot_back,
    cot_head,
    one_span,
    *params,
):
    lower = [p if p.ndim > 1 else p.reshape(1, -1) for p in params[:8]]
    upper = [p if p.ndim > 1 else p.reshape(1, -1) for p in params[8:]]
    side = lax.axis_index("tensor").astype(jnp.int32).reshape(1)
    spans = one_span
    orders = my_orders()

    tokens_other = swap(tokens)
    skip_other = swap(skip_tokens)
    cot_head_other = swap(cot_head)
    cot_back_other = swap(cot_back)

    x_l, qkv_l, prob_l, ctx_l, part = attend_first(side, spans, tokens, tokens_other, lower)
    first_l, low_l, normed_al, inv_al, act_l, slope_l, part = feed(x_l, part, swap(part), lower)
    x_u, normed_fl, inv_fl, back_out, qkv_u, prob_u, ctx_u, part = attend_second(
        side, spans, first_l, part, swap(part), lower[6], lower[7], skip_tokens, skip_other, upper
    )
    first_u, low_u, normed_au, inv_au, act_u, slope_u, part = feed(x_u, part, swap(part), upper)
    head_out, gs_u, gs_low_u, norms_fu, grad_pre_u, part = feed_back_second(
        side, spans, first_u, part, swap(part), cot_head, cot_head_other, slope_u, upper
    )
    split_out_u = out_grad(orders[0], act_u, gs_low_u)
    split_in_u = in_grad(orders[1], low_u, grad_pre_u)
    resid_u, gr_low_u, norms_au, grad_qkv_u, part = attend_back(
        gs_u, part, swap(part), normed_au, inv_au, qkv_u, prob_u, upper
    )
    split_at_u = attend_grad(orders[2], x_u, grad_qkv_u, ctx_u, gr_low_u)
    grad_skip, gs_l, gs_low_l, norms_fl, grad_pre_l, part = feed_back_first(
        side, spans, normed_fl, inv_fl, cot_back, cot_back_other, resid_u, part, swap(part),
        slope_l, lower,
    )
    split_out_l = out_grad(orders[0], act_l, gs_low_l)
    split_in_l = in_grad(orders[1], low_l, grad_pre_l)
    resid_l, gr_low_l, norms_al, grad_qkv_l, part = attend_back(
        gs_l, part, swap(part), normed_al, inv_al, qkv_l, prob_l, lower
    )
    split_at_l = attend_grad(orders[2], x_l, grad_qkv_l, ctx_l, gr_low_l)

    def mine_of(value, which):
        return lax.dynamic_slice_in_dim(value, which * HALF, HALF, 0)

    at = side[0]
    grad_tokens = (
        mine_of(resid_l, at)
        + mine_of(part, at).astype(F32)
        + swap(mine_of(part, 1 - at)).astype(F32)
    )

    sums = []
    for splits in ((split_out_u, split_in_u, split_at_u), (split_out_l, split_in_l, split_at_l)):
        chunks = [reduce_near(s[0], s[1], turn) for turn, s in enumerate(splits)]
        held = reduce_far(chunks)
        spreads = [spread_near(h, turn) for turn, h in enumerate(held)]
        w_out = place_out(orders[0], *spreads[0])
        w_in = place_in(orders[1], *spreads[1])
        qkv, proj = place_attend(orders[2], *spreads[2])
        sums.append((qkv, proj, w_in, w_out))

    norms = sum_norms(
        jnp.concatenate([norms_al[:2], norms_fl[:2], norms_au[:2], norms_fu[:2]])
    )
    (qkv_gu, proj_gu, in_gu, out_gu), (qkv_gl, proj_gl, in_gl, out_gl) = sums
    return (
        back_out,
        head_out,
        grad_tokens,
        grad_skip,
        qkv_gl,
        proj_gl,
        norms[0],
        norms[1],
        in_gl,
        out_gl,
        norms[2],
        norms[3],
        qkv_gu,
        proj_gu,
        norms[4],
        norms[5],
        in_gu,
        out_gu,
        norms[6],
        norms[7],
    )


def solution(mesh):
    rows = P(("dp", "tensor"), None)
    weights = (
        P(None, None, "tensor"),
        P("tensor", None),
        P(),
        P(),
        P(None, "tensor"),
        P("tensor", None),
        P(),
        P(),
    )
    return jax.shard_map(
        on_device,
        mesh=mesh,
        in_specs=(rows,) * 4 + (P("dp"),) + weights + weights,
        out_specs=(rows,) * 4 + weights + weights,
        check_vma=False,
    )
```

```python
import functools

import jax
import jax.numpy as jnp
import numpy as np
from jax import lax
from jax.experimental import pallas as pl
from jax.experimental.pallas import tpu as pltpu
from jax.sharding import PartitionSpec as P

SPAN = 128
EPS = 1e-06
SCALE = 0.125
NEG = -1000000000.0

D = 768
ROWS = 768
HALF = ROWS // 2
HIDDEN = 1536
PIECE = 384
PAIR = 128
BLOCK = (48, 384)
F32 = jnp.float32
BF16 = jnp.bfloat16

SWAP = [(0, 1), (1, 0)]


def dot_nn(left, right):
    return lax.dot_general(left, right, (((1,), (0,)), ((), ())), preferred_element_type=F32)


def dot_nt(left, right):
    return lax.dot_general(left, right, (((1,), (1,)), ((), ())), preferred_element_type=F32)


def dot_tn(left, right):
    return lax.dot_general(left, right, (((0,), (0,)), ((), ())), preferred_element_type=F32)


def normalize(resid):
    mean = jnp.mean(resid, axis=-1, keepdims=True)
    centered = resid - mean
    var = jnp.mean(centered * centered, axis=-1, keepdims=True)
    inv = lax.rsqrt(var + EPS)
    return centered * inv, inv


def norm_grad(grad_out, normed, inv, gain):
    grad = grad_out * gain
    first = jnp.mean(grad, axis=-1, keepdims=True)
    second = jnp.mean(grad * normed, axis=-1, keepdims=True)
    return inv * (grad - first - normed * second)


def fold(value):
    return jnp.sum(value.reshape(-1, 8, value.shape[-1]), axis=0)

DOC = 2 * SPAN
DOCS = ROWS // DOC


def doc_rows(doc):
    return slice(doc * DOC, (doc + 1) * DOC)


def half_rows(index):
    return pl.ds(pl.multiple_of(index * HALF, HALF), HALF)


def join_halves(side, own_ref, other_ref, full_ref):
    full_ref[half_rows(side), :] = own_ref[...]
    full_ref[half_rows(1 - side), :] = other_ref[...]


def doc_masks(spans_ref, doc):
    row = lax.broadcasted_iota(jnp.int32, (DOC, 1), 0)
    keep = jnp.where((row < SPAN) | (spans_ref[doc] == 0), 1.0, 0.0)
    return keep, (row & (SPAN - 1)) == 0


def spread(column):
    return jnp.broadcast_to(column, (column.shape[0], 128))


def head_masks():
    lane = lax.broadcasted_iota(jnp.int32, (1, PAIR), 1)
    return lane < 64


def both_heads(value, left):
    zero = jnp.zeros_like(value)
    return jnp.concatenate([jnp.where(left, value, zero), jnp.where(left, zero, value)], axis=0)


def attend(spans_ref, x_ref, qkv_w_ref, proj_ref, qkv_ref, prob_ref, ctx_ref, part_ref, wide):
    for index in range(3):
        wide[:, index * 384:(index + 1) * 384] = qkv_w_ref[index]
    for doc in range(DOCS):
        at = doc_rows(doc)
        out = dot_nn(x_ref[at, :], wide[...])
        qkv_ref[at, :384] = (out[:, :384] * SCALE).astype(BF16)
        qkv_ref[at, 384:] = out[:, 384:].astype(BF16)
    left = head_masks()
    col = lax.broadcasted_iota(jnp.int32, (1, 2 * DOC), 1) & (DOC - 1)
    for doc in range(DOCS):
        at = doc_rows(doc)
        key_ok = (col < SPAN) | (spans_ref[doc] == 0)
        scores = []
        for pair in range(3):
            query = qkv_ref[at, pair * PAIR:(pair + 1) * PAIR]
            keys = qkv_ref[at, 384 + pair * PAIR:384 + (pair + 1) * PAIR]
            scores.append(jnp.where(key_ok, dot_nt(query, both_heads(keys, left)), NEG))
        for pair in range(3):
            probs = []
            for head in range(2):
                score = scores[pair][:, head * DOC:(head + 1) * DOC]
                raised = jnp.exp(score - jnp.max(score, axis=-1, keepdims=True))
                probs.append(
                    (raised * (1.0 / jnp.sum(raised, axis=-1, keepdims=True))).astype(BF16)
                )
            prob = jnp.concatenate(probs, axis=1)
            prob_ref[doc, pair] = prob
            values = qkv_ref[at, 768 + pair * PAIR:768 + (pair + 1) * PAIR]
            mixed = dot_nn(prob, both_heads(values, left))
            ctx_ref[at, pair * PAIR:(pair + 1) * PAIR] = mixed.astype(BF16)
    for doc in range(DOCS):
        at = doc_rows(doc)
        part_ref[at, :] = dot_nn(ctx_ref[at, :], proj_ref[...]).astype(BF16)


def attend_first_kernel(
    ids_ref, spans_ref, own_ref, other_ref, qkv_w_ref, proj_ref,
    x_ref, qkv_ref, prob_ref, ctx_ref, part_ref, wide,
):
    join_halves(ids_ref[0], own_ref, other_ref, x_ref)
    attend(spans_ref, x_ref, qkv_w_ref, proj_ref, qkv_ref, prob_ref, ctx_ref, part_ref, wide)


def attend_second_kernel(
    base, ids_ref, spans_ref, first_ref, mine_ref, theirs_ref, vec_ref, own_ref, other_ref,
    qkv_w_ref, proj_ref,
    x_ref, normed_ref, inv_ref, out_ref, qkv_ref, prob_ref, ctx_ref, part_ref, wide, full,
):
    side = ids_ref[0]
    join_halves(side, own_ref, other_ref, x_ref)
    for doc in range(DOCS):
        at = doc_rows(doc)
        keep, cls = doc_masks(spans_ref, doc)
        resid = first_ref[at, :] + mine_ref[at, :].astype(F32) + theirs_ref[at, :].astype(F32)
        normed, inv = normalize(resid)
        back = normed * vec_ref[base:base + 1, :] + vec_ref[base + 1:base + 2, :]
        normed_ref[at, :] = normed.astype(BF16)
        inv_ref[at, :] = spread(inv)
        x_ref[at, :] = jnp.where(cls, back, x_ref[at, :].astype(F32)).astype(BF16)
        full[at, :] = (back * keep).astype(BF16)
    out_ref[...] = full[half_rows(side), :]
    attend(spans_ref, x_ref, qkv_w_ref, proj_ref, qkv_ref, prob_ref, ctx_ref, part_ref, wide)


def feed_kernel(
    base, x_ref, mine_ref, theirs_ref, vec_ref, in_ref, out_w_ref,
    first_ref, low_ref, normed_ref, inv_ref, act_ref, slope_ref, part_ref,
):
    for doc in range(DOCS):
        at = doc_rows(doc)
        resid = x_ref[at, :].astype(F32) + mine_ref[at, :].astype(F32) + theirs_ref[at, :].astype(F32)
        normed, inv = normalize(resid)
        first = normed * vec_ref[base:base + 1, :] + vec_ref[base + 1:base + 2, :]
        normed_ref[at, :] = normed.astype(BF16)
        inv_ref[at, :] = spread(inv)
        first_ref[at, :] = first
        low_ref[at, :] = first.astype(BF16)
    for doc in range(DOCS):
        at = doc_rows(doc)
        for piece in range(3):
            cut = slice(piece * 512, (piece + 1) * 512)
            pre = dot_nn(low_ref[at, :], in_ref[:, cut])
            share = 0.5 * (1.0 + lax.erf(pre * 0.7071067811865476))
            density = jnp.exp(-0.5 * pre * pre) * 0.3989422804014327
            act_ref[at, cut] = (pre * share).astype(BF16)
            slope_ref[at, cut] = (share + pre * density).astype(BF16)
    for doc in range(DOCS):
        at = doc_rows(doc)
        part_ref[at, :] = dot_nn(act_ref[at, :], out_w_ref[...]).astype(BF16)


def feed_back(gs_low_ref, slope_ref, in_ref, out_w_ref, grad_pre_ref, part_ref):
    for doc in range(DOCS):
        at = doc_rows(doc)
        for piece in range(3):
            cut = slice(piece * 512, (piece + 1) * 512)
            grad_act = dot_nt(gs_low_ref[at, :], out_w_ref[cut, :])
            grad_pre_ref[at, cut] = (grad_act * slope_ref[at, cut].astype(F32)).astype(BF16)
    for doc in range(DOCS):
        at = doc_rows(doc)
        part_ref[at, :] = dot_nt(grad_pre_ref[at, :], in_ref[...]).astype(BF16)


def put_norm_grads(norms_ref, sums):
    gain, shift = sums
    norms_ref[...] = jnp.zeros_like(norms_ref)
    norms_ref[0:1, :] = jnp.sum(gain, axis=0, keepdims=True)
    norms_ref[1:2, :] = jnp.sum(shift, axis=0, keepdims=True)


def add_sums(sums, grad_out, normed):
    new = (fold(grad_out * normed), fold(grad_out))
    return new if sums is None else (sums[0] + new[0], sums[1] + new[1])


def feed_back_second_kernel(
    base, ids_ref, spans_ref, first_ref, mine_ref, theirs_ref, vec_ref, own_ref, other_ref,
    slope_ref, in_ref, out_w_ref,
    head_ref, gs_ref, gs_low_ref, norms_ref, grad_pre_ref, part_ref, cot, full,
):
    side = ids_ref[0]
    join_halves(side, own_ref, other_ref, cot)
    sums = None
    for doc in range(DOCS):
        at = doc_rows(doc)
        keep, _ = doc_masks(spans_ref, doc)
        resid = first_ref[at, :] + mine_ref[at, :].astype(F32) + theirs_ref[at, :].astype(F32)
        normed, inv = normalize(resid)
        head = normed * vec_ref[base:base + 1, :] + vec_ref[base + 1:base + 2, :]
        full[at, :] = (head * keep).astype(BF16)
        grad_out = cot[at, :].astype(F32) * keep
        grad = norm_grad(grad_out, normed, inv, vec_ref[base:base + 1, :])
        gs_ref[at, :] = grad
        gs_low_ref[at, :] = grad.astype(BF16)
        sums = add_sums(sums, grad_out, normed)
    head_ref[...] = full[half_rows(side), :]
    put_norm_grads(norms_ref, sums)
    feed_back(gs_low_ref, slope_ref, in_ref, out_w_ref, grad_pre_ref, part_ref)


def feed_back_first_kernel(
    base, ids_ref, spans_ref, normed_ref, inv_ref, vec_ref, own_ref, other_ref,
    resid_ref, mine_ref, theirs_ref, slope_ref, in_ref, out_w_ref,
    skip_ref, gs_ref, gs_low_ref, norms_ref, grad_pre_ref, part_ref, cot, full,
):
    side = ids_ref[0]
    join_halves(side, own_ref, other_ref, cot)
    sums = None
    for doc in range(DOCS):
        at = doc_rows(doc)
        keep, cls = doc_masks(spans_ref, doc)
        above = resid_ref[at, :] + mine_ref[at, :].astype(F32) + theirs_ref[at, :].astype(F32)
        full[at, :] = jnp.where(cls, 0.0, above)
        normed = normed_ref[at, :].astype(F32)
        grad_out = cot[at, :].astype(F32) * keep + jnp.where(cls, above, 0.0)
        grad = norm_grad(grad_out, normed, inv_ref[at, 0:1], vec_ref[base:base + 1, :])
        gs_ref[at, :] = grad
        gs_low_ref[at, :] = grad.astype(BF16)
        sums = add_sums(sums, grad_out, normed)
    skip_ref[...] = full[half_rows(side), :]
    put_norm_grads(norms_ref, sums)
    feed_back(gs_low_ref, slope_ref, in_ref, out_w_ref, grad_pre_ref, part_ref)


def attend_back_kernel(
    base, ids_ref, gs_ref, mine_ref, theirs_ref, normed_ref, inv_ref, vec_ref, qkv_ref, prob_ref,
    qkv_w_ref, proj_ref,
    resid_ref, low_ref, norms_ref, grad_qkv_ref, part_ref, away_ref, grad_ctx, wide,
):
    for index in range(3):
        wide[:, index * 384:(index + 1) * 384] = qkv_w_ref[index]
    sums = None
    for doc in range(DOCS):
        at = doc_rows(doc)
        grad_out = gs_ref[at, :] + mine_ref[at, :].astype(F32) + theirs_ref[at, :].astype(F32)
        normed = normed_ref[at, :].astype(F32)
        grad = norm_grad(grad_out, normed, inv_ref[at, 0:1], vec_ref[base:base + 1, :])
        resid_ref[at, :] = grad
        low_ref[at, :] = grad.astype(BF16)
        sums = add_sums(sums, grad_out, normed)
    put_norm_grads(norms_ref, sums)
    for doc in range(DOCS):
        at = doc_rows(doc)
        grad_ctx[at, :] = dot_nt(low_ref[at, :], proj_ref[...]).astype(BF16)
    left = head_masks()
    for doc in range(DOCS):
        at = doc_rows(doc)
        pairs = [slice(pair * PAIR, (pair + 1) * PAIR) for pair in range(3)]
        grad_probs = []
        for pair in range(3):
            values = qkv_ref[at, 768 + pair * PAIR:768 + (pair + 1) * PAIR]
            grad_probs.append(dot_nt(grad_ctx[at, pairs[pair]], both_heads(values, left)))
        for pair in range(3):
            prob_low = prob_ref[doc, pair]
            scored = []
            for head in range(2):
                cut = slice(head * DOC, (head + 1) * DOC)
                prob = prob_low[:, cut].astype(F32)
                grad_prob = grad_probs[pair][:, cut]
                inner = jnp.sum(grad_prob * prob, axis=-1, keepdims=True)
                scored.append((prob * (grad_prob - inner)).astype(BF16))
            grad_scores = jnp.concatenate(scored, axis=1)
            query = qkv_ref[at, pairs[pair]]
            keys = qkv_ref[at, 384 + pair * PAIR:384 + (pair + 1) * PAIR]
            grad_query = dot_nn(grad_scores, both_heads(keys, left)) * SCALE
            grad_keys = dot_tn(grad_scores, query)
            grad_values = dot_tn(prob_low, grad_ctx[at, pairs[pair]])
            grad_qkv_ref[at, pair * PAIR:(pair + 1) * PAIR] = grad_query.astype(BF16)
            for index, grad in ((1, grad_keys), (2, grad_values)):
                cut = slice(index * 384 + pair * PAIR, index * 384 + (pair + 1) * PAIR)
                grad_qkv_ref[at, cut] = jnp.where(left, grad[:DOC], grad[DOC:]).astype(BF16)
    for doc in range(DOCS):
        at = doc_rows(doc)
        part_ref[at, :] = dot_nt(grad_qkv_ref[at, :], wide[...]).astype(BF16)
    if base == 0:
        away_ref[...] = part_ref[half_rows(1 - ids_ref[0]), :]
    else:
        away_ref[...] = jnp.zeros_like(away_ref)


def rows_kernel(ids_ref, resid_ref, mine_ref, theirs_ref, out_ref):
    at = half_rows(ids_ref[0])
    out_ref[...] = resid_ref[at, :] + mine_ref[at, :].astype(F32) + theirs_ref[...].astype(F32)


def cut_wide(value, blocks, piece):
    for half in range(2):
        for k in range(8):
            blocks[piece, half, k] = value[k * 48:(k + 1) * 48, half * 384:(half + 1) * 384]


def cut_tall(value, blocks, piece):
    for half in range(2):
        for k in range(8):
            at = half * 384 + k * 48
            blocks[piece, half, k] = value[at:at + 48, :]


def put_blocks(ids_ref, turn, blocks, send_ref, keep_ref):
    first, second, third, outer = [ids_ref[1 + 4 * turn + i] for i in range(4)]
    for rel, ref in ((1, send_ref), (0, keep_ref)):
        for b in range(2):
            piece = 2 * (rel ^ first) + (b ^ second)
            for e in range(2):
                for k in range(8):
                    ref[b, e, k] = blocks[piece, e ^ third, k ^ outer]


def out_grad_kernel(turn, ids_ref, act_ref, gs_ref, send_ref, keep_ref, blocks):
    for p in range(2):
        value = dot_tn(act_ref[:, p * 768:(p + 1) * 768], gs_ref[...]).astype(BF16)
        cut_wide(value[:384], blocks, 2 * p)
        cut_wide(value[384:], blocks, 2 * p + 1)
    put_blocks(ids_ref, turn, blocks, send_ref, keep_ref)


def in_grad_kernel(turn, ids_ref, low_ref, grad_ref, send_ref, keep_ref, blocks):
    for p in range(2):
        value = dot_tn(low_ref[...], grad_ref[:, p * 768:(p + 1) * 768]).astype(BF16)
        cut_tall(value[:, :384], blocks, 2 * p)
        cut_tall(value[:, 384:], blocks, 2 * p + 1)
    put_blocks(ids_ref, turn, blocks, send_ref, keep_ref)


def attend_grad_kernel(turn, ids_ref, x_ref, grad_ref, ctx_ref, low_ref, send_ref, keep_ref, blocks):
    value = dot_tn(x_ref[...], grad_ref[...]).astype(BF16)
    for piece in range(3):
        cut_tall(value[:, piece * 384:(piece + 1) * 384], blocks, piece)
    cut_wide(dot_tn(ctx_ref[...], low_ref[...]).astype(BF16), blocks, 3)
    put_blocks(ids_ref, turn, blocks, send_ref, keep_ref)


def join_kernel(held_ref, got_ref, out_ref):
    out_ref[0] = held_ref[...]
    out_ref[1] = got_ref[...]


def place_kernel(turn, far, ids_ref, from_ref, *refs):
    outs, squares, sems = refs[-2 - (2 if turn == 2 else 1):-2], refs[-2], refs[-1]
    first, second, third, outer = [ids_ref[1 + 4 * turn + i] for i in range(4)]

    def copy(b, e, ref):
        return pltpu.make_async_copy(squares.at[b, e], ref, sems.at[b, e])

    def places(b, e):
        piece = 2 * (far ^ first) + (b ^ second)
        at = pl.ds(pl.multiple_of(piece * PIECE, PIECE), PIECE)
        cut = slice(e * PIECE, (e + 1) * PIECE)
        if turn == 0:
            return [(None, outs[0].at[at, cut])]
        if turn == 1:
            return [(None, outs[0].at[cut, at])]
        return [
            (piece < 3, outs[0].at[jnp.minimum(piece, 2), cut, :]),
            (piece == 3, outs[1].at[:, cut]),
        ]

    def each(b, e, act):
        for when, ref in places(b, e):
            if when is None:
                act(copy(b, e, ref))
            else:
                pl.when(when)(functools.partial(lambda c: act(c), copy(b, e, ref)))

    for b in range(2):
        for e in range(2):
            for k in range(8):
                squares[b, e, k * 48:(k + 1) * 48, :] = from_ref[b, e ^ third, k ^ outer].astype(F32)
            each(b, e, lambda c: c.start())
    for b in range(2):
        for e in range(2):
            each(b, e, lambda c: c.wait())


def sds(*shape, dtype=BF16):
    return jax.ShapeDtypeStruct(shape, dtype)


SCALARS = pl.BlockSpec(memory_space=pltpu.SMEM)
LOCAL = pl.BlockSpec(memory_space=pltpu.VMEM)


def cost(flops, arrays, outs):
    moved = sum(a.size * a.dtype.itemsize for a in list(arrays) + list(outs))
    return pl.CostEstimate(flops=flops, bytes_accessed=moved, transcendentals=0)


LIMITS = {
    "attend_second_kernel": 14,
    "feed_back_second_kernel": 15,
    "feed_back_first_kernel": 14,
}


def run(kernel, scalars, arrays, outs, scratch, flops, *fixed):
    name = kernel.__name__
    return pl.pallas_call(
        functools.partial(kernel, *fixed),
        out_shape=list(outs),
        in_specs=[SCALARS] * len(scalars) + [LOCAL] * len(arrays),
        out_specs=[LOCAL] * len(outs),
        scratch_shapes=scratch,
        compiler_params=pltpu.CompilerParams(vmem_limit_bytes=LIMITS.get(name, 12) * 2**20),
        cost_estimate=cost(flops, arrays, outs),
        name=name,
    )(*scalars, *arrays)


STATS = sds(ROWS, 128, dtype=F32)
ATTEND_OUTS = [sds(ROWS, 1152), sds(3, 3, DOC, 2 * DOC), sds(ROWS, PIECE), sds(ROWS, D)]
WIDE = pltpu.VMEM((D, 1152), BF16)


def attend_first(ids, spans, own, other, weights):
    return run(
        attend_first_kernel, [ids, spans], [own, other, weights[0], weights[1]],
        [sds(ROWS, D)] + ATTEND_OUTS, [WIDE], 2_400_000_000,
    )


def attend_second(ids, spans, first, mine, theirs, vec, own, other, weights):
    return run(
        attend_second_kernel, [ids, spans],
        [first, mine, theirs, vec, own, other, weights[0], weights[1]],
        [sds(ROWS, D), sds(ROWS, D), STATS, sds(HALF, D)] + ATTEND_OUTS,
        [WIDE, pltpu.VMEM((ROWS, D), BF16)], 2_400_000_000, 2,
    )


def feed(base, x, mine, theirs, vec, weights):
    return run(
        feed_kernel, [], [x, mine, theirs, vec, weights[2], weights[3]],
        [sds(ROWS, D, dtype=F32), sds(ROWS, D), sds(ROWS, D), STATS,
         sds(ROWS, HIDDEN), sds(ROWS, HIDDEN), sds(ROWS, D)],
        [], 3_600_000_000, base,
    )


FEED_BACK_OUTS = [
    sds(ROWS, D, dtype=F32), sds(ROWS, D), sds(8, D, dtype=F32), sds(ROWS, HIDDEN), sds(ROWS, D),
]


def feed_back_second(ids, spans, first, mine, theirs, vec, own, other, slope, weights):
    return run(
        feed_back_second_kernel, [ids, spans],
        [first, mine, theirs, vec, own, other, slope, weights[2], weights[3]],
        [sds(HALF, D)] + FEED_BACK_OUTS,
        [pltpu.VMEM((ROWS, D), BF16), pltpu.VMEM((ROWS, D), BF16)], 3_600_000_000, 6,
    )


def feed_back_first(ids, spans, normed, inv, vec, own, other, resid, mine, theirs, slope, weights):
    return run(
        feed_back_first_kernel, [ids, spans],
        [normed, inv, vec, own, other, resid, mine, theirs, slope, weights[2], weights[3]],
        [sds(HALF, D, dtype=F32)] + FEED_BACK_OUTS,
        [pltpu.VMEM((ROWS, D), BF16), pltpu.VMEM((ROWS, D), F32)], 3_600_000_000, 2,
    )


def attend_back(base, ids, gs, mine, theirs, normed, inv, qkv, prob, vec, weights):
    return run(
        attend_back_kernel, [ids],
        [gs, mine, theirs, normed, inv, vec, qkv, prob, weights[0], weights[1]],
        [sds(ROWS, D, dtype=F32), sds(ROWS, D), sds(8, D, dtype=F32), sds(ROWS, 1152), sds(ROWS, D),
         sds(HALF if base == 0 else 16, D)],
        [pltpu.VMEM((ROWS, PIECE), BF16), WIDE], 2_800_000_000, base,
    )


SPLIT_OUTS = [sds(2, 2, 8, *BLOCK), sds(2, 2, 8, *BLOCK)]
BLOCKS = pltpu.VMEM((4, 2, 8) + BLOCK, BF16)


def out_grad(ids, act, gs_low):
    return run(out_grad_kernel, [ids], [act, gs_low], SPLIT_OUTS, [BLOCKS], 1_800_000_000, 0)


def in_grad(ids, low, grad_pre):
    return run(in_grad_kernel, [ids], [low, grad_pre], SPLIT_OUTS, [BLOCKS], 1_800_000_000, 1)


def attend_grad(ids, x, grad_qkv, ctx, low):
    return run(
        attend_grad_kernel, [ids], [x, grad_qkv, ctx, low], SPLIT_OUTS, [BLOCKS], 1_800_000_000, 2
    )


def join(held, got):
    return run(join_kernel, [], [held, got], [sds(2, *held.shape)], [], 1_000)[0]


PLACED = [
    [sds(HIDDEN, D, dtype=F32)],
    [sds(D, HIDDEN, dtype=F32)],
    [sds(3, D, PIECE, dtype=F32), sds(PIECE, D, dtype=F32)],
]
REMOTE = pl.BlockSpec(memory_space=pl.ANY)


def place(ids, turn, far, value, into=()):
    outs = PLACED[turn]
    return pl.pallas_call(
        functools.partial(place_kernel, turn, far),
        out_shape=outs,
        in_specs=[SCALARS, LOCAL] + [REMOTE] * len(into),
        out_specs=[REMOTE] * len(outs),
        scratch_shapes=[
            pltpu.VMEM((2, 2, PIECE, PIECE), F32),
            pltpu.SemaphoreType.DMA((2, 2)),
        ],
        input_output_aliases={2 + i: i for i in range(len(into))},
        compiler_params=pltpu.CompilerParams(vmem_limit_bytes=12 * 2**20),
        cost_estimate=pl.CostEstimate(flops=1_000, bytes_accessed=7_000_000, transcendentals=0),
        name="place_kernel",
    )(ids, value, *into)


def swap(value):
    return lax.ppermute(value, "tensor", SWAP)


def flip(chip, core, stage, axis):
    pos = [chip % 4, chip // 4 % 4, chip // 16]
    low = (core == 0) == (stage == 0)
    pos[axis] = pos[axis] ^ 1 if low else 3 - pos[axis]
    return pos[0] + 4 * pos[1] + 16 * pos[2]


def exchange(value, stage, axis):
    pairs = [
        (2 * chip + core, 2 * flip(chip, core, stage, axis) + core)
        for chip in range(64)
        for core in range(2)
    ]
    return lax.ppermute(value, ("dp", "tensor"), pairs)


def device_table():
    rows = []
    for chip in range(64):
        pos = [chip % 4, chip // 4 % 4, chip // 16]
        low = [(p ^ (p >> 1)) & 1 for p in pos]
        high = [p >> 1 for p in pos]
        for core in range(2):
            near = low if core == 0 else high
            row = [core]
            for turn in range(3):
                row += [near[turn], near[(turn + 1) % 3], near[(turn + 2) % 3], 0]
            rows.append(row + [0, 0, 0])
    return np.array(rows, np.int32)


def after(value, token):
    return lax.optimization_barrier((value, token))[0]


def added(one, two):
    return (one.astype(F32) + two.astype(F32)).astype(BF16)


class Chunk:
    def __init__(self, turn, send, keep):
        self.turn, self.keep, self.round = turn, keep, 0
        self.got = exchange(send, 0, turn)

    def axis(self, j):
        return (self.turn + j) % 3

    def next(self, token=None):
        got = self.got if token is None else after(self.got, token)
        self.round += 1
        if self.round < 3:
            send = added(self.keep[1], got[1])
            self.keep = added(self.keep[0], got[0])
            self.got = exchange(send, 0, self.axis(self.round))
        elif self.round < 6:
            self.keep = added(self.keep, got)
            self.got = exchange(self.keep, 1, self.axis(self.round))
        elif self.round == 6:
            self.keep = added(self.keep, got)
            self.got = exchange(self.keep, 0, self.axis(2))
        else:
            self.keep = join(self.keep, got)
            self.got = exchange(self.keep, 0, self.axis(8 - self.round))

    def finish(self, ids):
        part = place(ids, self.turn, 0, self.keep)
        return place(ids, self.turn, 1, self.got, part)


def sum_norms(value):
    for stage in range(2):
        for axis in range(3):
            value = value + exchange(value, stage, axis)
            yield value


def on_device(
    tokens,
    skip_tokens,
    cot_back,
    cot_head,
    one_span,
    *params,
):
    lower = [params[i] for i in (0, 1, 4, 5)]
    upper = [params[i] for i in (8, 9, 12, 13)]
    vec = jnp.stack([params[i] for i in (2, 3, 6, 7, 10, 11, 14, 15)])
    device = lax.axis_index("dp") * 2 + lax.axis_index("tensor")
    ids = lax.dynamic_index_in_dim(jnp.asarray(device_table()), device, 0, keepdims=False)
    spans = one_span

    tokens_other = swap(tokens)
    tokens, ids, vec = lax.optimization_barrier((tokens, ids, vec))
    skip_other = swap(skip_tokens)
    cot_head_other = swap(cot_head)
    cot_back_other = swap(cot_back)

    x_l, qkv_l, prob_l, ctx_l, part = attend_first(ids, spans, tokens, tokens_other, lower)
    first_l, low_l, normed_al, inv_al, act_l, slope_l, part = feed(
        0, x_l, part, swap(part), vec, lower
    )
    x_u, normed_fl, inv_fl, back_out, qkv_u, prob_u, ctx_u, part = attend_second(
        ids, spans, first_l, part, swap(part), vec, skip_tokens, skip_other, upper
    )
    first_u, low_u, normed_au, inv_au, act_u, slope_u, part = feed(
        4, x_u, part, swap(part), vec, upper
    )
    head_out, gs_u, gs_low_u, norms_fu, grad_pre_u, part = feed_back_second(
        ids, spans, first_u, part, swap(part), vec, cot_head, cot_head_other, slope_u, upper
    )
    out_u = Chunk(0, *out_grad(ids, act_u, gs_low_u))
    in_u = Chunk(1, *in_grad(ids, low_u, grad_pre_u))
    resid_u, gr_low_u, norms_au, grad_qkv_u, part, _ = attend_back(
        4, ids, gs_u, part, swap(part), normed_au, inv_au, qkv_u, prob_u, vec=vec, weights=upper
    )
    split = attend_grad(ids, x_u, grad_qkv_u, ctx_u, gr_low_u)
    at_u = Chunk(2, *split)
    out_u.next(split[0])
    in_u.next(split[0])
    grad_skip, gs_l, gs_low_l, norms_fl, grad_pre_l, part = feed_back_first(
        ids, spans, normed_fl, inv_fl, vec, cot_back, cot_back_other, resid_u, part, swap(part),
        slope_l, lower,
    )
    out_u.next(gs_low_l)
    in_u.next(gs_low_l)
    split = out_grad(ids, act_l, gs_low_l)
    out_l = Chunk(0, *split)
    split = in_grad(ids, low_l, grad_pre_l)
    in_l = Chunk(1, *split)
    at_u.next(split[0])
    out_u.next(split[0])
    in_u.next(split[0])
    resid_l, gr_low_l, norms_al, grad_qkv_l, part, away = attend_back(
        0, ids, gs_l, part, swap(part), normed_al, inv_al, qkv_l, prob_l, vec=vec, weights=lower
    )
    split = attend_grad(ids, x_l, grad_qkv_l, ctx_l, gr_low_l)
    at_l = Chunk(2, *split)
    for chunk in (out_l, in_l, at_u, out_u, in_u):
        chunk.next(split[0])

    grad_tokens = run(
        rows_kernel, [ids], [resid_l, part, swap(away)], [sds(HALF, D, dtype=F32)], [], 1_000_000
    )[0]
    steps = sum_norms(
        jnp.concatenate([norms_al[:2], norms_fl[:2], norms_au[:2], norms_fu[:2]])
    )
    at_l.next(next(steps))
    at_l.next((next(steps), grad_tokens))
    for _ in range(4):
        norms = next(steps)
        at_l.next(norms)
    upper_chunks, lower_chunks = (out_u, in_u, at_u), (out_l, in_l, at_l)
    for chunk in upper_chunks:
        while chunk.round < 8:
            chunk.next()
    done_u = [chunk.finish(ids) for chunk in upper_chunks]
    for chunk, done in zip(lower_chunks, done_u):
        while chunk.round < 7:
            chunk.next()
        chunk.next(done[0])
    done_out_u, done_in_u, done_at_u = done_u
    done_out_l, done_in_l, done_at_l = [chunk.finish(ids) for chunk in lower_chunks]
    return (
        back_out,
        head_out,
        grad_tokens,
        grad_skip,
        *done_at_l,
        norms[0],
        norms[1],
        *done_in_l,
        *done_out_l,
        norms[2],
        norms[3],
        *done_at_u,
        norms[4],
        norms[5],
        *done_in_u,
        *done_out_u,
        norms[6],
        norms[7],
    )


def solution(mesh):
    rows = P(("dp", "tensor"), None)
    weights = (
        P(None, None, "tensor"),
        P("tensor", None),
        P(),
        P(),
        P(None, "tensor"),
        P("tensor", None),
        P(),
        P(),
    )
    return jax.shard_map(
        on_device,
        mesh=mesh,
        in_specs=(rows,) * 4 + (P("dp"),) + weights + weights,
        out_specs=(rows,) * 4 + weights + weights,
        check_vma=False,
    )
```

```python
import functools

import jax
import jax.numpy as jnp
import numpy as np
from jax import lax
from jax.experimental import pallas as pl
from jax.experimental.pallas import tpu as pltpu
from jax.sharding import PartitionSpec as P

SPAN = 128
EPS = 1e-06
SCALE = 0.125
NEG = -1000000000.0

D = 768
ROWS = 768
HALF = ROWS // 2
HIDDEN = 1536
PIECE = 384
PAIR = 128
BLOCK = (48, 384)
F32 = jnp.float32
BF16 = jnp.bfloat16

SWAP = [(0, 1), (1, 0)]


def dot_nn(left, right):
    return lax.dot_general(left, right, (((1,), (0,)), ((), ())), preferred_element_type=F32)


def dot_nt(left, right):
    return lax.dot_general(left, right, (((1,), (1,)), ((), ())), preferred_element_type=F32)


def dot_tn(left, right):
    return lax.dot_general(left, right, (((0,), (0,)), ((), ())), preferred_element_type=F32)


def normalize(resid):
    mean = jnp.mean(resid, axis=-1, keepdims=True)
    centered = resid - mean
    var = jnp.mean(centered * centered, axis=-1, keepdims=True)
    inv = lax.rsqrt(var + EPS)
    return centered * inv, inv


def norm_grad(grad_out, normed, inv, gain):
    grad = grad_out * gain
    first = jnp.mean(grad, axis=-1, keepdims=True)
    second = jnp.mean(grad * normed, axis=-1, keepdims=True)
    return inv * (grad - first - normed * second)


def fold(value):
    return jnp.sum(value.reshape(-1, 8, value.shape[-1]), axis=0)

DOC = 2 * SPAN
DOCS = ROWS // DOC


def doc_rows(doc):
    return slice(doc * DOC, (doc + 1) * DOC)


def half_rows(index):
    return pl.ds(pl.multiple_of(index * HALF, HALF), HALF)


def join_halves(side, own_ref, other_ref, full_ref):
    full_ref[half_rows(side), :] = own_ref[...]
    full_ref[half_rows(1 - side), :] = other_ref[...]


def doc_masks(spans_ref, doc):
    row = lax.broadcasted_iota(jnp.int32, (DOC, 1), 0)
    keep = jnp.where((row < SPAN) | (spans_ref[doc] == 0), 1.0, 0.0)
    return keep, (row & (SPAN - 1)) == 0


def spread(column):
    return jnp.broadcast_to(column, (column.shape[0], 128))


def head_masks():
    lane = lax.broadcasted_iota(jnp.int32, (1, PAIR), 1)
    return lane < 64


def both_heads(value, left):
    zero = jnp.zeros_like(value)
    return jnp.concatenate([jnp.where(left, value, zero), jnp.where(left, zero, value)], axis=0)


def attend(spans_ref, x_ref, qkv_w_ref, proj_ref, qkv_ref, prob_ref, ctx_ref, part_ref, wide):
    for index in range(3):
        wide[:, index * 384:(index + 1) * 384] = qkv_w_ref[index]
    for doc in range(DOCS):
        at = doc_rows(doc)
        out = dot_nn(x_ref[at, :], wide[...])
        qkv_ref[at, :384] = (out[:, :384] * SCALE).astype(BF16)
        qkv_ref[at, 384:] = out[:, 384:].astype(BF16)
    left = head_masks()
    col = lax.broadcasted_iota(jnp.int32, (1, 2 * DOC), 1) & (DOC - 1)
    for doc in range(DOCS):
        at = doc_rows(doc)
        key_ok = (col < SPAN) | (spans_ref[doc] == 0)
        scores = []
        for pair in range(3):
            query = qkv_ref[at, pair * PAIR:(pair + 1) * PAIR]
            keys = qkv_ref[at, 384 + pair * PAIR:384 + (pair + 1) * PAIR]
            scores.append(jnp.where(key_ok, dot_nt(query, both_heads(keys, left)), NEG))
        for pair in range(3):
            probs = []
            for head in range(2):
                score = scores[pair][:, head * DOC:(head + 1) * DOC]
                raised = jnp.exp(score - jnp.max(score, axis=-1, keepdims=True))
                probs.append(
                    (raised * (1.0 / jnp.sum(raised, axis=-1, keepdims=True))).astype(BF16)
                )
            prob = jnp.concatenate(probs, axis=1)
            prob_ref[doc, pair] = prob
            values = qkv_ref[at, 768 + pair * PAIR:768 + (pair + 1) * PAIR]
            mixed = dot_nn(prob, both_heads(values, left))
            ctx_ref[at, pair * PAIR:(pair + 1) * PAIR] = mixed.astype(BF16)
    for doc in range(DOCS):
        at = doc_rows(doc)
        part_ref[at, :] = dot_nn(ctx_ref[at, :], proj_ref[...]).astype(BF16)


def attend_first_kernel(
    ids_ref, spans_ref, own_ref, other_ref, qkv_w_ref, proj_ref,
    x_ref, qkv_ref, prob_ref, ctx_ref, part_ref, wide,
):
    join_halves(ids_ref[0], own_ref, other_ref, x_ref)
    attend(spans_ref, x_ref, qkv_w_ref, proj_ref, qkv_ref, prob_ref, ctx_ref, part_ref, wide)


def attend_second_kernel(
    base, ids_ref, spans_ref, first_ref, mine_ref, theirs_ref, vec_ref, own_ref, other_ref,
    qkv_w_ref, proj_ref,
    x_ref, normed_ref, inv_ref, out_ref, qkv_ref, prob_ref, ctx_ref, part_ref, wide, full,
):
    side = ids_ref[0]
    join_halves(side, own_ref, other_ref, x_ref)
    for doc in range(DOCS):
        at = doc_rows(doc)
        keep, cls = doc_masks(spans_ref, doc)
        resid = first_ref[at, :] + mine_ref[at, :].astype(F32) + theirs_ref[at, :].astype(F32)
        normed, inv = normalize(resid)
        back = normed * vec_ref[base:base + 1, :] + vec_ref[base + 1:base + 2, :]
        normed_ref[at, :] = normed.astype(BF16)
        inv_ref[at, :] = spread(inv)
        x_ref[at, :] = jnp.where(cls, back, x_ref[at, :].astype(F32)).astype(BF16)
        full[at, :] = (back * keep).astype(BF16)
    out_ref[...] = full[half_rows(side), :]
    attend(spans_ref, x_ref, qkv_w_ref, proj_ref, qkv_ref, prob_ref, ctx_ref, part_ref, wide)


def feed_kernel(
    base, x_ref, mine_ref, theirs_ref, vec_ref, in_ref, out_w_ref,
    first_ref, low_ref, normed_ref, inv_ref, act_ref, slope_ref, part_ref,
):
    for doc in range(DOCS):
        at = doc_rows(doc)
        resid = x_ref[at, :].astype(F32) + mine_ref[at, :].astype(F32) + theirs_ref[at, :].astype(F32)
        normed, inv = normalize(resid)
        first = normed * vec_ref[base:base + 1, :] + vec_ref[base + 1:base + 2, :]
        normed_ref[at, :] = normed.astype(BF16)
        inv_ref[at, :] = spread(inv)
        first_ref[at, :] = first
        low_ref[at, :] = first.astype(BF16)
    for doc in range(DOCS):
        at = doc_rows(doc)
        for piece in range(3):
            cut = slice(piece * 512, (piece + 1) * 512)
            pre = dot_nn(low_ref[at, :], in_ref[:, cut])
            share = 0.5 * (1.0 + lax.erf(pre * 0.7071067811865476))
            density = jnp.exp(-0.5 * pre * pre) * 0.3989422804014327
            act_ref[at, cut] = (pre * share).astype(BF16)
            slope_ref[at, cut] = (share + pre * density).astype(BF16)
    for doc in range(DOCS):
        at = doc_rows(doc)
        part_ref[at, :] = dot_nn(act_ref[at, :], out_w_ref[...]).astype(BF16)


def feed_back(gs_low_ref, slope_ref, in_ref, out_w_ref, grad_pre_ref, part_ref):
    for doc in range(DOCS):
        at = doc_rows(doc)
        for piece in range(3):
            cut = slice(piece * 512, (piece + 1) * 512)
            grad_act = dot_nt(gs_low_ref[at, :], out_w_ref[cut, :])
            grad_pre_ref[at, cut] = (grad_act * slope_ref[at, cut].astype(F32)).astype(BF16)
    for doc in range(DOCS):
        at = doc_rows(doc)
        part_ref[at, :] = dot_nt(grad_pre_ref[at, :], in_ref[...]).astype(BF16)


def put_norm_grads(norms_ref, sums):
    gain, shift = sums
    norms_ref[...] = jnp.zeros_like(norms_ref)
    norms_ref[0:1, :] = jnp.sum(gain, axis=0, keepdims=True)
    norms_ref[1:2, :] = jnp.sum(shift, axis=0, keepdims=True)


def add_sums(sums, grad_out, normed):
    new = (fold(grad_out * normed), fold(grad_out))
    return new if sums is None else (sums[0] + new[0], sums[1] + new[1])


def feed_back_second_kernel(
    base, ids_ref, spans_ref, first_ref, mine_ref, theirs_ref, vec_ref, own_ref, other_ref,
    slope_ref, in_ref, out_w_ref,
    head_ref, gs_ref, gs_low_ref, norms_ref, grad_pre_ref, part_ref, cot, full,
):
    side = ids_ref[0]
    join_halves(side, own_ref, other_ref, cot)
    sums = None
    for doc in range(DOCS):
        at = doc_rows(doc)
        keep, _ = doc_masks(spans_ref, doc)
        resid = first_ref[at, :] + mine_ref[at, :].astype(F32) + theirs_ref[at, :].astype(F32)
        normed, inv = normalize(resid)
        head = normed * vec_ref[base:base + 1, :] + vec_ref[base + 1:base + 2, :]
        full[at, :] = (head * keep).astype(BF16)
        grad_out = cot[at, :].astype(F32) * keep
        grad = norm_grad(grad_out, normed, inv, vec_ref[base:base + 1, :])
        gs_ref[at, :] = grad
        gs_low_ref[at, :] = grad.astype(BF16)
        sums = add_sums(sums, grad_out, normed)
    head_ref[...] = full[half_rows(side), :]
    put_norm_grads(norms_ref, sums)
    feed_back(gs_low_ref, slope_ref, in_ref, out_w_ref, grad_pre_ref, part_ref)


def feed_back_first_kernel(
    base, ids_ref, spans_ref, normed_ref, inv_ref, vec_ref, own_ref, other_ref,
    resid_ref, mine_ref, theirs_ref, slope_ref, in_ref, out_w_ref,
    skip_ref, gs_ref, gs_low_ref, norms_ref, grad_pre_ref, part_ref, cot, full,
):
    side = ids_ref[0]
    join_halves(side, own_ref, other_ref, cot)
    sums = None
    for doc in range(DOCS):
        at = doc_rows(doc)
        keep, cls = doc_masks(spans_ref, doc)
        above = resid_ref[at, :] + mine_ref[at, :].astype(F32) + theirs_ref[at, :].astype(F32)
        full[at, :] = jnp.where(cls, 0.0, above)
        normed = normed_ref[at, :].astype(F32)
        grad_out = cot[at, :].astype(F32) * keep + jnp.where(cls, above, 0.0)
        grad = norm_grad(grad_out, normed, inv_ref[at, 0:1], vec_ref[base:base + 1, :])
        gs_ref[at, :] = grad
        gs_low_ref[at, :] = grad.astype(BF16)
        sums = add_sums(sums, grad_out, normed)
    skip_ref[...] = full[half_rows(side), :]
    put_norm_grads(norms_ref, sums)
    feed_back(gs_low_ref, slope_ref, in_ref, out_w_ref, grad_pre_ref, part_ref)


def attend_back_kernel(
    base, ids_ref, gs_ref, mine_ref, theirs_ref, normed_ref, inv_ref, vec_ref, qkv_ref, prob_ref,
    qkv_w_ref, proj_ref,
    resid_ref, low_ref, norms_ref, grad_qkv_ref, part_ref, away_ref, grad_ctx, wide,
):
    for index in range(3):
        wide[:, index * 384:(index + 1) * 384] = qkv_w_ref[index]
    sums = None
    for doc in range(DOCS):
        at = doc_rows(doc)
        grad_out = gs_ref[at, :] + mine_ref[at, :].astype(F32) + theirs_ref[at, :].astype(F32)
        normed = normed_ref[at, :].astype(F32)
        grad = norm_grad(grad_out, normed, inv_ref[at, 0:1], vec_ref[base:base + 1, :])
        resid_ref[at, :] = grad
        low_ref[at, :] = grad.astype(BF16)
        sums = add_sums(sums, grad_out, normed)
    put_norm_grads(norms_ref, sums)
    for doc in range(DOCS):
        at = doc_rows(doc)
        grad_ctx[at, :] = dot_nt(low_ref[at, :], proj_ref[...]).astype(BF16)
    left = head_masks()
    for doc in range(DOCS):
        at = doc_rows(doc)
        pairs = [slice(pair * PAIR, (pair + 1) * PAIR) for pair in range(3)]
        grad_probs = []
        for pair in range(3):
            values = qkv_ref[at, 768 + pair * PAIR:768 + (pair + 1) * PAIR]
            grad_probs.append(dot_nt(grad_ctx[at, pairs[pair]], both_heads(values, left)))
        for pair in range(3):
            prob_low = prob_ref[doc, pair]
            scored = []
            for head in range(2):
                cut = slice(head * DOC, (head + 1) * DOC)
                prob = prob_low[:, cut].astype(F32)
                grad_prob = grad_probs[pair][:, cut]
                inner = jnp.sum(grad_prob * prob, axis=-1, keepdims=True)
                scored.append((prob * (grad_prob - inner)).astype(BF16))
            grad_scores = jnp.concatenate(scored, axis=1)
            query = qkv_ref[at, pairs[pair]]
            keys = qkv_ref[at, 384 + pair * PAIR:384 + (pair + 1) * PAIR]
            grad_query = dot_nn(grad_scores, both_heads(keys, left)) * SCALE
            grad_keys = dot_tn(grad_scores, query)
            grad_values = dot_tn(prob_low, grad_ctx[at, pairs[pair]])
            grad_qkv_ref[at, pair * PAIR:(pair + 1) * PAIR] = grad_query.astype(BF16)
            for index, grad in ((1, grad_keys), (2, grad_values)):
                cut = slice(index * 384 + pair * PAIR, index * 384 + (pair + 1) * PAIR)
                grad_qkv_ref[at, cut] = jnp.where(left, grad[:DOC], grad[DOC:]).astype(BF16)
    for doc in range(DOCS):
        at = doc_rows(doc)
        part_ref[at, :] = dot_nt(grad_qkv_ref[at, :], wide[...]).astype(BF16)
    if base == 0:
        away_ref[...] = part_ref[half_rows(1 - ids_ref[0]), :]
    else:
        away_ref[...] = jnp.zeros_like(away_ref)


def rows_kernel(ids_ref, resid_ref, mine_ref, theirs_ref, out_ref):
    at = half_rows(ids_ref[0])
    out_ref[...] = resid_ref[at, :] + mine_ref[at, :].astype(F32) + theirs_ref[...].astype(F32)


def cut_wide(value, blocks, piece):
    for half in range(2):
        for k in range(8):
            blocks[piece, half, k] = value[k * 48:(k + 1) * 48, half * 384:(half + 1) * 384]


def cut_tall(value, blocks, piece):
    for half in range(2):
        for k in range(8):
            at = half * 384 + k * 48
            blocks[piece, half, k] = value[at:at + 48, :]


def put_blocks(ids_ref, turn, blocks, send_ref, keep_ref):
    first, second, third, outer = [ids_ref[1 + 4 * turn + i] for i in range(4)]
    for rel, ref in ((1, send_ref), (0, keep_ref)):
        for b in range(2):
            piece = 2 * (rel ^ first) + (b ^ second)
            for e in range(2):
                for k in range(8):
                    ref[16 * b + 8 * e + k] = blocks[piece, e ^ third, k ^ outer]


def out_grad_kernel(turn, ids_ref, act_ref, gs_ref, send_ref, keep_ref, blocks):
    for p in range(2):
        value = dot_tn(act_ref[:, p * 768:(p + 1) * 768], gs_ref[...]).astype(BF16)
        cut_wide(value[:384], blocks, 2 * p)
        cut_wide(value[384:], blocks, 2 * p + 1)
    put_blocks(ids_ref, turn, blocks, send_ref, keep_ref)


def in_grad_kernel(turn, ids_ref, low_ref, grad_ref, send_ref, keep_ref, blocks):
    for p in range(2):
        value = dot_tn(low_ref[...], grad_ref[:, p * 768:(p + 1) * 768]).astype(BF16)
        cut_tall(value[:, :384], blocks, 2 * p)
        cut_tall(value[:, 384:], blocks, 2 * p + 1)
    put_blocks(ids_ref, turn, blocks, send_ref, keep_ref)


def attend_grad_kernel(turn, ids_ref, x_ref, grad_ref, ctx_ref, low_ref, *refs):
    norm_refs, (send_ref, keep_ref), blocks = refs[:-3 - (len(refs) > 3)], refs[-3:-1], refs[-1]
    if norm_refs:
        send_ref, keep_ref = refs[-4:-2]
        value = jnp.concatenate([ref[0:2, :] for ref in norm_refs], axis=0)
        refs[-2][...] = value
        send_ref[32] = norm_block(value)
    value = dot_tn(x_ref[...], grad_ref[...]).astype(BF16)
    for piece in range(3):
        cut_tall(value[:, piece * 384:(piece + 1) * 384], blocks, piece)
    cut_wide(dot_tn(ctx_ref[...], low_ref[...]).astype(BF16), blocks, 3)
    put_blocks(ids_ref, turn, blocks, send_ref, keep_ref)


def vectors_kernel(*refs):
    out_ref = refs[-1]
    for i in range(8):
        out_ref[i:i + 1, :] = refs[i][...].reshape(1, D)


def plus(one, two):
    return (one.astype(F32) + two.astype(F32)).astype(BF16)


def norm_block(value):
    high = value.astype(BF16)
    low = (value - high.astype(F32)).astype(BF16)
    rows = [high[:, :PIECE], high[:, PIECE:], low[:, :PIECE], low[:, PIECE:]]
    return jnp.concatenate(rows + [jnp.zeros((16, PIECE), BF16)], axis=0)


def block_norm(block):
    high = jnp.concatenate([block[0:8], block[8:16]], axis=1)
    low = jnp.concatenate([block[16:24], block[24:32]], axis=1)
    return high.astype(F32) + low.astype(F32)


def add_norm(value, block):
    return block_norm(norm_block(value)) + block_norm(block)


def split_kernel(sizes, with_norm, *refs):
    count = len(sizes)
    ins, outs = refs[:2 * count], refs[2 * count + with_norm:]
    at = 0
    for i, m in enumerate(sizes):
        keep, got = ins[2 * i], ins[2 * i + 1]
        outs[1][at:at + m] = plus(keep[:m], got[:m])
        outs[0][at:at + m] = plus(keep[m:], got[m:2 * m])
        at += m
    if with_norm:
        value = add_norm(refs[2 * count][...], ins[1][2 * sizes[0]])
        outs[0][at] = norm_block(value)
        outs[2][...] = value


def far_kernel(with_norm, *refs):
    if with_norm:
        keep, got, norm, out, norm_out = refs
        count = keep.shape[0] - (keep.shape[0] % 8)
        value = add_norm(norm[...], got[got.shape[0] - 1])
        out[count] = norm_block(value)
        norm_out[...] = value
    else:
        keep, got, out = refs
        count = keep.shape[0]
    out[:count] = plus(keep[:count], got[:count])


def join_kernel(count, held_ref, got_ref, *outs):
    size = outs[0].shape[0] // 2
    for i in range(count):
        at = slice(i * size, (i + 1) * size)
        outs[i][:size] = held_ref[at]
        outs[i][size:] = got_ref[at]


def place_kernel(items, ids_ref, *refs):
    ins, outs, squares, sems = refs[:len(items)], refs[-6:-2], refs[-2], refs[-1]
    slots = squares.shape[0]

    def copies(index, chunk, far, b, e):
        first, second = ids_ref[1 + 4 * chunk], ids_ref[2 + 4 * chunk]
        turn = chunk % 3
        slot = index % slots
        piece = 2 * (far ^ first) + (b ^ second)
        at = pl.ds(pl.multiple_of(piece * PIECE, PIECE), PIECE)
        cut = slice(e * PIECE, (e + 1) * PIECE)

        def copy(ref):
            return pltpu.make_async_copy(squares.at[slot], ref, sems.at[slot])

        if turn == 0:
            return [(None, copy(outs[0].at[at, cut]))]
        if turn == 1:
            return [(None, copy(outs[1].at[cut, at]))]
        return [
            (piece < 3, copy(outs[2].at[jnp.minimum(piece, 2), cut, :])),
            (piece == 3, copy(outs[3].at[:, cut])),
        ]

    def each(pairs, wait):
        for when, copy in pairs:
            def act(copy=copy):
                copy.wait() if wait else copy.start()

            if when is None:
                act()
            else:
                pl.when(when)(act)

    flight = []
    for (chunk, far), from_ref in zip(items, ins):
        third, outer = ids_ref[3 + 4 * chunk], ids_ref[4 + 4 * chunk]
        for b in range(2):
            for e in range(2):
                index = len(flight)
                if index >= slots:
                    each(flight[index - slots], True)
                for k in range(8):
                    block = from_ref[16 * b + 8 * (e ^ third) + (k ^ outer)]
                    squares[index % slots, k * 48:(k + 1) * 48, :] = block.astype(F32)
                flight.append(copies(index, chunk, far, b, e))
                each(flight[index], False)
    for pairs in flight[-slots:]:
        each(pairs, True)


def sds(*shape, dtype=BF16):
    return jax.ShapeDtypeStruct(shape, dtype)


SCALARS = pl.BlockSpec(memory_space=pltpu.SMEM)
LOCAL = pl.BlockSpec(memory_space=pltpu.VMEM)


def cost(flops, arrays, outs):
    moved = sum(a.size * a.dtype.itemsize for a in list(arrays) + list(outs))
    return pl.CostEstimate(flops=flops, bytes_accessed=moved, transcendentals=0)


LIMITS = {
    "attend_second_kernel": 8,
    "feed_back_second_kernel": 9,
    "feed_back_first_kernel": 11,
}


def run(kernel, scalars, arrays, outs, scratch, flops, *fixed):
    name = kernel.__name__
    return pl.pallas_call(
        functools.partial(kernel, *fixed),
        out_shape=list(outs),
        in_specs=[SCALARS] * len(scalars) + [LOCAL] * len(arrays),
        out_specs=[LOCAL] * len(outs),
        scratch_shapes=scratch,
        compiler_params=pltpu.CompilerParams(vmem_limit_bytes=LIMITS.get(name, 6) * 2**20),
        cost_estimate=cost(flops, arrays, outs),
        name=name,
    )(*scalars, *arrays)


STATS = sds(ROWS, 128, dtype=F32)
ATTEND_OUTS = [sds(ROWS, 1152), sds(3, 3, DOC, 2 * DOC), sds(ROWS, PIECE), sds(ROWS, D)]
WIDE = pltpu.VMEM((D, 1152), BF16)


def attend_first(ids, spans, own, other, weights):
    return run(
        attend_first_kernel, [ids, spans], [own, other, weights[0], weights[1]],
        [sds(ROWS, D)] + ATTEND_OUTS, [WIDE], 2_400_000_000,
    )


def attend_second(ids, spans, first, mine, theirs, vec, own, other, weights):
    return run(
        attend_second_kernel, [ids, spans],
        [first, mine, theirs, vec, own, other, weights[0], weights[1]],
        [sds(ROWS, D), sds(ROWS, D), STATS, sds(HALF, D)] + ATTEND_OUTS,
        [WIDE, pltpu.VMEM((ROWS, D), BF16)], 2_400_000_000, 2,
    )


def feed(base, x, mine, theirs, vec, weights):
    return run(
        feed_kernel, [], [x, mine, theirs, vec, weights[2], weights[3]],
        [sds(ROWS, D, dtype=F32), sds(ROWS, D), sds(ROWS, D), STATS,
         sds(ROWS, HIDDEN), sds(ROWS, HIDDEN), sds(ROWS, D)],
        [], 3_600_000_000, base,
    )


FEED_BACK_OUTS = [
    sds(ROWS, D, dtype=F32), sds(ROWS, D), sds(8, D, dtype=F32), sds(ROWS, HIDDEN), sds(ROWS, D),
]


def feed_back_second(ids, spans, first, mine, theirs, vec, own, other, slope, weights):
    return run(
        feed_back_second_kernel, [ids, spans],
        [first, mine, theirs, vec, own, other, slope, weights[2], weights[3]],
        [sds(HALF, D)] + FEED_BACK_OUTS,
        [pltpu.VMEM((ROWS, D), BF16), pltpu.VMEM((ROWS, D), BF16)], 3_600_000_000, 6,
    )


def feed_back_first(ids, spans, normed, inv, vec, own, other, resid, mine, theirs, slope, weights):
    return run(
        feed_back_first_kernel, [ids, spans],
        [normed, inv, vec, own, other, resid, mine, theirs, slope, weights[2], weights[3]],
        [sds(HALF, D, dtype=F32)] + FEED_BACK_OUTS,
        [pltpu.VMEM((ROWS, D), BF16), pltpu.VMEM((ROWS, D), F32)], 3_600_000_000, 2,
    )


def attend_back(base, ids, gs, mine, theirs, normed, inv, qkv, prob, vec, weights):
    return run(
        attend_back_kernel, [ids],
        [gs, mine, theirs, normed, inv, vec, qkv, prob, weights[0], weights[1]],
        [sds(ROWS, D, dtype=F32), sds(ROWS, D), sds(8, D, dtype=F32), sds(ROWS, 1152), sds(ROWS, D),
         sds(HALF if base == 0 else 16, D)],
        [pltpu.VMEM((ROWS, PIECE), BF16), WIDE], 2_800_000_000, base,
    )


SPLIT_OUTS = [sds(32, *BLOCK), sds(32, *BLOCK)]
BLOCKS = pltpu.VMEM((4, 2, 8) + BLOCK, BF16)


def out_grad(chunk, ids, act, gs_low):
    return run(out_grad_kernel, [ids], [act, gs_low], SPLIT_OUTS, [BLOCKS], 1_800_000_000, chunk)


def in_grad(chunk, ids, low, grad_pre):
    return run(in_grad_kernel, [ids], [low, grad_pre], SPLIT_OUTS, [BLOCKS], 1_800_000_000, chunk)


def attend_grad(chunk, ids, x, grad_qkv, ctx, low, norms=()):
    outs = SPLIT_OUTS
    if norms:
        outs = [sds(33, *BLOCK), sds(32, *BLOCK), sds(8, D, dtype=F32)]
    return run(
        attend_grad_kernel, [ids], [x, grad_qkv, ctx, low, *norms], outs, [BLOCKS], 1_800_000_000, chunk
    )


def vectors(rows):
    return run(vectors_kernel, [], rows, [sds(8, D, dtype=F32)], [], 1_000)[0]


def split(sources, norm=None):
    arrays = [a for pair in sources for a in pair]
    sizes = tuple(keep.shape[0] // 2 for keep, _ in sources)
    count = sum(sizes)
    outs = [sds(count + (norm is not None), *BLOCK), sds(count, *BLOCK)]
    if norm is not None:
        arrays, outs = arrays + [norm], outs + [sds(8, D, dtype=F32)]
    return run(split_kernel, [], arrays, outs, [], 1_000_000, sizes, int(norm is not None))


def far_add(keep, got, norm=None):
    if norm is None:
        return run(far_kernel, [], [keep, got], [sds(*keep.shape)], [], 1_000_000, 0)
    count = keep.shape[0] - keep.shape[0] % 8
    outs = [sds(count + 1, *BLOCK), sds(8, D, dtype=F32)]
    return run(far_kernel, [], [keep, got, norm], outs, [], 1_000_000, 1)


def join(held, got, count=1):
    size = held.shape[0] // count
    return run(join_kernel, [], [held, got], [sds(2 * size, *BLOCK)] * count, [], 1_000_000, count)


PLACED = [
    sds(HIDDEN, D, dtype=F32),
    sds(D, HIDDEN, dtype=F32),
    sds(3, D, PIECE, dtype=F32),
    sds(PIECE, D, dtype=F32),
]
REMOTE = pl.BlockSpec(memory_space=pl.ANY)


def place(ids, items, values, into=()):
    return pl.pallas_call(
        functools.partial(place_kernel, tuple(items)),
        out_shape=PLACED,
        in_specs=[SCALARS] + [LOCAL] * len(values) + [REMOTE] * len(into),
        out_specs=[REMOTE] * 4,
        scratch_shapes=[pltpu.VMEM((6, PIECE, PIECE), F32), pltpu.SemaphoreType.DMA((6,))],
        input_output_aliases={1 + len(values) + i: i for i in range(len(into))},
        compiler_params=pltpu.CompilerParams(vmem_limit_bytes=6 * 2**20),
        cost_estimate=pl.CostEstimate(
            flops=1_000, bytes_accessed=3_600_000 * len(values), transcendentals=0
        ),
        name="place_kernel",
    )(ids, *values, *into)


def swap(value):
    return lax.ppermute(value, "tensor", SWAP)


def flip(chip, core, stage, axis):
    pos = [chip % 4, chip // 4 % 4, chip // 16]
    low = (core == 0) == (stage == 0)
    pos[axis] = pos[axis] ^ 1 if low else 3 - pos[axis]
    return pos[0] + 4 * pos[1] + 16 * pos[2]


def exchange(value, stage, axis):
    pairs = [
        (2 * chip + core, 2 * flip(chip, core, stage, axis) + core)
        for chip in range(64)
        for core in range(2)
    ]
    return lax.ppermute(value, ("dp", "tensor"), pairs)


class Order:
    def __init__(self):
        self.token = None

    def hold(self, value):
        if self.token is None:
            return value
        return lax.optimization_barrier((value, self.token))[0]


class Single:
    def __init__(self, order, turn, send, keep, norm=None):
        self.order, self.turn, self.keep, self.norm, self.round = order, turn, keep, norm, 0
        self.send(send, 0, 0)

    def send(self, value, stage, j):
        self.order.token = value
        self.got = exchange(value, stage, (self.turn + j) % 3)

    def next(self):
        got = self.order.hold(self.got)
        self.round += 1
        if self.round < 3:
            value, self.keep, *norm = split([(self.keep, got)], self.norm)
            self.send(value, 0, self.round)
        elif self.round < 6:
            self.keep, *norm = far_add(self.keep, got, self.norm)
            self.send(self.keep, 1, self.round)
        elif self.round == 6:
            self.keep, *norm = far_add(self.keep, got, self.norm)
            if norm:
                self.keep = self.keep[:8]
            self.send(self.keep, 0, 2)
        else:
            norm = ()
            self.keep = join(self.keep, got)[0]
            self.send(self.keep, 0, 8 - self.round)
        if norm:
            self.norm = norm[0]


class Pair:
    def __init__(self, order, axes):
        self.order, self.axes = order, axes
        self.keep, self.got, self.round = [None, None], [None, None], [0, 0]
        self.both = 2

    def axis(self, i, j):
        return self.axes[j if j == 2 else i ^ j]

    def start(self, i, send, keep):
        self.keep[i] = keep
        self.send(i, send, 0)

    def send(self, i, value, j):
        self.order.token = value
        self.got[i] = exchange(value, 0, self.axis(i, j))

    def next(self, i):
        got = self.order.hold(self.got[i])
        self.round[i] += 1
        if self.round[i] == 1:
            value, self.keep[i] = split([(self.keep[i], got)])
            self.send(i, value, 1)
        else:
            self.keep[i] = join(self.keep[i], got)[0]
            self.send(i, self.keep[i], 0)

    def merge(self):
        got = [self.order.hold(g) for g in self.got]
        value, self.held = split([(self.keep[0], got[0]), (self.keep[1], got[1])])
        self.order.token = value
        self.arrived = exchange(value, 0, self.axes[2])

    def next_both(self):
        got = self.order.hold(self.arrived)
        self.both += 1
        if self.both <= 6:
            self.held = far_add(self.held, got)[0]
            self.order.token = self.held
            if self.both < 6:
                self.arrived = exchange(self.held, 1, self.axes[self.both - 3])
            else:
                self.arrived = exchange(self.held, 0, self.axes[2])
        else:
            self.keep = list(join(self.held, got, 2))
            for i in range(2):
                self.send(i, self.keep[i], 1)


UPPER_PAIR = (1, 2, 0)
LOWER_PAIR = (0, 1, 2)
CHUNK_AXES = [
    (UPPER_PAIR[0], UPPER_PAIR[1], UPPER_PAIR[2]),
    (UPPER_PAIR[1], UPPER_PAIR[0], UPPER_PAIR[2]),
    (0, 1, 2),
    (LOWER_PAIR[0], LOWER_PAIR[1], LOWER_PAIR[2]),
    (LOWER_PAIR[1], LOWER_PAIR[0], LOWER_PAIR[2]),
    (2, 0, 1),
]


def device_table():
    rows = []
    for chip in range(64):
        pos = [chip % 4, chip // 4 % 4, chip // 16]
        low = [(p ^ (p >> 1)) & 1 for p in pos]
        high = [p >> 1 for p in pos]
        for core in range(2):
            near = low if core == 0 else high
            row = [core]
            for axes in CHUNK_AXES:
                row += [near[axis] for axis in axes] + [0]
            rows.append(row + [0] * 7)
    return np.array(rows, np.int32)


def on_device(
    tokens,
    skip_tokens,
    cot_back,
    cot_head,
    one_span,
    *params,
):
    lower = [params[i] for i in (0, 1, 4, 5)]
    upper = [params[i] for i in (8, 9, 12, 13)]
    device = lax.axis_index("dp") * 2 + lax.axis_index("tensor")
    ids = lax.dynamic_index_in_dim(jnp.asarray(device_table()), device, 0, keepdims=False)
    spans = one_span
    tokens_other = swap(tokens)
    tokens, ids = lax.optimization_barrier((tokens, ids))
    vec = vectors([params[i] for i in (2, 3, 6, 7, 10, 11, 14, 15)])
    skip_other = swap(skip_tokens)
    cot_head_other = swap(cot_head)
    cot_back_other = swap(cot_back)
    order = Order()

    x_l, qkv_l, prob_l, ctx_l, part = attend_first(ids, spans, tokens, tokens_other, lower)
    first_l, low_l, normed_al, inv_al, act_l, slope_l, part = feed(
        0, x_l, part, swap(part), vec, lower
    )
    x_u, normed_fl, inv_fl, back_out, qkv_u, prob_u, ctx_u, part = attend_second(
        ids, spans, first_l, part, swap(part), vec, skip_tokens, skip_other, upper
    )
    first_u, low_u, normed_au, inv_au, act_u, slope_u, part = feed(
        4, x_u, part, swap(part), vec, upper
    )
    head_out, gs_u, gs_low_u, norms_fu, grad_pre_u, part = feed_back_second(
        ids, spans, first_u, part, swap(part), vec, cot_head, cot_head_other, slope_u, upper
    )
    pair_u, pair_l = Pair(order, UPPER_PAIR), Pair(order, LOWER_PAIR)
    theirs = swap(part)
    pair_u.start(0, *out_grad(0, ids, act_u, gs_low_u))
    pair_u.start(1, *in_grad(1, ids, low_u, order.hold(grad_pre_u)))
    resid_u, gr_low_u, norms_au, grad_qkv_u, part, _ = attend_back(
        4, ids, order.hold(gs_u), part, theirs, normed_au, inv_au, qkv_u, prob_u, vec=vec,
        weights=upper,
    )
    theirs = swap(part)
    at_u = Single(order, 0, *attend_grad(2, ids, x_u, grad_qkv_u, ctx_u, gr_low_u))
    pair_u.next(0)
    pair_u.next(1)
    grad_skip, gs_l, gs_low_l, norms_fl, grad_pre_l, part = feed_back_first(
        ids, spans, normed_fl, inv_fl, vec, cot_back, cot_back_other, order.hold(resid_u), part,
        theirs, slope_l, lower,
    )
    theirs = swap(part)
    order.token = gs_low_l
    pair_u.merge()
    pair_l.start(0, *out_grad(3, ids, act_l, order.hold(gs_low_l)))
    pair_l.start(1, *in_grad(4, ids, low_l, order.hold(grad_pre_l)))
    at_u.next()
    pair_u.next_both()
    resid_l, gr_low_l, norms_al, grad_qkv_l, part, away = attend_back(
        0, ids, order.hold(gs_l), part, theirs, normed_al, inv_al, qkv_l, prob_l, vec=vec,
        weights=lower,
    )
    away = swap(away)
    at_l = Single(
        order, 2,
        *attend_grad(
            5, ids, x_l, grad_qkv_l, ctx_l, gr_low_l, (norms_al, norms_fl, norms_au, norms_fu)
        ),
    )
    pair_l.next(0)
    pair_l.next(1)
    at_u.next()
    grad_tokens = run(
        rows_kernel, [ids], [order.hold(resid_l), part, away], [sds(HALF, D, dtype=F32)], [],
        1_000_000,
    )[0]
    pair_u.next_both()
    at_u.next()
    pair_l.merge()
    at_l.next()
    at_u.next()
    pair_u.next_both()
    at_u.next()
    at_l.next()
    pair_l.next_both()
    at_u.next()
    at_l.next()
    pair_u.next_both()
    at_u.next()
    pair_l.next_both()
    at_l.next()
    pair_u.next_both()
    at_l.next()
    at_u.next()
    pair_l.next_both()
    pair_u.next(0)
    pair_u.next(1)
    at_l.next()
    pair_l.next_both()
    done_u = place(
        ids,
        [(0, 0), (0, 1), (1, 0), (1, 1), (2, 0), (2, 1)],
        [pair_u.keep[0], pair_u.got[0], pair_u.keep[1], pair_u.got[1], at_u.keep,
         order.hold(at_u.got)],
    )
    order.token = done_u[0]
    at_l.next()
    pair_l.next_both()
    at_l.next()
    pair_l.next(0)
    pair_l.next(1)
    done_l = place(
        ids, [(3, 0), (4, 0), (5, 0)],
        [pair_l.keep[0], pair_l.keep[1], order.hold(at_l.keep)],
    )
    done_l = place(
        ids, [(5, 1), (3, 1), (4, 1)], [at_l.got, pair_l.got[0], pair_l.got[1]], done_l
    )
    norms = at_l.norm
    out_gu, in_gu, qkv_gu, proj_gu = done_u
    out_gl, in_gl, qkv_gl, proj_gl = done_l
    return (
        back_out,
        head_out,
        grad_tokens,
        grad_skip,
        qkv_gl,
        proj_gl,
        norms[0],
        norms[1],
        in_gl,
        out_gl,
        norms[2],
        norms[3],
        qkv_gu,
        proj_gu,
        norms[4],
        norms[5],
        in_gu,
        out_gu,
        norms[6],
        norms[7],
    )


def solution(mesh):
    rows = P(("dp", "tensor"), None)
    weights = (
        P(None, None, "tensor"),
        P("tensor", None),
        P(),
        P(),
        P(None, "tensor"),
        P("tensor", None),
        P(),
        P(),
    )
    return jax.shard_map(
        on_device,
        mesh=mesh,
        in_specs=(rows,) * 4 + (P("dp"),) + weights + weights,
        out_specs=(rows,) * 4 + weights + weights,
        check_vma=False,
    )
```

```python
import functools

import jax
import jax.numpy as jnp
import numpy as np
from jax import lax
from jax.experimental import pallas as pl
from jax.experimental.pallas import tpu as pltpu
from jax.sharding import PartitionSpec as P

SPAN = 128
EPS = 1e-06
SCALE = 0.125
NEG = -1000000000.0

D = 768
ROWS = 768
HALF = ROWS // 2
HIDDEN = 1536
PIECE = 384
PAIR = 128
BLOCK = (48, 384)
F32 = jnp.float32
BF16 = jnp.bfloat16
SPANS_AT = 32

SWAP = [(0, 1), (1, 0)]


def dot_nn(left, right):
    return lax.dot_general(left, right, (((1,), (0,)), ((), ())), preferred_element_type=F32)


def dot_nt(left, right):
    return lax.dot_general(left, right, (((1,), (1,)), ((), ())), preferred_element_type=F32)


def dot_tn(left, right):
    return lax.dot_general(left, right, (((0,), (0,)), ((), ())), preferred_element_type=F32)


def normalize(resid):
    mean = jnp.mean(resid, axis=-1, keepdims=True)
    centered = resid - mean
    var = jnp.mean(centered * centered, axis=-1, keepdims=True)
    inv = lax.rsqrt(var + EPS)
    return centered * inv, inv


def norm_grad(grad_out, normed, inv, gain):
    grad = grad_out * gain
    first = jnp.mean(grad, axis=-1, keepdims=True)
    second = jnp.mean(grad * normed, axis=-1, keepdims=True)
    return inv * (grad - first - normed * second)


def fold(value):
    return jnp.sum(value.reshape(-1, 8, value.shape[-1]), axis=0)

DOC = 2 * SPAN
DOCS = ROWS // DOC


def doc_rows(doc):
    return slice(doc * DOC, (doc + 1) * DOC)


def half_rows(index):
    return pl.ds(pl.multiple_of(index * HALF, HALF), HALF)


def join_halves(side, own_ref, other_ref, full_ref):
    full_ref[half_rows(side), :] = own_ref[...]
    full_ref[half_rows(1 - side), :] = other_ref[...]


def doc_masks(ids_ref, doc):
    row = lax.broadcasted_iota(jnp.int32, (DOC, 1), 0)
    keep = jnp.where((row < SPAN) | (ids_ref[SPANS_AT + doc] == 0), 1.0, 0.0)
    return keep, (row & (SPAN - 1)) == 0


def spread(column):
    return jnp.broadcast_to(column, (column.shape[0], 128))


def head_masks():
    lane = lax.broadcasted_iota(jnp.int32, (1, PAIR), 1)
    return lane < 64


def both_heads(value, left):
    zero = jnp.zeros_like(value)
    return jnp.concatenate([jnp.where(left, value, zero), jnp.where(left, zero, value)], axis=0)


def attend(ids_ref, x_ref, proj_ref, qkv_ref, prob_ref, ctx_ref, part_ref, wide):
    for doc in range(DOCS):
        at = doc_rows(doc)
        out = dot_nn(x_ref[at, :], wide[...])
        qkv_ref[at, :384] = (out[:, :384] * SCALE).astype(BF16)
        qkv_ref[at, 384:] = out[:, 384:].astype(BF16)
    left = head_masks()
    col = lax.broadcasted_iota(jnp.int32, (1, 2 * DOC), 1) & (DOC - 1)
    for doc in range(DOCS):
        at = doc_rows(doc)
        key_ok = (col < SPAN) | (ids_ref[SPANS_AT + doc] == 0)
        scores = []
        for pair in range(3):
            query = qkv_ref[at, pair * PAIR:(pair + 1) * PAIR]
            keys = qkv_ref[at, 384 + pair * PAIR:384 + (pair + 1) * PAIR]
            scores.append(jnp.where(key_ok, dot_nt(query, both_heads(keys, left)), NEG))
        for pair in range(3):
            probs = []
            for head in range(2):
                score = scores[pair][:, head * DOC:(head + 1) * DOC]
                raised = jnp.exp(score - jnp.max(score, axis=-1, keepdims=True))
                probs.append(
                    (raised * (1.0 / jnp.sum(raised, axis=-1, keepdims=True))).astype(BF16)
                )
            prob = jnp.concatenate(probs, axis=1)
            prob_ref[doc, pair] = prob
            values = qkv_ref[at, 768 + pair * PAIR:768 + (pair + 1) * PAIR]
            mixed = dot_nn(prob, both_heads(values, left))
            ctx_ref[at, pair * PAIR:(pair + 1) * PAIR] = mixed.astype(BF16)
    for doc in range(DOCS):
        at = doc_rows(doc)
        part_ref[at, :] = dot_nn(ctx_ref[at, :], proj_ref[...]).astype(BF16)


def attend_first_kernel(
    ids_ref, other_ref, own_ref, qkv_w_ref, proj_w_ref,
    x_ref, qkv_ref, prob_ref, ctx_ref, part_ref, wide, proj, sems,
):
    side = ids_ref[0]
    copies = [pltpu.make_async_copy(own_ref, x_ref.at[half_rows(side), :], sems.at[0])]
    for index in range(3):
        cut = slice(index * 384, (index + 1) * 384)
        copies.append(
            pltpu.make_async_copy(qkv_w_ref.at[index], wide.at[:, cut], sems.at[1 + index])
        )
    copies.append(pltpu.make_async_copy(proj_w_ref, proj, sems.at[4]))
    for copy in copies:
        copy.start()
    x_ref[half_rows(1 - side), :] = other_ref[...]
    for copy in copies:
        copy.wait()
    attend(ids_ref, x_ref, proj, qkv_ref, prob_ref, ctx_ref, part_ref, wide)


def attend_second_kernel(
    base, ids_ref, first_ref, mine_ref, theirs_ref, vec_ref, own_ref, other_ref,
    qkv_w_ref, proj_ref,
    x_ref, normed_ref, inv_ref, out_ref, qkv_ref, prob_ref, ctx_ref, part_ref, wide, full,
):
    side = ids_ref[0]
    join_halves(side, own_ref, other_ref, x_ref)
    for doc in range(DOCS):
        at = doc_rows(doc)
        keep, cls = doc_masks(ids_ref, doc)
        resid = first_ref[at, :] + mine_ref[at, :].astype(F32) + theirs_ref[at, :].astype(F32)
        normed, inv = normalize(resid)
        back = normed * vec_ref[base:base + 1, :] + vec_ref[base + 1:base + 2, :]
        normed_ref[at, :] = normed.astype(BF16)
        inv_ref[at, :] = spread(inv)
        x_ref[at, :] = jnp.where(cls, back, x_ref[at, :].astype(F32)).astype(BF16)
        full[at, :] = (back * keep).astype(BF16)
    out_ref[...] = full[half_rows(side), :]
    for index in range(3):
        wide[:, index * 384:(index + 1) * 384] = qkv_w_ref[index]
    attend(ids_ref, x_ref, proj_ref, qkv_ref, prob_ref, ctx_ref, part_ref, wide)


def feed_kernel(
    base, x_ref, mine_ref, theirs_ref, vec_ref, in_ref, out_w_ref,
    first_ref, low_ref, normed_ref, inv_ref, act_ref, slope_ref, part_ref,
):
    for doc in range(DOCS):
        at = doc_rows(doc)
        resid = x_ref[at, :].astype(F32) + mine_ref[at, :].astype(F32) + theirs_ref[at, :].astype(F32)
        normed, inv = normalize(resid)
        first = normed * vec_ref[base:base + 1, :] + vec_ref[base + 1:base + 2, :]
        normed_ref[at, :] = normed.astype(BF16)
        inv_ref[at, :] = spread(inv)
        first_ref[at, :] = first
        low_ref[at, :] = first.astype(BF16)
    for doc in range(DOCS):
        at = doc_rows(doc)
        for piece in range(3):
            cut = slice(piece * 512, (piece + 1) * 512)
            pre = dot_nn(low_ref[at, :], in_ref[:, cut])
            share = 0.5 * (1.0 + lax.erf(pre * 0.7071067811865476))
            density = jnp.exp(-0.5 * pre * pre) * 0.3989422804014327
            act_ref[at, cut] = (pre * share).astype(BF16)
            slope_ref[at, cut] = (share + pre * density).astype(BF16)
    for doc in range(DOCS):
        at = doc_rows(doc)
        part_ref[at, :] = dot_nn(act_ref[at, :], out_w_ref[...]).astype(BF16)


def feed_back(gs_low_ref, slope_ref, in_ref, out_w_ref, grad_pre_ref, part_ref):
    for doc in range(DOCS):
        at = doc_rows(doc)
        for piece in range(3):
            cut = slice(piece * 512, (piece + 1) * 512)
            grad_act = dot_nt(gs_low_ref[at, :], out_w_ref[cut, :])
            grad_pre_ref[at, cut] = (grad_act * slope_ref[at, cut].astype(F32)).astype(BF16)
    for doc in range(DOCS):
        at = doc_rows(doc)
        part_ref[at, :] = dot_nt(grad_pre_ref[at, :], in_ref[...]).astype(BF16)


def put_norm_grads(norms_ref, sums):
    gain, shift = sums
    norms_ref[...] = jnp.zeros_like(norms_ref)
    norms_ref[0:1, :] = jnp.sum(gain, axis=0, keepdims=True)
    norms_ref[1:2, :] = jnp.sum(shift, axis=0, keepdims=True)


def add_sums(sums, grad_out, normed):
    new = (fold(grad_out * normed), fold(grad_out))
    return new if sums is None else (sums[0] + new[0], sums[1] + new[1])


def feed_back_second_kernel(
    base, ids_ref, first_ref, mine_ref, theirs_ref, vec_ref, own_ref, other_ref,
    slope_ref, in_ref, out_w_ref,
    head_ref, gs_ref, gs_low_ref, norms_ref, grad_pre_ref, part_ref, cot, full,
):
    side = ids_ref[0]
    join_halves(side, own_ref, other_ref, cot)
    sums = None
    for doc in range(DOCS):
        at = doc_rows(doc)
        keep, _ = doc_masks(ids_ref, doc)
        resid = first_ref[at, :] + mine_ref[at, :].astype(F32) + theirs_ref[at, :].astype(F32)
        normed, inv = normalize(resid)
        head = normed * vec_ref[base:base + 1, :] + vec_ref[base + 1:base + 2, :]
        full[at, :] = (head * keep).astype(BF16)
        grad_out = cot[at, :].astype(F32) * keep
        grad = norm_grad(grad_out, normed, inv, vec_ref[base:base + 1, :])
        gs_ref[at, :] = grad
        gs_low_ref[at, :] = grad.astype(BF16)
        sums = add_sums(sums, grad_out, normed)
    head_ref[...] = full[half_rows(side), :]
    put_norm_grads(norms_ref, sums)
    feed_back(gs_low_ref, slope_ref, in_ref, out_w_ref, grad_pre_ref, part_ref)


def feed_back_first_kernel(
    base, ids_ref, normed_ref, inv_ref, vec_ref, own_ref, other_ref,
    resid_ref, mine_ref, theirs_ref, slope_ref, in_ref, out_w_ref,
    skip_ref, gs_ref, gs_low_ref, norms_ref, grad_pre_ref, part_ref, cot, full,
):
    side = ids_ref[0]
    join_halves(side, own_ref, other_ref, cot)
    sums = None
    for doc in range(DOCS):
        at = doc_rows(doc)
        keep, cls = doc_masks(ids_ref, doc)
        above = resid_ref[at, :] + mine_ref[at, :].astype(F32) + theirs_ref[at, :].astype(F32)
        full[at, :] = jnp.where(cls, 0.0, above)
        normed = normed_ref[at, :].astype(F32)
        grad_out = cot[at, :].astype(F32) * keep + jnp.where(cls, above, 0.0)
        grad = norm_grad(grad_out, normed, inv_ref[at, 0:1], vec_ref[base:base + 1, :])
        gs_ref[at, :] = grad
        gs_low_ref[at, :] = grad.astype(BF16)
        sums = add_sums(sums, grad_out, normed)
    skip_ref[...] = full[half_rows(side), :]
    put_norm_grads(norms_ref, sums)
    feed_back(gs_low_ref, slope_ref, in_ref, out_w_ref, grad_pre_ref, part_ref)


def attend_back_kernel(
    base, ids_ref, gs_ref, mine_ref, theirs_ref, normed_ref, inv_ref, vec_ref, qkv_ref, prob_ref,
    qkv_w_ref, proj_ref,
    resid_ref, low_ref, norms_ref, grad_qkv_ref, part_ref, away_ref, grad_ctx, wide,
):
    for index in range(3):
        wide[:, index * 384:(index + 1) * 384] = qkv_w_ref[index]
    sums = None
    for doc in range(DOCS):
        at = doc_rows(doc)
        grad_out = gs_ref[at, :] + mine_ref[at, :].astype(F32) + theirs_ref[at, :].astype(F32)
        normed = normed_ref[at, :].astype(F32)
        grad = norm_grad(grad_out, normed, inv_ref[at, 0:1], vec_ref[base:base + 1, :])
        resid_ref[at, :] = grad
        low_ref[at, :] = grad.astype(BF16)
        sums = add_sums(sums, grad_out, normed)
    put_norm_grads(norms_ref, sums)
    for doc in range(DOCS):
        at = doc_rows(doc)
        grad_ctx[at, :] = dot_nt(low_ref[at, :], proj_ref[...]).astype(BF16)
    left = head_masks()
    for doc in range(DOCS):
        at = doc_rows(doc)
        pairs = [slice(pair * PAIR, (pair + 1) * PAIR) for pair in range(3)]
        grad_probs = []
        for pair in range(3):
            values = qkv_ref[at, 768 + pair * PAIR:768 + (pair + 1) * PAIR]
            grad_probs.append(dot_nt(grad_ctx[at, pairs[pair]], both_heads(values, left)))
        for pair in range(3):
            prob_low = prob_ref[doc, pair]
            scored = []
            for head in range(2):
                cut = slice(head * DOC, (head + 1) * DOC)
                prob = prob_low[:, cut].astype(F32)
                grad_prob = grad_probs[pair][:, cut]
                inner = jnp.sum(grad_prob * prob, axis=-1, keepdims=True)
                scored.append((prob * (grad_prob - inner)).astype(BF16))
            grad_scores = jnp.concatenate(scored, axis=1)
            query = qkv_ref[at, pairs[pair]]
            keys = qkv_ref[at, 384 + pair * PAIR:384 + (pair + 1) * PAIR]
            grad_query = dot_nn(grad_scores, both_heads(keys, left)) * SCALE
            grad_keys = dot_tn(grad_scores, query)
            grad_values = dot_tn(prob_low, grad_ctx[at, pairs[pair]])
            grad_qkv_ref[at, pair * PAIR:(pair + 1) * PAIR] = grad_query.astype(BF16)
            for index, grad in ((1, grad_keys), (2, grad_values)):
                cut = slice(index * 384 + pair * PAIR, index * 384 + (pair + 1) * PAIR)
                grad_qkv_ref[at, cut] = jnp.where(left, grad[:DOC], grad[DOC:]).astype(BF16)
    for doc in range(DOCS):
        at = doc_rows(doc)
        part_ref[at, :] = dot_nt(grad_qkv_ref[at, :], wide[...]).astype(BF16)
    if base == 0:
        away_ref[...] = part_ref[half_rows(1 - ids_ref[0]), :]
    else:
        away_ref[...] = jnp.zeros_like(away_ref)


def rows_kernel(ids_ref, resid_ref, mine_ref, theirs_ref, out_ref):
    at = half_rows(ids_ref[0])
    out_ref[...] = resid_ref[at, :] + mine_ref[at, :].astype(F32) + theirs_ref[...].astype(F32)


def cut_wide(value, blocks, piece):
    for half in range(2):
        for k in range(8):
            blocks[piece, half, k] = value[k * 48:(k + 1) * 48, half * 384:(half + 1) * 384]


def cut_tall(value, blocks, piece):
    for half in range(2):
        for k in range(8):
            at = half * 384 + k * 48
            blocks[piece, half, k] = value[at:at + 48, :]


def put_blocks(ids_ref, turn, blocks, send_ref, keep_ref):
    first, second, third, outer = [ids_ref[1 + 4 * turn + i] for i in range(4)]
    for rel, ref in ((1, send_ref), (0, keep_ref)):
        for b in range(2):
            piece = 2 * (rel ^ first) + (b ^ second)
            for e in range(2):
                for k in range(8):
                    ref[16 * b + 8 * e + k] = blocks[piece, e ^ third, k ^ outer]


def out_grad_kernel(turn, ids_ref, act_ref, gs_ref, send_ref, keep_ref, blocks):
    for p in range(2):
        value = dot_tn(act_ref[:, p * 768:(p + 1) * 768], gs_ref[...]).astype(BF16)
        cut_wide(value[:384], blocks, 2 * p)
        cut_wide(value[384:], blocks, 2 * p + 1)
    put_blocks(ids_ref, turn, blocks, send_ref, keep_ref)


def in_grad_kernel(turn, ids_ref, low_ref, grad_ref, send_ref, keep_ref, blocks):
    for p in range(2):
        value = dot_tn(low_ref[...], grad_ref[:, p * 768:(p + 1) * 768]).astype(BF16)
        cut_tall(value[:, :384], blocks, 2 * p)
        cut_tall(value[:, 384:], blocks, 2 * p + 1)
    put_blocks(ids_ref, turn, blocks, send_ref, keep_ref)


def attend_grad_kernel(turn, ids_ref, x_ref, grad_ref, ctx_ref, low_ref, *refs):
    norm_refs, (send_ref, keep_ref), blocks = refs[:-3 - (len(refs) > 3)], refs[-3:-1], refs[-1]
    if norm_refs:
        send_ref, keep_ref = refs[-4:-2]
        value = jnp.concatenate([ref[0:2, :] for ref in norm_refs], axis=0)
        refs[-2][...] = value
        send_ref[32] = norm_block(value)
    value = dot_tn(x_ref[...], grad_ref[...]).astype(BF16)
    for piece in range(3):
        cut_tall(value[:, piece * 384:(piece + 1) * 384], blocks, piece)
    cut_wide(dot_tn(ctx_ref[...], low_ref[...]).astype(BF16), blocks, 3)
    put_blocks(ids_ref, turn, blocks, send_ref, keep_ref)


def vectors_kernel(*refs):
    out_ref = refs[-1]
    for i in range(8):
        out_ref[i:i + 1, :] = refs[i][...].reshape(1, D)


def plus(one, two):
    return (one.astype(F32) + two.astype(F32)).astype(BF16)


def norm_block(value):
    high = value.astype(BF16)
    low = (value - high.astype(F32)).astype(BF16)
    rows = [high[:, :PIECE], high[:, PIECE:], low[:, :PIECE], low[:, PIECE:]]
    return jnp.concatenate(rows + [jnp.zeros((16, PIECE), BF16)], axis=0)


def block_norm(block):
    high = jnp.concatenate([block[0:8], block[8:16]], axis=1)
    low = jnp.concatenate([block[16:24], block[24:32]], axis=1)
    return high.astype(F32) + low.astype(F32)


def add_norm(value, block):
    return block_norm(norm_block(value)) + block_norm(block)


def split_kernel(sizes, with_norm, *refs):
    count = len(sizes)
    ins, outs = refs[:2 * count], refs[2 * count + with_norm:]
    at = 0
    for i, m in enumerate(sizes):
        keep, got = ins[2 * i], ins[2 * i + 1]
        outs[1][at:at + m] = plus(keep[:m], got[:m])
        outs[0][at:at + m] = plus(keep[m:], got[m:2 * m])
        at += m
    if with_norm:
        value = add_norm(refs[2 * count][...], ins[1][2 * sizes[0]])
        outs[0][at] = norm_block(value)
        outs[2][...] = value


def far_kernel(with_norm, *refs):
    if with_norm:
        keep, got, norm, out, norm_out = refs
        count = keep.shape[0] - (keep.shape[0] % 8)
        value = add_norm(norm[...], got[got.shape[0] - 1])
        out[count] = norm_block(value)
        norm_out[...] = value
    else:
        keep, got, out = refs
        count = keep.shape[0]
    out[:count] = plus(keep[:count], got[:count])


def join_kernel(count, held_ref, got_ref, *outs):
    size = outs[0].shape[0] // 2
    for i in range(count):
        at = slice(i * size, (i + 1) * size)
        outs[i][:size] = held_ref[at]
        outs[i][size:] = got_ref[at]


def place_kernel(items, ids_ref, *refs):
    ins, outs, squares, sems = refs[:len(items)], refs[-6:-2], refs[-2], refs[-1]
    slots = squares.shape[0]

    def copies(index, chunk, far, b, e):
        first, second = ids_ref[1 + 4 * chunk], ids_ref[2 + 4 * chunk]
        turn = chunk % 3
        slot = index % slots
        piece = 2 * (far ^ first) + (b ^ second)
        at = pl.ds(pl.multiple_of(piece * PIECE, PIECE), PIECE)
        cut = slice(e * PIECE, (e + 1) * PIECE)

        def copy(ref):
            return pltpu.make_async_copy(squares.at[slot], ref, sems.at[slot])

        if turn == 0:
            return [(None, copy(outs[0].at[at, cut]))]
        if turn == 1:
            return [(None, copy(outs[1].at[cut, at]))]
        return [
            (piece < 3, copy(outs[2].at[jnp.minimum(piece, 2), cut, :])),
            (piece == 3, copy(outs[3].at[:, cut])),
        ]

    def each(pairs, wait):
        for when, copy in pairs:
            def act(copy=copy):
                copy.wait() if wait else copy.start()

            if when is None:
                act()
            else:
                pl.when(when)(act)

    flight = []
    for (chunk, far), from_ref in zip(items, ins):
        third, outer = ids_ref[3 + 4 * chunk], ids_ref[4 + 4 * chunk]
        for b in range(2):
            for e in range(2):
                index = len(flight)
                if index >= slots:
                    each(flight[index - slots], True)
                for k in range(8):
                    block = from_ref[16 * b + 8 * (e ^ third) + (k ^ outer)]
                    squares[index % slots, k * 48:(k + 1) * 48, :] = block.astype(F32)
                flight.append(copies(index, chunk, far, b, e))
                each(flight[index], False)
    for pairs in flight[-slots:]:
        each(pairs, True)


def sds(*shape, dtype=BF16):
    return jax.ShapeDtypeStruct(shape, dtype)


SCALARS = pl.BlockSpec(memory_space=pltpu.SMEM)
LOCAL = pl.BlockSpec(memory_space=pltpu.VMEM)
REMOTE = pl.BlockSpec(memory_space=pl.ANY)


COST = pl.CostEstimate(flops=1, bytes_accessed=1, transcendentals=0)


LIMITS = {
    "attend_second_kernel": 8,
    "feed_back_second_kernel": 9,
    "feed_back_first_kernel": 11,
}


def run(kernel, scalars, arrays, outs, scratch, *fixed):
    name = kernel.__name__
    return pl.pallas_call(
        functools.partial(kernel, *fixed),
        out_shape=list(outs),
        in_specs=[SCALARS] * len(scalars) + [LOCAL] * len(arrays),
        out_specs=[LOCAL] * len(outs),
        scratch_shapes=scratch,
        compiler_params=pltpu.CompilerParams(vmem_limit_bytes=LIMITS.get(name, 6) * 2**20),
        cost_estimate=COST,
        name=name,
    )(*scalars, *arrays)


STATS = sds(ROWS, 128, dtype=F32)
ATTEND_OUTS = [sds(ROWS, 1152), sds(3, 3, DOC, 2 * DOC), sds(ROWS, PIECE), sds(ROWS, D)]
WIDE = pltpu.VMEM((D, 1152), BF16)


def attend_first(ids, own, other, weights):
    outs = [sds(ROWS, D)] + ATTEND_OUTS
    arrays = [other, own, weights[0], weights[1]]
    return pl.pallas_call(
        attend_first_kernel,
        out_shape=outs,
        in_specs=[SCALARS, LOCAL] + [REMOTE] * 3,
        out_specs=[LOCAL] * len(outs),
        scratch_shapes=[WIDE, pltpu.VMEM((PIECE, D), BF16), pltpu.SemaphoreType.DMA((5,))],
        compiler_params=pltpu.CompilerParams(vmem_limit_bytes=7 * 2**20),
        cost_estimate=COST,
        name="attend_first_kernel",
    )(ids, *arrays)


def attend_second(ids, first, mine, theirs, vec, own, other, weights):
    return run(
        attend_second_kernel, [ids],
        [first, mine, theirs, vec, own, other, weights[0], weights[1]],
        [sds(ROWS, D), sds(ROWS, D), STATS, sds(HALF, D)] + ATTEND_OUTS,
        [WIDE, pltpu.VMEM((ROWS, D), BF16)], 2,
    )


def feed(base, x, mine, theirs, vec, weights):
    return run(
        feed_kernel, [], [x, mine, theirs, vec, weights[2], weights[3]],
        [sds(ROWS, D, dtype=F32), sds(ROWS, D), sds(ROWS, D), STATS,
         sds(ROWS, HIDDEN), sds(ROWS, HIDDEN), sds(ROWS, D)],
        [], base,
    )


FEED_BACK_OUTS = [
    sds(ROWS, D, dtype=F32), sds(ROWS, D), sds(8, D, dtype=F32), sds(ROWS, HIDDEN), sds(ROWS, D),
]


def feed_back_second(ids, first, mine, theirs, vec, own, other, slope, weights):
    return run(
        feed_back_second_kernel, [ids],
        [first, mine, theirs, vec, own, other, slope, weights[2], weights[3]],
        [sds(HALF, D)] + FEED_BACK_OUTS,
        [pltpu.VMEM((ROWS, D), BF16), pltpu.VMEM((ROWS, D), BF16)], 6,
    )


def feed_back_first(ids, normed, inv, vec, own, other, resid, mine, theirs, slope, weights):
    return run(
        feed_back_first_kernel, [ids],
        [normed, inv, vec, own, other, resid, mine, theirs, slope, weights[2], weights[3]],
        [sds(HALF, D, dtype=F32)] + FEED_BACK_OUTS,
        [pltpu.VMEM((ROWS, D), BF16), pltpu.VMEM((ROWS, D), F32)], 2,
    )


def attend_back(base, ids, gs, mine, theirs, normed, inv, qkv, prob, vec, weights):
    return run(
        attend_back_kernel, [ids],
        [gs, mine, theirs, normed, inv, vec, qkv, prob, weights[0], weights[1]],
        [sds(ROWS, D, dtype=F32), sds(ROWS, D), sds(8, D, dtype=F32), sds(ROWS, 1152), sds(ROWS, D),
         sds(HALF if base == 0 else 16, D)],
        [pltpu.VMEM((ROWS, PIECE), BF16), WIDE], base,
    )


SPLIT_OUTS = [sds(32, *BLOCK), sds(32, *BLOCK)]
BLOCKS = pltpu.VMEM((4, 2, 8) + BLOCK, BF16)


def out_grad(chunk, ids, act, gs_low):
    return run(out_grad_kernel, [ids], [act, gs_low], SPLIT_OUTS, [BLOCKS], chunk)


def in_grad(chunk, ids, low, grad_pre):
    return run(in_grad_kernel, [ids], [low, grad_pre], SPLIT_OUTS, [BLOCKS], chunk)


def attend_grad(chunk, ids, x, grad_qkv, ctx, low, norms=()):
    outs = SPLIT_OUTS
    if norms:
        outs = [sds(33, *BLOCK), sds(32, *BLOCK), sds(8, D, dtype=F32)]
    return run(
        attend_grad_kernel, [ids], [x, grad_qkv, ctx, low, *norms], outs, [BLOCKS], chunk
    )


def vectors(rows):
    return run(vectors_kernel, [], rows, [sds(8, D, dtype=F32)], [])[0]


def split(sources, norm=None):
    arrays = [a for pair in sources for a in pair]
    sizes = tuple(keep.shape[0] // 2 for keep, _ in sources)
    count = sum(sizes)
    outs = [sds(count + (norm is not None), *BLOCK), sds(count, *BLOCK)]
    if norm is not None:
        arrays, outs = arrays + [norm], outs + [sds(8, D, dtype=F32)]
    return run(split_kernel, [], arrays, outs, [], sizes, int(norm is not None))


def far_add(keep, got, norm=None):
    if norm is None:
        return run(far_kernel, [], [keep, got], [sds(*keep.shape)], [], 0)
    count = keep.shape[0] - keep.shape[0] % 8
    outs = [sds(count + 1, *BLOCK), sds(8, D, dtype=F32)]
    return run(far_kernel, [], [keep, got, norm], outs, [], 1)


def join(held, got, count=1):
    size = held.shape[0] // count
    return run(join_kernel, [], [held, got], [sds(2 * size, *BLOCK)] * count, [], count)


PLACED = [
    sds(HIDDEN, D, dtype=F32),
    sds(D, HIDDEN, dtype=F32),
    sds(3, D, PIECE, dtype=F32),
    sds(PIECE, D, dtype=F32),
]


def place(ids, items, values, into=()):
    return pl.pallas_call(
        functools.partial(place_kernel, tuple(items)),
        out_shape=PLACED,
        in_specs=[SCALARS] + [LOCAL] * len(values) + [REMOTE] * len(into),
        out_specs=[REMOTE] * 4,
        scratch_shapes=[pltpu.VMEM((6, PIECE, PIECE), F32), pltpu.SemaphoreType.DMA((6,))],
        input_output_aliases={1 + len(values) + i: i for i in range(len(into))},
        compiler_params=pltpu.CompilerParams(vmem_limit_bytes=6 * 2**20),
        cost_estimate=COST,
        name="place_kernel",
    )(ids, *values, *into)


def swap(value):
    return lax.ppermute(value, "tensor", SWAP)


def flip(chip, core, stage, axis):
    pos = [chip % 4, chip // 4 % 4, chip // 16]
    low = (core == 0) == (stage == 0)
    pos[axis] = pos[axis] ^ 1 if low else 3 - pos[axis]
    return pos[0] + 4 * pos[1] + 16 * pos[2]


def exchange(value, stage, axis):
    pairs = [
        (2 * chip + core, 2 * flip(chip, core, stage, axis) + core)
        for chip in range(64)
        for core in range(2)
    ]
    return lax.ppermute(value, ("dp", "tensor"), pairs)


class Order:
    def __init__(self):
        self.token = None

    def hold(self, value):
        if self.token is None:
            return value
        return lax.optimization_barrier((value, self.token))[0]


class Single:
    def __init__(self, order, axes, send, keep, norm=None):
        self.order, self.axes, self.keep, self.norm, self.round = order, axes, keep, norm, 0
        self.send(send, 0, 0)

    def send(self, value, stage, j):
        self.order.token = value
        self.got = exchange(value, stage, self.axes[j % 3])

    def next(self):
        self.round += 1
        got = self.order.hold(self.got)
        if self.round > 8:
            self.got = self.order.token = got
            return
        if self.round < 3:
            value, self.keep, *norm = split([(self.keep, got)], self.norm)
            self.send(value, 0, self.round)
        elif self.round < 6:
            self.keep, *norm = far_add(self.keep, got, self.norm)
            self.send(self.keep, 1, self.round)
        elif self.round == 6:
            self.keep, *norm = far_add(self.keep, got, self.norm)
            if norm:
                self.keep = self.keep[:8]
            self.send(self.keep, 0, 2)
        else:
            norm = ()
            self.keep = join(self.keep, got)[0]
            self.send(self.keep, 0, 8 - self.round)
        if norm:
            self.norm = norm[0]


class Pair:
    def __init__(self, order, axes):
        self.order, self.axes = order, axes
        self.keep, self.got, self.calls = [None, None], [None, None], [0, 0]
        self.both = 2

    def start(self, i, send, keep):
        self.keep[i] = keep
        self.send(i, send, 0)

    def send(self, i, value, j):
        self.order.token = value
        self.got[i] = exchange(value, 0, self.axes[i ^ j])

    def next(self, i):
        self.calls[i] += 1
        if self.calls[i] == 1:
            value, self.keep[i] = split([(self.keep[i], self.order.hold(self.got[i]))])
            self.send(i, value, 1)
        elif self.calls[i] == 2 and self.calls[1 - i] == 2:
            got = [self.order.hold(g) for g in self.got]
            value, self.held = split([(self.keep[0], got[0]), (self.keep[1], got[1])])
            self.order.token = value
            self.arrived = exchange(value, 0, self.axes[2])
        elif self.calls[i] == 3:
            self.keep[i] = join(self.keep[i], self.order.hold(self.got[i]))[0]
            self.send(i, self.keep[i], 0)
        elif self.calls[i] == 4:
            self.got[i] = self.order.token = self.order.hold(self.got[i])

    def next_both(self):
        got = self.order.hold(self.arrived)
        self.both += 1
        if self.both <= 6:
            self.held = far_add(self.held, got)[0]
            self.order.token = self.held
            if self.both < 6:
                self.arrived = exchange(self.held, 1, self.axes[self.both - 3])
            else:
                self.arrived = exchange(self.held, 0, self.axes[2])
        else:
            self.keep = list(join(self.held, got, 2))
            for i in range(2):
                self.send(i, self.keep[i], 1)


UPPER_PAIR, UPPER_LAST = (0, 1, 2), (2, 1, 0)
LOWER_PAIR, LOWER_LAST = (0, 1, 2), (2, 0, 1)
CHUNK_AXES = [
    UPPER_PAIR,
    (UPPER_PAIR[1], UPPER_PAIR[0], UPPER_PAIR[2]),
    UPPER_LAST,
    LOWER_PAIR,
    (LOWER_PAIR[1], LOWER_PAIR[0], LOWER_PAIR[2]),
    LOWER_LAST,
]
TAIL = (
    "Lp", "Lq", "Ub", "Um", "Lp", "Lb", "Lq", "Ub", "Um", "Lb", "Lm", "Ub", "Lb",
    "Um", "Lm", "Lb", "Ub", "Um", "Lb", "Lm", "Ub", "Up", "Lb", "Ub", "Lm", "Uq",
    "Lb", "Ub", "Up", "Lm", "Lb", "Uq", "Lq", "Ub", "Lp",
)


def device_table():
    rows = []
    for chip in range(64):
        pos = [chip % 4, chip // 4 % 4, chip // 16]
        low = [(p ^ (p >> 1)) & 1 for p in pos]
        high = [p >> 1 for p in pos]
        for core in range(2):
            near = low if core == 0 else high
            row = [core]
            for axes in CHUNK_AXES:
                row += [near[axis] for axis in axes] + [0]
            rows.append(row + [0] * 7)
    return np.array(rows, np.int32)


def on_device(
    tokens,
    skip_tokens,
    cot_back,
    cot_head,
    one_span,
    *params,
):
    lower = [params[i] for i in (0, 1, 4, 5)]
    upper = [params[i] for i in (8, 9, 12, 13)]
    device = lax.axis_index("dp") * 2 + lax.axis_index("tensor")
    row = lax.dynamic_index_in_dim(jnp.asarray(device_table()), device, 0, keepdims=False)
    ids = jnp.concatenate([row, one_span])
    tokens_other = swap(tokens)
    tokens, ids = lax.optimization_barrier((tokens, ids))
    vec = vectors([params[i] for i in (2, 3, 6, 7, 10, 11, 14, 15)])
    skip_other = swap(skip_tokens)
    cot_head_other = swap(cot_head)
    cot_back_other = swap(cot_back)
    order = Order()

    x_l, qkv_l, prob_l, ctx_l, part = attend_first(ids, tokens, tokens_other, lower)
    first_l, low_l, normed_al, inv_al, act_l, slope_l, part = feed(
        0, x_l, part, swap(part), vec, lower
    )
    x_u, normed_fl, inv_fl, back_out, qkv_u, prob_u, ctx_u, part = attend_second(
        ids, first_l, part, swap(part), vec, skip_tokens, skip_other, upper
    )
    first_u, low_u, normed_au, inv_au, act_u, slope_u, part = feed(
        4, x_u, part, swap(part), vec, upper
    )
    head_out, gs_u, gs_low_u, norms_fu, grad_pre_u, part = feed_back_second(
        ids, first_u, part, swap(part), vec, cot_head, cot_head_other, slope_u, upper
    )
    pair_u, pair_l = Pair(order, UPPER_PAIR), Pair(order, LOWER_PAIR)
    theirs = swap(part)
    pair_u.start(0, *out_grad(0, ids, act_u, gs_low_u))
    pair_u.start(1, *in_grad(1, ids, low_u, order.hold(grad_pre_u)))
    resid_u, gr_low_u, norms_au, grad_qkv_u, part, _ = attend_back(
        4, ids, order.hold(gs_u), part, theirs, normed_au, inv_au, qkv_u, prob_u, vec=vec,
        weights=upper,
    )
    theirs = swap(part)
    at_u = Single(
        order, UPPER_LAST, *attend_grad(2, ids, x_u, grad_qkv_u, ctx_u, order.hold(gr_low_u))
    )
    pair_u.next(0)
    pair_u.next(1)
    grad_skip, gs_l, gs_low_l, norms_fl, grad_pre_l, part = feed_back_first(
        ids, normed_fl, inv_fl, vec, cot_back, cot_back_other, order.hold(resid_u), part,
        theirs, slope_l, lower,
    )
    theirs = swap(part)
    order.token = gs_low_l
    pair_u.next(0)
    pair_u.next(1)
    pair_l.start(0, *out_grad(3, ids, act_l, order.hold(gs_low_l)))
    pair_l.start(1, *in_grad(4, ids, low_l, order.hold(grad_pre_l)))
    at_u.next()
    pair_u.next_both()
    resid_l, gr_low_l, norms_al, grad_qkv_l, part, away = attend_back(
        0, ids, order.hold(gs_l), part, theirs, normed_al, inv_al, qkv_l, prob_l, vec=vec,
        weights=lower,
    )
    away = swap(away)
    at_l = Single(
        order, LOWER_LAST,
        *attend_grad(
            5, ids, x_l, grad_qkv_l, ctx_l, gr_low_l, (norms_al, norms_fl, norms_au, norms_fu)
        ),
    )
    act = {
        "Up": lambda: pair_u.next(0),
        "Uq": lambda: pair_u.next(1),
        "Um": pair_u.next_both,
        "Ub": at_u.next,
        "Lp": lambda: pair_l.next(0),
        "Lq": lambda: pair_l.next(1),
        "Lm": pair_l.next_both,
        "Lb": at_l.next,
    }
    grad_tokens = run(
        rows_kernel, [ids], [order.hold(resid_l), part, away], [sds(HALF, D, dtype=F32)], []
    )[0]
    order.token = grad_tokens
    for name in TAIL:
        act[name]()
    done_u = place(
        ids,
        [(0, 0), (0, 1), (1, 0), (1, 1), (2, 0), (2, 1)],
        [pair_u.keep[0], pair_u.got[0], pair_u.keep[1], pair_u.got[1], at_u.keep,
         order.hold(at_u.got)],
    )
    order.token = done_u[0]
    done_l = place(
        ids, [(3, 0), (4, 0), (5, 0)],
        [pair_l.keep[0], pair_l.keep[1], order.hold(at_l.keep)],
    )
    done_l = place(
        ids, [(4, 1), (3, 1), (5, 1)], [pair_l.got[1], pair_l.got[0], at_l.got], done_l
    )
    norms = at_l.norm
    out_gu, in_gu, qkv_gu, proj_gu = done_u
    out_gl, in_gl, qkv_gl, proj_gl = done_l
    return (
        back_out,
        head_out,
        grad_tokens,
        grad_skip,
        qkv_gl,
        proj_gl,
        norms[0],
        norms[1],
        in_gl,
        out_gl,
        norms[2],
        norms[3],
        qkv_gu,
        proj_gu,
        norms[4],
        norms[5],
        in_gu,
        out_gu,
        norms[6],
        norms[7],
    )


def solution(mesh):
    rows = P(("dp", "tensor"), None)
    weights = (
        P(None, None, "tensor"),
        P("tensor", None),
        P(),
        P(),
        P(None, "tensor"),
        P("tensor", None),
        P(),
        P(),
    )
    return jax.shard_map(
        on_device,
        mesh=mesh,
        in_specs=(rows,) * 4 + (P("dp"),) + weights + weights,
        out_specs=(rows,) * 4 + weights + weights,
        check_vma=False,
    )
```

```python
import functools

import jax
import jax.numpy as jnp
import numpy as np
from jax import lax
from jax.experimental import pallas as pl
from jax.experimental.pallas import tpu as pltpu
from jax.sharding import PartitionSpec as P

SPAN = 128
EPS = 1e-06
SCALE = 0.125
NEG = -1000000000.0

D = 768
ROWS = 768
HALF = ROWS // 2
HIDDEN = 1536
PIECE = 384
PAIR = 128
BLOCK = (48, 384)
F32 = jnp.float32
BF16 = jnp.bfloat16
SPANS_AT = 32

SWAP = [(0, 1), (1, 0)]


def dot_nn(left, right):
    return lax.dot_general(left, right, (((1,), (0,)), ((), ())), preferred_element_type=F32)


def dot_nt(left, right):
    return lax.dot_general(left, right, (((1,), (1,)), ((), ())), preferred_element_type=F32)


def dot_tn(left, right):
    return lax.dot_general(left, right, (((0,), (0,)), ((), ())), preferred_element_type=F32)


def normalize(resid):
    mean = jnp.mean(resid, axis=-1, keepdims=True)
    centered = resid - mean
    var = jnp.mean(centered * centered, axis=-1, keepdims=True)
    inv = lax.rsqrt(var + EPS)
    return centered * inv, inv


def norm_grad(grad_out, normed, inv, gain):
    grad = grad_out * gain
    first = jnp.mean(grad, axis=-1, keepdims=True)
    second = jnp.mean(grad * normed, axis=-1, keepdims=True)
    return inv * (grad - first - normed * second)


def fold(value):
    return jnp.sum(value.reshape(-1, 8, value.shape[-1]), axis=0)

DOC = 2 * SPAN
DOCS = ROWS // DOC


def doc_rows(doc):
    return slice(doc * DOC, (doc + 1) * DOC)


def half_rows(index):
    return pl.ds(pl.multiple_of(index * HALF, HALF), HALF)


def join_halves(side, own_ref, other_ref, full_ref):
    full_ref[half_rows(side), :] = own_ref[...]
    full_ref[half_rows(1 - side), :] = other_ref[...]


def doc_masks(ids_ref, doc):
    row = lax.broadcasted_iota(jnp.int32, (DOC, 1), 0)
    keep = jnp.where((row < SPAN) | (ids_ref[SPANS_AT + doc] == 0), 1.0, 0.0)
    return keep, (row & (SPAN - 1)) == 0


def spread(column):
    return jnp.broadcast_to(column, (column.shape[0], 128))


def head_masks():
    lane = lax.broadcasted_iota(jnp.int32, (1, PAIR), 1)
    return lane < 64


def both_heads(value, left):
    zero = jnp.zeros_like(value)
    return jnp.concatenate([jnp.where(left, value, zero), jnp.where(left, zero, value)], axis=0)


class Rows:
    def __init__(self, *refs):
        self.refs = refs

    def find(self, index):
        head = index[0] if isinstance(index, tuple) else index
        rest = index[1:] if isinstance(index, tuple) else ()
        at = head if isinstance(head, int) else head.start
        base = 0
        for ref in self.refs:
            if at < base + ref.shape[0]:
                break
            base += ref.shape[0]
        head = head - base if isinstance(head, int) else slice(at - base, head.stop - base)
        return ref, (head, *rest)

    def __getitem__(self, index):
        head = index[0] if isinstance(index, tuple) else index
        if head is Ellipsis or head == slice(None):
            return jnp.concatenate([ref[index] for ref in self.refs], axis=0)
        ref, index = self.find(index)
        return ref[index]


GROUPS = ((0, 1), (2,))


def attend(ids_ref, docs, x_ref, proj_ref, qkv_ref, prob_ref, ctx_ref, part_ref, wide, skip=0):
    for i, doc in enumerate(docs):
        at = doc_rows(i)
        out = dot_nn(x_ref[doc_rows(i + skip), :], wide[...])
        qkv_ref[at, :384] = (out[:, :384] * SCALE).astype(BF16)
        qkv_ref[at, 384:] = out[:, 384:].astype(BF16)
    left = head_masks()
    col = lax.broadcasted_iota(jnp.int32, (1, 2 * DOC), 1) & (DOC - 1)
    for i, doc in enumerate(docs):
        at = doc_rows(i)
        key_ok = (col < SPAN) | (ids_ref[SPANS_AT + doc] == 0)
        scores = []
        for pair in range(3):
            query = qkv_ref[at, pair * PAIR:(pair + 1) * PAIR]
            keys = qkv_ref[at, 384 + pair * PAIR:384 + (pair + 1) * PAIR]
            scores.append(jnp.where(key_ok, dot_nt(query, both_heads(keys, left)), NEG))
        for pair in range(3):
            probs = []
            for head in range(2):
                score = scores[pair][:, head * DOC:(head + 1) * DOC]
                raised = jnp.exp(score - jnp.max(score, axis=-1, keepdims=True))
                probs.append(
                    (raised * (1.0 / jnp.sum(raised, axis=-1, keepdims=True))).astype(BF16)
                )
            prob = jnp.concatenate(probs, axis=1)
            prob_ref[i, pair] = prob
            values = qkv_ref[at, 768 + pair * PAIR:768 + (pair + 1) * PAIR]
            mixed = dot_nn(prob, both_heads(values, left))
            ctx_ref[at, pair * PAIR:(pair + 1) * PAIR] = mixed.astype(BF16)
    for i, doc in enumerate(docs):
        at = doc_rows(i)
        part_ref[at, :] = dot_nn(ctx_ref[at, :], proj_ref[...]).astype(BF16)


def attend_first_kernel(
    docs, ids_ref, other_ref, own_ref, qkv_w_ref, proj_w_ref,
    x_ref, wide, proj, qkv_ref, prob_ref, ctx_ref, part_ref, sems,
):
    side = ids_ref[0]
    copies = [pltpu.make_async_copy(own_ref, x_ref.at[half_rows(side), :], sems.at[0])]
    for index in range(3):
        cut = slice(index * 384, (index + 1) * 384)
        copies.append(
            pltpu.make_async_copy(qkv_w_ref.at[index], wide.at[:, cut], sems.at[1 + index])
        )
    copies.append(pltpu.make_async_copy(proj_w_ref, proj, sems.at[4]))
    for copy in copies:
        copy.start()
    x_ref[half_rows(1 - side), :] = other_ref[...]
    for copy in copies:
        copy.wait()
    attend(ids_ref, docs, x_ref, proj, qkv_ref, prob_ref, ctx_ref, part_ref, wide)


def attend_more_kernel(
    docs, ids_ref, x_ref, wide_ref, proj_ref, qkv_ref, prob_ref, ctx_ref, part_ref,
):
    attend(
        ids_ref, docs, x_ref, proj_ref, qkv_ref, prob_ref, ctx_ref, part_ref, wide_ref, docs[0]
    )


def attend_second_kernel(
    docs, base, ids_ref, first_ref, mine_ref, theirs_ref, vec_ref, own_ref, other_ref,
    qkv_w_ref, proj_ref,
    x_ref, normed_ref, inv_ref, back_ref, qkv_ref, prob_ref, ctx_ref, part_ref, *rest,
):
    *wide_out, full = rest
    join_halves(ids_ref[0], own_ref, other_ref, full)
    for i, doc in enumerate(docs):
        at = doc_rows(i)
        keep, cls = doc_masks(ids_ref, doc)
        resid = first_ref[at, :] + mine_ref[at, :].astype(F32) + theirs_ref[at, :].astype(F32)
        normed, inv = normalize(resid)
        back = normed * vec_ref[base:base + 1, :] + vec_ref[base + 1:base + 2, :]
        normed_ref[at, :] = normed.astype(BF16)
        inv_ref[at, :] = spread(inv)
        x_ref[at, :] = jnp.where(cls, back, full[doc_rows(doc), :].astype(F32)).astype(BF16)
        back_ref[at, :] = (back * keep).astype(BF16)
    wide = qkv_w_ref
    if wide_out:
        wide = wide_out[0]
        for index in range(3):
            wide[:, index * 384:(index + 1) * 384] = qkv_w_ref[index]
    attend(ids_ref, docs, x_ref, proj_ref, qkv_ref, prob_ref, ctx_ref, part_ref, wide)


def feed_kernel(
    docs, skip, base, x_ref, mine_ref, theirs_ref, vec_ref, in_ref, out_w_ref,
    first_ref, low_ref, normed_ref, inv_ref, act_ref, slope_ref, part_ref,
):
    for i, doc in enumerate(docs):
        at = doc_rows(i)
        resid = x_ref[doc_rows(i + skip), :].astype(F32) + mine_ref[at, :].astype(F32)
        resid = resid + theirs_ref[at, :].astype(F32)
        normed, inv = normalize(resid)
        first = normed * vec_ref[base:base + 1, :] + vec_ref[base + 1:base + 2, :]
        normed_ref[at, :] = normed.astype(BF16)
        inv_ref[at, :] = spread(inv)
        first_ref[at, :] = first
        low_ref[at, :] = first.astype(BF16)
    for i, doc in enumerate(docs):
        at = doc_rows(i)
        for piece in range(3):
            cut = slice(piece * 512, (piece + 1) * 512)
            pre = dot_nn(low_ref[at, :], in_ref[:, cut])
            share = 0.5 * (1.0 + lax.erf(pre * 0.7071067811865476))
            density = jnp.exp(-0.5 * pre * pre) * 0.3989422804014327
            act_ref[at, cut] = (pre * share).astype(BF16)
            slope_ref[at, cut] = (share + pre * density).astype(BF16)
    for i, doc in enumerate(docs):
        at = doc_rows(i)
        part_ref[at, :] = dot_nn(act_ref[at, :], out_w_ref[...]).astype(BF16)


def feed_back(gs_low_ref, slope_ref, in_ref, out_w_ref, grad_pre_ref, part_ref):
    for doc in range(DOCS):
        at = doc_rows(doc)
        for piece in range(3):
            cut = slice(piece * 512, (piece + 1) * 512)
            grad_act = dot_nt(gs_low_ref[at, :], out_w_ref[cut, :])
            grad_pre_ref[at, cut] = (grad_act * slope_ref[at, cut].astype(F32)).astype(BF16)
    for doc in range(DOCS):
        at = doc_rows(doc)
        part_ref[at, :] = dot_nt(grad_pre_ref[at, :], in_ref[...]).astype(BF16)


def put_norm_grads(norms_ref, sums):
    gain, shift = sums
    norms_ref[...] = jnp.zeros_like(norms_ref)
    norms_ref[0:1, :] = jnp.sum(gain, axis=0, keepdims=True)
    norms_ref[1:2, :] = jnp.sum(shift, axis=0, keepdims=True)


def add_sums(sums, grad_out, normed):
    new = (fold(grad_out * normed), fold(grad_out))
    return new if sums is None else (sums[0] + new[0], sums[1] + new[1])


def feed_back_second_kernel(
    base, ids_ref, first_ref, mine_ref, theirs_ref, vec_ref, own_ref, other_ref,
    slope_ref, in_ref, out_w_ref,
    head_ref, gs_ref, gs_low_ref, norms_ref, grad_pre_ref, part_ref, cot, full,
):
    side = ids_ref[0]
    join_halves(side, own_ref, other_ref, cot)
    sums = None
    for doc in range(DOCS):
        at = doc_rows(doc)
        keep, _ = doc_masks(ids_ref, doc)
        resid = first_ref[at, :] + mine_ref[at, :].astype(F32) + theirs_ref[at, :].astype(F32)
        normed, inv = normalize(resid)
        head = normed * vec_ref[base:base + 1, :] + vec_ref[base + 1:base + 2, :]
        full[at, :] = (head * keep).astype(BF16)
        grad_out = cot[at, :].astype(F32) * keep
        grad = norm_grad(grad_out, normed, inv, vec_ref[base:base + 1, :])
        gs_ref[at, :] = grad
        gs_low_ref[at, :] = grad.astype(BF16)
        sums = add_sums(sums, grad_out, normed)
    head_ref[...] = full[half_rows(side), :]
    put_norm_grads(norms_ref, sums)
    feed_back(gs_low_ref, slope_ref, in_ref, out_w_ref, grad_pre_ref, part_ref)


def feed_back_first_kernel(
    base, ids_ref, normed_ref, inv_ref, vec_ref, own_ref, other_ref,
    resid_ref, mine_ref, theirs_ref, slope_ref, in_ref, out_w_ref,
    skip_ref, gs_ref, gs_low_ref, norms_ref, grad_pre_ref, part_ref, cot, full,
):
    side = ids_ref[0]
    join_halves(side, own_ref, other_ref, cot)
    sums = None
    for doc in range(DOCS):
        at = doc_rows(doc)
        keep, cls = doc_masks(ids_ref, doc)
        above = resid_ref[at, :] + mine_ref[at, :].astype(F32) + theirs_ref[at, :].astype(F32)
        full[at, :] = jnp.where(cls, 0.0, above)
        normed = normed_ref[at, :].astype(F32)
        grad_out = cot[at, :].astype(F32) * keep + jnp.where(cls, above, 0.0)
        grad = norm_grad(grad_out, normed, inv_ref[at, 0:1], vec_ref[base:base + 1, :])
        gs_ref[at, :] = grad
        gs_low_ref[at, :] = grad.astype(BF16)
        sums = add_sums(sums, grad_out, normed)
    skip_ref[...] = full[half_rows(side), :]
    put_norm_grads(norms_ref, sums)
    feed_back(gs_low_ref, slope_ref, in_ref, out_w_ref, grad_pre_ref, part_ref)


def attend_back_kernel(
    base, ids_ref, gs_ref, mine_ref, theirs_ref, normed_ref, inv_ref, vec_ref, qkv_ref, prob_ref,
    qkv_w_ref, proj_ref,
    resid_ref, low_ref, norms_ref, grad_qkv_ref, part_ref, away_ref, grad_ctx, wide,
):
    for index in range(3):
        wide[:, index * 384:(index + 1) * 384] = qkv_w_ref[index]
    sums = None
    for doc in range(DOCS):
        at = doc_rows(doc)
        grad_out = gs_ref[at, :] + mine_ref[at, :].astype(F32) + theirs_ref[at, :].astype(F32)
        normed = normed_ref[at, :].astype(F32)
        grad = norm_grad(grad_out, normed, inv_ref[at, 0:1], vec_ref[base:base + 1, :])
        resid_ref[at, :] = grad
        low_ref[at, :] = grad.astype(BF16)
        sums = add_sums(sums, grad_out, normed)
    put_norm_grads(norms_ref, sums)
    for doc in range(DOCS):
        at = doc_rows(doc)
        grad_ctx[at, :] = dot_nt(low_ref[at, :], proj_ref[...]).astype(BF16)
    left = head_masks()
    for doc in range(DOCS):
        at = doc_rows(doc)
        pairs = [slice(pair * PAIR, (pair + 1) * PAIR) for pair in range(3)]
        grad_probs = []
        for pair in range(3):
            values = qkv_ref[at, 768 + pair * PAIR:768 + (pair + 1) * PAIR]
            grad_probs.append(dot_nt(grad_ctx[at, pairs[pair]], both_heads(values, left)))
        for pair in range(3):
            prob_low = prob_ref[doc, pair]
            scored = []
            for head in range(2):
                cut = slice(head * DOC, (head + 1) * DOC)
                prob = prob_low[:, cut].astype(F32)
                grad_prob = grad_probs[pair][:, cut]
                inner = jnp.sum(grad_prob * prob, axis=-1, keepdims=True)
                scored.append((prob * (grad_prob - inner)).astype(BF16))
            grad_scores = jnp.concatenate(scored, axis=1)
            query = qkv_ref[at, pairs[pair]]
            keys = qkv_ref[at, 384 + pair * PAIR:384 + (pair + 1) * PAIR]
            grad_query = dot_nn(grad_scores, both_heads(keys, left)) * SCALE
            grad_keys = dot_tn(grad_scores, query)
            grad_values = dot_tn(prob_low, grad_ctx[at, pairs[pair]])
            grad_qkv_ref[at, pair * PAIR:(pair + 1) * PAIR] = grad_query.astype(BF16)
            for index, grad in ((1, grad_keys), (2, grad_values)):
                cut = slice(index * 384 + pair * PAIR, index * 384 + (pair + 1) * PAIR)
                grad_qkv_ref[at, cut] = jnp.where(left, grad[:DOC], grad[DOC:]).astype(BF16)
    for doc in range(DOCS):
        at = doc_rows(doc)
        part_ref[at, :] = dot_nt(grad_qkv_ref[at, :], wide[...]).astype(BF16)
    if base == 0:
        away_ref[...] = part_ref[half_rows(1 - ids_ref[0]), :]
    else:
        away_ref[...] = jnp.zeros_like(away_ref)


def rows_kernel(ids_ref, resid_ref, mine_ref, theirs_ref, back_ref, out_ref, back_out_ref, full):
    at = half_rows(ids_ref[0])
    out_ref[...] = resid_ref[at, :] + mine_ref[at, :].astype(F32) + theirs_ref[...].astype(F32)
    full[...] = back_ref[...]
    back_out_ref[...] = full[at, :]


def cut_wide(value, blocks, piece):
    for half in range(2):
        for k in range(8):
            blocks[piece, half, k] = value[k * 48:(k + 1) * 48, half * 384:(half + 1) * 384]


def cut_tall(value, blocks, piece):
    for half in range(2):
        for k in range(8):
            at = half * 384 + k * 48
            blocks[piece, half, k] = value[at:at + 48, :]


def put_blocks(ids_ref, turn, blocks, send_ref, keep_ref):
    first, second, third, outer = [ids_ref[1 + 4 * turn + i] for i in range(4)]
    for rel, ref in ((1, send_ref), (0, keep_ref)):
        for b in range(2):
            piece = 2 * (rel ^ first) + (b ^ second)
            for e in range(2):
                for k in range(8):
                    ref[16 * b + 8 * e + k] = blocks[piece, e ^ third, k ^ outer]


def out_grad_kernel(turn, ids_ref, act_ref, gs_ref, send_ref, keep_ref, blocks):
    for p in range(2):
        value = dot_tn(act_ref[:, p * 768:(p + 1) * 768], gs_ref[...]).astype(BF16)
        cut_wide(value[:384], blocks, 2 * p)
        cut_wide(value[384:], blocks, 2 * p + 1)
    put_blocks(ids_ref, turn, blocks, send_ref, keep_ref)


def in_grad_kernel(turn, ids_ref, low_ref, grad_ref, send_ref, keep_ref, blocks):
    for p in range(2):
        value = dot_tn(low_ref[...], grad_ref[:, p * 768:(p + 1) * 768]).astype(BF16)
        cut_tall(value[:, :384], blocks, 2 * p)
        cut_tall(value[:, 384:], blocks, 2 * p + 1)
    put_blocks(ids_ref, turn, blocks, send_ref, keep_ref)


def attend_grad_kernel(turn, ids_ref, x_ref, grad_ref, ctx_ref, low_ref, *refs):
    norm_refs, (send_ref, keep_ref), blocks = refs[:-3 - (len(refs) > 3)], refs[-3:-1], refs[-1]
    if norm_refs:
        send_ref, keep_ref = refs[-4:-2]
        value = jnp.concatenate([ref[0:2, :] for ref in norm_refs], axis=0)
        refs[-2][...] = value
        send_ref[32] = norm_block(value)
    value = dot_tn(x_ref[...], grad_ref[...]).astype(BF16)
    for piece in range(3):
        cut_tall(value[:, piece * 384:(piece + 1) * 384], blocks, piece)
    cut_wide(dot_tn(ctx_ref[...], low_ref[...]).astype(BF16), blocks, 3)
    put_blocks(ids_ref, turn, blocks, send_ref, keep_ref)


def vectors_kernel(*refs):
    out_ref = refs[-1]
    for i in range(8):
        out_ref[i:i + 1, :] = refs[i][...].reshape(1, D)


def plus(one, two):
    return (one.astype(F32) + two.astype(F32)).astype(BF16)


def norm_block(value):
    high = value.astype(BF16)
    low = (value - high.astype(F32)).astype(BF16)
    rows = [high[:, :PIECE], high[:, PIECE:], low[:, :PIECE], low[:, PIECE:]]
    return jnp.concatenate(rows + [jnp.zeros((16, PIECE), BF16)], axis=0)


def block_norm(block):
    high = jnp.concatenate([block[0:8], block[8:16]], axis=1)
    low = jnp.concatenate([block[16:24], block[24:32]], axis=1)
    return high.astype(F32) + low.astype(F32)


def add_norm(value, block):
    return block_norm(norm_block(value)) + block_norm(block)


def split_kernel(sizes, with_norm, *refs):
    count = len(sizes)
    ins, outs = refs[:2 * count], refs[2 * count + with_norm:]
    at = 0
    for i, m in enumerate(sizes):
        keep, got = ins[2 * i], ins[2 * i + 1]
        outs[1][at:at + m] = plus(keep[:m], got[:m])
        outs[0][at:at + m] = plus(keep[m:], got[m:2 * m])
        at += m
    if with_norm:
        value = add_norm(refs[2 * count][...], ins[1][2 * sizes[0]])
        outs[0][at] = norm_block(value)
        outs[2][...] = value


def far_kernel(with_norm, *refs):
    if with_norm:
        keep, got, norm, out, norm_out = refs
        count = keep.shape[0] - (keep.shape[0] % 8)
        value = add_norm(norm[...], got[got.shape[0] - 1])
        out[count] = norm_block(value)
        norm_out[...] = value
    else:
        keep, got, out = refs
        count = keep.shape[0]
    out[:count] = plus(keep[:count], got[:count])


def join_kernel(count, held_ref, got_ref, *outs):
    size = outs[0].shape[0] // 2
    for i in range(count):
        at = slice(i * size, (i + 1) * size)
        outs[i][:size] = held_ref[at]
        outs[i][size:] = got_ref[at]


def place_kernel(items, ids_ref, *refs):
    ins, outs, squares, sems = refs[:len(items)], refs[-6:-2], refs[-2], refs[-1]
    slots = squares.shape[0]

    def copies(index, chunk, far, b, e):
        first, second = ids_ref[1 + 4 * chunk], ids_ref[2 + 4 * chunk]
        turn = chunk % 3
        slot = index % slots
        piece = 2 * (far ^ first) + (b ^ second)
        at = pl.ds(pl.multiple_of(piece * PIECE, PIECE), PIECE)
        cut = slice(e * PIECE, (e + 1) * PIECE)

        def copy(ref):
            return pltpu.make_async_copy(squares.at[slot], ref, sems.at[slot])

        if turn == 0:
            return [(None, copy(outs[0].at[at, cut]))]
        if turn == 1:
            return [(None, copy(outs[1].at[cut, at]))]
        return [
            (piece < 3, copy(outs[2].at[jnp.minimum(piece, 2), cut, :])),
            (piece == 3, copy(outs[3].at[:, cut])),
        ]

    def each(pairs, wait):
        for when, copy in pairs:
            def act(copy=copy):
                copy.wait() if wait else copy.start()

            if when is None:
                act()
            else:
                pl.when(when)(act)

    flight = []
    for (chunk, far), from_ref in zip(items, ins):
        third, outer = ids_ref[3 + 4 * chunk], ids_ref[4 + 4 * chunk]
        for b in range(2):
            for e in range(2):
                index = len(flight)
                if index >= slots:
                    each(flight[index - slots], True)
                for k in range(8):
                    block = from_ref[16 * b + 8 * (e ^ third) + (k ^ outer)]
                    squares[index % slots, k * 48:(k + 1) * 48, :] = block.astype(F32)
                flight.append(copies(index, chunk, far, b, e))
                each(flight[index], False)
    for pairs in flight[-slots:]:
        each(pairs, True)


def sds(*shape, dtype=BF16):
    return jax.ShapeDtypeStruct(shape, dtype)


SCALARS = pl.BlockSpec(memory_space=pltpu.SMEM)
LOCAL = pl.BlockSpec(memory_space=pltpu.VMEM)
REMOTE = pl.BlockSpec(memory_space=pl.ANY)
DISTANT = pl.BlockSpec(memory_space=pltpu.HBM)


COST = pl.CostEstimate(flops=1, bytes_accessed=1, transcendentals=0)


LIMITS = {
    "attend_second_kernel": 8,
    "feed_back_second_kernel": 9,
    "feed_back_first_kernel": 11,
}


def run(kernel, scalars, arrays, outs, scratch, *fixed):
    name = kernel.__name__
    flat = [part for a in arrays for part in (a if isinstance(a, tuple) else (a,))]

    def grouped(*refs):
        refs = list(refs)
        ins = [refs.pop(0) for _ in scalars]
        for a in arrays:
            parts = [refs.pop(0) for _ in (a if isinstance(a, tuple) else (a,))]
            ins.append(Rows(*parts) if isinstance(a, tuple) else parts[0])
        kernel(*fixed, *ins, *refs)

    return pl.pallas_call(
        grouped,
        out_shape=list(outs),
        in_specs=[SCALARS] * len(scalars) + [LOCAL] * len(flat),
        out_specs=[LOCAL] * len(outs),
        scratch_shapes=scratch,
        compiler_params=pltpu.CompilerParams(vmem_limit_bytes=LIMITS.get(name, 6) * 2**20),
        cost_estimate=COST,
        name=name,
    )(*scalars, *flat)


WIDE = (D, 1152)


def attend_outs(docs):
    rows = DOC * len(docs)
    return [sds(rows, 1152), sds(len(docs), 3, DOC, 2 * DOC), sds(rows, PIECE), sds(rows, D)]


def stats(docs):
    return sds(DOC * len(docs), 128, dtype=F32)


def attend_first(ids, own, other, weights):
    docs = GROUPS[0]
    outs = [sds(ROWS, D), sds(*WIDE), sds(PIECE, D)] + attend_outs(docs)
    x, wide, proj, *one = pl.pallas_call(
        functools.partial(attend_first_kernel, docs),
        out_shape=outs,
        in_specs=[SCALARS, LOCAL] + [DISTANT] * 3,
        out_specs=[LOCAL] * len(outs),
        scratch_shapes=[pltpu.SemaphoreType.DMA((5,))],
        compiler_params=pltpu.CompilerParams(vmem_limit_bytes=44 * 2**20),
        cost_estimate=COST,
        name="attend_first_kernel",
    )(ids, other, own, weights[0], weights[1])
    docs = GROUPS[1]
    two = run(attend_more_kernel, [ids], [x, wide, proj], attend_outs(docs), [], docs)
    return x, *zip(one, two)


def attend_second(ids, first, mine, theirs, vec, own, other, weights):
    results, wide = [], weights[0]
    for g, docs in enumerate(GROUPS):
        rows = DOC * len(docs)
        outs = [sds(rows, D), sds(rows, D), stats(docs), sds(rows, D)] + attend_outs(docs)
        made = run(
            attend_second_kernel, [ids],
            [first[g], mine[g], theirs[g], vec, own, other, wide, weights[1]],
            outs + ([sds(*WIDE)] if g == 0 else []), [pltpu.VMEM((ROWS, D), BF16)], docs, 2,
        )
        if g == 0:
            *made, wide = made
        results.append(made)
    return tuple(zip(*results))


def feed(base, x, mine, theirs, vec, weights):
    results = []
    for g, docs in enumerate(GROUPS):
        rows = DOC * len(docs)
        split_x = isinstance(x, tuple)
        results.append(run(
            feed_kernel, [],
            [x[g] if split_x else x, mine[g], theirs[g], vec, weights[2], weights[3]],
            [sds(rows, D, dtype=F32), sds(rows, D), sds(rows, D), stats(docs),
             sds(rows, HIDDEN), sds(rows, HIDDEN), sds(rows, D)],
            [], docs, 0 if split_x else docs[0], base,
        ))
    return tuple(zip(*results))


FEED_BACK_OUTS = [
    sds(ROWS, D, dtype=F32), sds(ROWS, D), sds(8, D, dtype=F32), sds(ROWS, HIDDEN), sds(ROWS, D),
]


def feed_back_second(ids, first, mine, theirs, vec, own, other, slope, weights):
    return run(
        feed_back_second_kernel, [ids],
        [first, mine, theirs, vec, own, other, slope, weights[2], weights[3]],
        [sds(HALF, D)] + FEED_BACK_OUTS,
        [pltpu.VMEM((ROWS, D), BF16), pltpu.VMEM((ROWS, D), BF16)], 6,
    )


def feed_back_first(ids, normed, inv, vec, own, other, resid, mine, theirs, slope, weights):
    return run(
        feed_back_first_kernel, [ids],
        [normed, inv, vec, own, other, resid, mine, theirs, slope, weights[2], weights[3]],
        [sds(HALF, D, dtype=F32)] + FEED_BACK_OUTS,
        [pltpu.VMEM((ROWS, D), BF16), pltpu.VMEM((ROWS, D), F32)], 2,
    )


def attend_back(base, ids, gs, mine, theirs, normed, inv, qkv, prob, vec, weights):
    return run(
        attend_back_kernel, [ids],
        [gs, mine, theirs, normed, inv, vec, qkv, prob, weights[0], weights[1]],
        [sds(ROWS, D, dtype=F32), sds(ROWS, D), sds(8, D, dtype=F32), sds(ROWS, 1152), sds(ROWS, D),
         sds(HALF if base == 0 else 16, D)],
        [pltpu.VMEM((ROWS, PIECE), BF16), pltpu.VMEM(WIDE, BF16)], base,
    )


SPLIT_OUTS = [sds(32, *BLOCK), sds(32, *BLOCK)]
BLOCKS = pltpu.VMEM((4, 2, 8) + BLOCK, BF16)


def out_grad(chunk, ids, act, gs_low):
    return run(out_grad_kernel, [ids], [act, gs_low], SPLIT_OUTS, [BLOCKS], chunk)


def in_grad(chunk, ids, low, grad_pre):
    return run(in_grad_kernel, [ids], [low, grad_pre], SPLIT_OUTS, [BLOCKS], chunk)


def attend_grad(chunk, ids, x, grad_qkv, ctx, low, norms=()):
    outs = SPLIT_OUTS
    if norms:
        outs = [sds(33, *BLOCK), sds(32, *BLOCK), sds(8, D, dtype=F32)]
    return run(
        attend_grad_kernel, [ids], [x, grad_qkv, ctx, low, *norms], outs, [BLOCKS], chunk
    )


def vectors(rows):
    return run(vectors_kernel, [], rows, [sds(8, D, dtype=F32)], [])[0]


def split(sources, norm=None):
    arrays = [a for pair in sources for a in pair]
    sizes = tuple(keep.shape[0] // 2 for keep, _ in sources)
    count = sum(sizes)
    outs = [sds(count + (norm is not None), *BLOCK), sds(count, *BLOCK)]
    if norm is not None:
        arrays, outs = arrays + [norm], outs + [sds(8, D, dtype=F32)]
    return run(split_kernel, [], arrays, outs, [], sizes, int(norm is not None))


def far_add(keep, got, norm=None):
    if norm is None:
        return run(far_kernel, [], [keep, got], [sds(*keep.shape)], [], 0)
    count = keep.shape[0] - keep.shape[0] % 8
    outs = [sds(count + 1, *BLOCK), sds(8, D, dtype=F32)]
    return run(far_kernel, [], [keep, got, norm], outs, [], 1)


def join(held, got, count=1):
    size = held.shape[0] // count
    return run(join_kernel, [], [held, got], [sds(2 * size, *BLOCK)] * count, [], count)


PLACED = [
    sds(HIDDEN, D, dtype=F32),
    sds(D, HIDDEN, dtype=F32),
    sds(3, D, PIECE, dtype=F32),
    sds(PIECE, D, dtype=F32),
]


def place(ids, items, values, into=()):
    return pl.pallas_call(
        functools.partial(place_kernel, tuple(items)),
        out_shape=PLACED,
        in_specs=[SCALARS] + [LOCAL] * len(values) + [REMOTE] * len(into),
        out_specs=[REMOTE] * 4,
        scratch_shapes=[pltpu.VMEM((6, PIECE, PIECE), F32), pltpu.SemaphoreType.DMA((6,))],
        input_output_aliases={1 + len(values) + i: i for i in range(len(into))},
        compiler_params=pltpu.CompilerParams(vmem_limit_bytes=6 * 2**20),
        cost_estimate=COST,
        name="place_kernel",
    )(ids, *values, *into)


def swap(value):
    if isinstance(value, tuple):
        one, two = [swap(part) for part in value]
        return lax.optimization_barrier((one, value[1]))[0], two
    return lax.ppermute(value, "tensor", SWAP)


def flip(chip, core, stage, axis):
    pos = [chip % 4, chip // 4 % 4, chip // 16]
    low = (core == 0) == (stage == 0)
    pos[axis] = pos[axis] ^ 1 if low else 3 - pos[axis]
    return pos[0] + 4 * pos[1] + 16 * pos[2]


def exchange(value, stage, axis):
    pairs = [
        (2 * chip + core, 2 * flip(chip, core, stage, axis) + core)
        for chip in range(64)
        for core in range(2)
    ]
    return lax.ppermute(value, ("dp", "tensor"), pairs)


class Order:
    def __init__(self):
        self.token = None

    def hold(self, value):
        if self.token is None:
            return value
        return lax.optimization_barrier((value, self.token))[0]


class Single:
    def __init__(self, order, axes, send, keep, norm=None):
        self.order, self.axes, self.keep, self.norm, self.round = order, axes, keep, norm, 0
        self.send(send, 0, 0)

    def send(self, value, stage, j):
        self.order.token = value
        self.got = exchange(value, stage, self.axes[j % 3])

    def next(self):
        self.round += 1
        got = self.order.hold(self.got)
        if self.round > 8:
            self.got = self.order.token = got
            return
        if self.round < 3:
            value, self.keep, *norm = split([(self.keep, got)], self.norm)
            self.send(value, 0, self.round)
        elif self.round < 6:
            self.keep, *norm = far_add(self.keep, got, self.norm)
            self.send(self.keep, 1, self.round)
        elif self.round == 6:
            self.keep, *norm = far_add(self.keep, got, self.norm)
            if norm:
                self.keep = self.keep[:8]
            self.send(self.keep, 0, 2)
        else:
            norm = ()
            self.keep = join(self.keep, got)[0]
            self.send(self.keep, 0, 8 - self.round)
        if norm:
            self.norm = norm[0]


class Pair:
    def __init__(self, order, axes):
        self.order, self.axes = order, axes
        self.keep, self.got, self.calls = [None, None], [None, None], [0, 0]
        self.both = 2

    def start(self, i, send, keep):
        self.keep[i] = keep
        self.send(i, send, 0)

    def send(self, i, value, j):
        self.order.token = value
        self.got[i] = exchange(value, 0, self.axes[i ^ j])

    def next(self, i):
        self.calls[i] += 1
        if self.calls[i] == 1:
            value, self.keep[i] = split([(self.keep[i], self.order.hold(self.got[i]))])
            self.send(i, value, 1)
        elif self.calls[i] == 2 and self.calls[1 - i] == 2:
            got = [self.order.hold(g) for g in self.got]
            value, self.held = split([(self.keep[0], got[0]), (self.keep[1], got[1])])
            self.order.token = value
            self.arrived = exchange(value, 0, self.axes[2])
        elif self.calls[i] == 3:
            self.keep[i] = join(self.keep[i], self.order.hold(self.got[i]))[0]
            self.send(i, self.keep[i], 0)
        elif self.calls[i] == 4:
            self.got[i] = self.order.token = self.order.hold(self.got[i])

    def next_both(self):
        got = self.order.hold(self.arrived)
        self.both += 1
        if self.both <= 6:
            self.held = far_add(self.held, got)[0]
            self.order.token = self.held
            if self.both < 6:
                self.arrived = exchange(self.held, 1, self.axes[self.both - 3])
            else:
                self.arrived = exchange(self.held, 0, self.axes[2])
        else:
            self.keep = list(join(self.held, got, 2))
            for i in range(2):
                self.send(i, self.keep[i], 1)


UPPER_PAIR, UPPER_LAST = (0, 1, 2), (2, 1, 0)
LOWER_PAIR, LOWER_LAST = (0, 1, 2), (2, 0, 1)
CHUNK_AXES = [
    UPPER_PAIR,
    (UPPER_PAIR[1], UPPER_PAIR[0], UPPER_PAIR[2]),
    UPPER_LAST,
    LOWER_PAIR,
    (LOWER_PAIR[1], LOWER_PAIR[0], LOWER_PAIR[2]),
    LOWER_LAST,
]
TAIL = (
    "Lp", "Lq", "Ub", "Um", "Lp", "Lb", "Lq", "Ub", "Um", "Lb", "Lm", "Ub", "Lb",
    "Um", "Lm", "Lb", "Ub", "Um", "Lb", "Lm", "Ub", "Up", "Lb", "Ub", "Lm", "Uq",
    "Lb", "Ub", "Up", "Lm", "Lb", "Uq", "Lq", "Ub", "Lp",
)


def device_table():
    rows = []
    for chip in range(64):
        pos = [chip % 4, chip // 4 % 4, chip // 16]
        low = [(p ^ (p >> 1)) & 1 for p in pos]
        high = [p >> 1 for p in pos]
        for core in range(2):
            near = low if core == 0 else high
            row = [core]
            for axes in CHUNK_AXES:
                row += [near[axis] for axis in axes] + [0]
            rows.append(row + [0] * 7)
    return np.array(rows, np.int32)


def on_device(
    tokens,
    skip_tokens,
    cot_back,
    cot_head,
    one_span,
    *params,
):
    lower = [params[i] for i in (0, 1, 4, 5)]
    upper = [params[i] for i in (8, 9, 12, 13)]
    device = lax.axis_index("dp") * 2 + lax.axis_index("tensor")
    row = lax.dynamic_index_in_dim(jnp.asarray(device_table()), device, 0, keepdims=False)
    ids = jnp.concatenate([row, one_span])
    tokens_other = swap(tokens)
    tokens, ids = lax.optimization_barrier((tokens, ids))
    vec = vectors([params[i] for i in (2, 3, 6, 7, 10, 11, 14, 15)])
    skip_other = swap(skip_tokens)
    cot_head_other = swap(cot_head)
    cot_back_other = swap(cot_back)
    order = Order()

    x_l, qkv_l, prob_l, ctx_l, part = attend_first(ids, tokens, tokens_other, lower)
    first_l, low_l, normed_al, inv_al, act_l, slope_l, part = feed(
        0, x_l, part, swap(part), vec, lower
    )
    x_u, normed_fl, inv_fl, backs, qkv_u, prob_u, ctx_u, part = attend_second(
        ids, first_l, part, swap(part), vec, skip_tokens, skip_other, upper
    )
    first_u, low_u, normed_au, inv_au, act_u, slope_u, part = feed(
        4, x_u, part, swap(part), vec, upper
    )
    head_out, gs_u, gs_low_u, norms_fu, grad_pre_u, part = feed_back_second(
        ids, first_u, part, swap(part), vec, cot_head, cot_head_other, slope_u, upper
    )
    pair_u, pair_l = Pair(order, UPPER_PAIR), Pair(order, LOWER_PAIR)
    theirs = swap(part)
    pair_u.start(0, *out_grad(0, ids, act_u, gs_low_u))
    pair_u.start(1, *in_grad(1, ids, low_u, order.hold(grad_pre_u)))
    resid_u, gr_low_u, norms_au, grad_qkv_u, part, _ = attend_back(
        4, ids, order.hold(gs_u), part, theirs, normed_au, inv_au, qkv_u, prob_u, vec=vec,
        weights=upper,
    )
    theirs = swap(part)
    at_u = Single(
        order, UPPER_LAST, *attend_grad(2, ids, x_u, grad_qkv_u, ctx_u, order.hold(gr_low_u))
    )
    pair_u.next(0)
    pair_u.next(1)
    grad_skip, gs_l, gs_low_l, norms_fl, grad_pre_l, part = feed_back_first(
        ids, normed_fl, inv_fl, vec, cot_back, cot_back_other, order.hold(resid_u), part,
        theirs, slope_l, lower,
    )
    theirs = swap(part)
    order.token = gs_low_l
    pair_u.next(0)
    pair_u.next(1)
    pair_l.start(0, *out_grad(3, ids, act_l, order.hold(gs_low_l)))
    pair_l.start(1, *in_grad(4, ids, low_l, order.hold(grad_pre_l)))
    at_u.next()
    pair_u.next_both()
    resid_l, gr_low_l, norms_al, grad_qkv_l, part, away = attend_back(
        0, ids, order.hold(gs_l), part, theirs, normed_al, inv_al, qkv_l, prob_l, vec=vec,
        weights=lower,
    )
    at_l = Single(
        order, LOWER_LAST,
        *attend_grad(
            5, ids, x_l, grad_qkv_l, ctx_l, gr_low_l, (norms_al, norms_fl, norms_au, norms_fu)
        ),
    )
    act = {
        "Up": lambda: pair_u.next(0),
        "Uq": lambda: pair_u.next(1),
        "Um": pair_u.next_both,
        "Ub": at_u.next,
        "Lp": lambda: pair_l.next(0),
        "Lq": lambda: pair_l.next(1),
        "Lm": pair_l.next_both,
        "Lb": at_l.next,
    }
    away = swap(order.hold(away))
    for index, name in enumerate(TAIL):
        act[name]()
        if index == 1:
            grad_tokens, back_out = run(
                rows_kernel, [ids], [resid_l, part, order.hold(away), backs],
                [sds(HALF, D, dtype=F32), sds(HALF, D)], [pltpu.VMEM((ROWS, D), BF16)],
            )
            order.token = grad_tokens
    done_u = place(
        ids,
        [(0, 0), (0, 1), (1, 0), (1, 1), (2, 0), (2, 1)],
        [pair_u.keep[0], pair_u.got[0], pair_u.keep[1], pair_u.got[1], at_u.keep,
         order.hold(at_u.got)],
    )
    order.token = done_u[0]
    done_l = place(
        ids, [(3, 0), (4, 0), (5, 0)],
        [pair_l.keep[0], pair_l.keep[1], order.hold(at_l.keep)],
    )
    for chunk, got in ((5, at_l.got), (4, pair_l.got[1]), (3, pair_l.got[0])):
        done_l = place(ids, [(chunk, 1)], [got], done_l)
    norms = at_l.norm
    out_gu, in_gu, qkv_gu, proj_gu = done_u
    out_gl, in_gl, qkv_gl, proj_gl = done_l
    return (
        back_out,
        head_out,
        grad_tokens,
        grad_skip,
        qkv_gl,
        proj_gl,
        norms[0],
        norms[1],
        in_gl,
        out_gl,
        norms[2],
        norms[3],
        qkv_gu,
        proj_gu,
        norms[4],
        norms[5],
        in_gu,
        out_gu,
        norms[6],
        norms[7],
    )


def solution(mesh):
    rows = P(("dp", "tensor"), None)
    weights = (
        P(None, None, "tensor"),
        P("tensor", None),
        P(),
        P(),
        P(None, "tensor"),
        P("tensor", None),
        P(),
        P(),
    )
    return jax.shard_map(
        on_device,
        mesh=mesh,
        in_specs=(rows,) * 4 + (P("dp"),) + weights + weights,
        out_specs=(rows,) * 4 + weights + weights,
        check_vma=False,
    )
```

```python
import functools

import jax
import jax.numpy as jnp
import numpy as np
from jax import lax
from jax.experimental import pallas as pl
from jax.experimental.pallas import tpu as pltpu
from jax.sharding import PartitionSpec as P

SPAN = 128
EPS = 1e-06
SCALE = 0.125
NEG = -1000000000.0

D = 768
ROWS = 768
HALF = ROWS // 2
HIDDEN = 1536
PIECE = 384
PAIR = 128
BLOCK = (48, 384)
F32 = jnp.float32
BF16 = jnp.bfloat16
SPANS_AT = 32

SWAP = [(0, 1), (1, 0)]


def dot_nn(left, right):
    return lax.dot_general(left, right, (((1,), (0,)), ((), ())), preferred_element_type=F32)


def dot_nt(left, right):
    return lax.dot_general(left, right, (((1,), (1,)), ((), ())), preferred_element_type=F32)


def dot_tn(left, right):
    return lax.dot_general(left, right, (((0,), (0,)), ((), ())), preferred_element_type=F32)


def normalize(resid):
    mean = jnp.mean(resid, axis=-1, keepdims=True)
    centered = resid - mean
    var = jnp.mean(centered * centered, axis=-1, keepdims=True)
    inv = lax.rsqrt(var + EPS)
    return centered * inv, inv


def norm_grad(grad_out, normed, inv, gain):
    grad = grad_out * gain
    first = jnp.mean(grad, axis=-1, keepdims=True)
    second = jnp.mean(grad * normed, axis=-1, keepdims=True)
    return inv * (grad - first - normed * second)


def fold(value):
    return jnp.sum(value.reshape(-1, 8, value.shape[-1]), axis=0)

DOC = 2 * SPAN
DOCS = ROWS // DOC


def doc_rows(doc):
    return slice(doc * DOC, (doc + 1) * DOC)


def half_rows(index):
    return pl.ds(pl.multiple_of(index * HALF, HALF), HALF)


def join_halves(side, own_ref, other_ref, full_ref):
    full_ref[half_rows(side), :] = own_ref[...]
    full_ref[half_rows(1 - side), :] = other_ref[...]


def doc_masks(ids_ref, doc):
    row = lax.broadcasted_iota(jnp.int32, (DOC, 1), 0)
    keep = jnp.where((row < SPAN) | (ids_ref[SPANS_AT + doc] == 0), 1.0, 0.0)
    return keep, (row & (SPAN - 1)) == 0


def spread(column):
    return jnp.broadcast_to(column, (column.shape[0], 128))


def head_masks():
    lane = lax.broadcasted_iota(jnp.int32, (1, PAIR), 1)
    return lane < 64


def both_heads(value, left):
    zero = jnp.zeros_like(value)
    return jnp.concatenate([jnp.where(left, value, zero), jnp.where(left, zero, value)], axis=0)


class Rows:
    def __init__(self, *refs):
        self.refs = refs

    def find(self, index):
        head = index[0] if isinstance(index, tuple) else index
        rest = index[1:] if isinstance(index, tuple) else ()
        at = head if isinstance(head, int) else head.start
        base = 0
        for ref in self.refs:
            if at < base + ref.shape[0]:
                break
            base += ref.shape[0]
        head = head - base if isinstance(head, int) else slice(at - base, head.stop - base)
        return ref, (head, *rest)

    def __getitem__(self, index):
        head = index[0] if isinstance(index, tuple) else index
        if head is Ellipsis or head == slice(None):
            return jnp.concatenate([ref[index] for ref in self.refs], axis=0)
        ref, index = self.find(index)
        return ref[index]


GROUPS = ((0, 1), (2,))


def attend(ids_ref, docs, x_ref, proj_ref, qkv_ref, prob_ref, ctx_ref, part_ref, wide, skip=0):
    for i, doc in enumerate(docs):
        at = doc_rows(i)
        out = dot_nn(x_ref[doc_rows(i + skip), :], wide[...])
        qkv_ref[at, :384] = (out[:, :384] * SCALE).astype(BF16)
        qkv_ref[at, 384:] = out[:, 384:].astype(BF16)
    left = head_masks()
    col = lax.broadcasted_iota(jnp.int32, (1, 2 * DOC), 1) & (DOC - 1)
    for i, doc in enumerate(docs):
        at = doc_rows(i)
        key_ok = (col < SPAN) | (ids_ref[SPANS_AT + doc] == 0)
        scores = []
        for pair in range(3):
            query = qkv_ref[at, pair * PAIR:(pair + 1) * PAIR]
            keys = qkv_ref[at, 384 + pair * PAIR:384 + (pair + 1) * PAIR]
            scores.append(jnp.where(key_ok, dot_nt(query, both_heads(keys, left)), NEG))
        for pair in range(3):
            probs = []
            for head in range(2):
                score = scores[pair][:, head * DOC:(head + 1) * DOC]
                raised = jnp.exp(score - jnp.max(score, axis=-1, keepdims=True))
                probs.append(
                    (raised * (1.0 / jnp.sum(raised, axis=-1, keepdims=True))).astype(BF16)
                )
            prob = jnp.concatenate(probs, axis=1)
            prob_ref[i, pair] = prob
            values = qkv_ref[at, 768 + pair * PAIR:768 + (pair + 1) * PAIR]
            mixed = dot_nn(prob, both_heads(values, left))
            ctx_ref[at, pair * PAIR:(pair + 1) * PAIR] = mixed.astype(BF16)
    for i, doc in enumerate(docs):
        at = doc_rows(i)
        part_ref[at, :] = dot_nn(ctx_ref[at, :], proj_ref[...]).astype(BF16)


def attend_first_kernel(
    docs, ids_ref, other_ref, own_ref, qkv_w_ref, proj_w_ref,
    x_ref, wide, proj, qkv_ref, prob_ref, ctx_ref, part_ref, sems,
):
    side = ids_ref[0]
    copies = [pltpu.make_async_copy(own_ref, x_ref.at[half_rows(side), :], sems.at[0])]
    for index in range(3):
        cut = slice(index * 384, (index + 1) * 384)
        copies.append(
            pltpu.make_async_copy(qkv_w_ref.at[index], wide.at[:, cut], sems.at[1 + index])
        )
    copies.append(pltpu.make_async_copy(proj_w_ref, proj, sems.at[4]))
    for copy in copies:
        copy.start()
    x_ref[half_rows(1 - side), :] = other_ref[...]
    for copy in copies:
        copy.wait()
    attend(ids_ref, docs, x_ref, proj, qkv_ref, prob_ref, ctx_ref, part_ref, wide)


def attend_more_kernel(
    docs, ids_ref, x_ref, wide_ref, proj_ref, qkv_ref, prob_ref, ctx_ref, part_ref,
):
    attend(
        ids_ref, docs, x_ref, proj_ref, qkv_ref, prob_ref, ctx_ref, part_ref, wide_ref, docs[0]
    )


def attend_second_kernel(
    docs, base, ids_ref, first_ref, mine_ref, theirs_ref, vec_ref, own_ref, other_ref,
    qkv_w_ref, proj_ref,
    x_ref, normed_ref, inv_ref, back_ref, qkv_ref, prob_ref, ctx_ref, part_ref, *rest,
):
    *wide_out, full = rest
    join_halves(ids_ref[0], own_ref, other_ref, full)
    for i, doc in enumerate(docs):
        at = doc_rows(i)
        keep, cls = doc_masks(ids_ref, doc)
        resid = first_ref[at, :] + mine_ref[at, :].astype(F32) + theirs_ref[at, :].astype(F32)
        normed, inv = normalize(resid)
        back = normed * vec_ref[base:base + 1, :] + vec_ref[base + 1:base + 2, :]
        normed_ref[at, :] = normed.astype(BF16)
        inv_ref[at, :] = spread(inv)
        x_ref[at, :] = jnp.where(cls, back, full[doc_rows(doc), :].astype(F32)).astype(BF16)
        back_ref[at, :] = (back * keep).astype(BF16)
    wide = qkv_w_ref
    if wide_out:
        wide = wide_out[0]
        for index in range(3):
            wide[:, index * 384:(index + 1) * 384] = qkv_w_ref[index]
    attend(ids_ref, docs, x_ref, proj_ref, qkv_ref, prob_ref, ctx_ref, part_ref, wide)


def feed_kernel(
    docs, skip, base, x_ref, mine_ref, theirs_ref, vec_ref, in_ref, out_w_ref,
    first_ref, low_ref, normed_ref, inv_ref, act_ref, slope_ref, part_ref,
):
    for i, doc in enumerate(docs):
        at = doc_rows(i)
        resid = x_ref[doc_rows(i + skip), :].astype(F32) + mine_ref[at, :].astype(F32)
        resid = resid + theirs_ref[at, :].astype(F32)
        normed, inv = normalize(resid)
        first = normed * vec_ref[base:base + 1, :] + vec_ref[base + 1:base + 2, :]
        normed_ref[at, :] = normed.astype(BF16)
        inv_ref[at, :] = spread(inv)
        first_ref[at, :] = first
        low_ref[at, :] = first.astype(BF16)
    for i, doc in enumerate(docs):
        at = doc_rows(i)
        for piece in range(3):
            cut = slice(piece * 512, (piece + 1) * 512)
            pre = dot_nn(low_ref[at, :], in_ref[:, cut])
            share = 0.5 * (1.0 + lax.erf(pre * 0.7071067811865476))
            density = jnp.exp(-0.5 * pre * pre) * 0.3989422804014327
            act_ref[at, cut] = (pre * share).astype(BF16)
            slope_ref[at, cut] = (share + pre * density).astype(BF16)
    for i, doc in enumerate(docs):
        at = doc_rows(i)
        part_ref[at, :] = dot_nn(act_ref[at, :], out_w_ref[...]).astype(BF16)


def feed_back(gs_low_ref, slope_ref, in_ref, out_w_ref, grad_pre_ref, part_ref):
    for doc in range(DOCS):
        at = doc_rows(doc)
        for piece in range(3):
            cut = slice(piece * 512, (piece + 1) * 512)
            grad_act = dot_nt(gs_low_ref[at, :], out_w_ref[cut, :])
            grad_pre_ref[at, cut] = (grad_act * slope_ref[at, cut].astype(F32)).astype(BF16)
    for doc in range(DOCS):
        at = doc_rows(doc)
        part_ref[at, :] = dot_nt(grad_pre_ref[at, :], in_ref[...]).astype(BF16)


def put_norm_grads(norms_ref, sums):
    gain, shift = sums
    norms_ref[...] = jnp.zeros_like(norms_ref)
    norms_ref[0:1, :] = jnp.sum(gain, axis=0, keepdims=True)
    norms_ref[1:2, :] = jnp.sum(shift, axis=0, keepdims=True)


def add_sums(sums, grad_out, normed):
    new = (fold(grad_out * normed), fold(grad_out))
    return new if sums is None else (sums[0] + new[0], sums[1] + new[1])


def feed_back_second_kernel(
    base, ids_ref, first_ref, mine_ref, theirs_ref, vec_ref, own_ref, other_ref,
    slope_ref, in_ref, out_w_ref,
    head_ref, gs_ref, gs_low_ref, norms_ref, grad_pre_ref, part_ref, cot, full,
):
    side = ids_ref[0]
    join_halves(side, own_ref, other_ref, cot)
    sums = None
    for doc in range(DOCS):
        at = doc_rows(doc)
        keep, _ = doc_masks(ids_ref, doc)
        resid = first_ref[at, :] + mine_ref[at, :].astype(F32) + theirs_ref[at, :].astype(F32)
        normed, inv = normalize(resid)
        head = normed * vec_ref[base:base + 1, :] + vec_ref[base + 1:base + 2, :]
        full[at, :] = (head * keep).astype(BF16)
        grad_out = cot[at, :].astype(F32) * keep
        grad = norm_grad(grad_out, normed, inv, vec_ref[base:base + 1, :])
        gs_ref[at, :] = grad
        gs_low_ref[at, :] = grad.astype(BF16)
        sums = add_sums(sums, grad_out, normed)
    head_ref[...] = full[half_rows(side), :]
    put_norm_grads(norms_ref, sums)
    feed_back(gs_low_ref, slope_ref, in_ref, out_w_ref, grad_pre_ref, part_ref)


def feed_back_first_kernel(
    base, ids_ref, normed_ref, inv_ref, vec_ref, own_ref, other_ref,
    resid_ref, mine_ref, theirs_ref, slope_ref, in_ref, out_w_ref,
    skip_ref, gs_ref, gs_low_ref, norms_ref, grad_pre_ref, part_ref, cot, full,
):
    side = ids_ref[0]
    join_halves(side, own_ref, other_ref, cot)
    sums = None
    for doc in range(DOCS):
        at = doc_rows(doc)
        keep, cls = doc_masks(ids_ref, doc)
        above = resid_ref[at, :] + mine_ref[at, :].astype(F32) + theirs_ref[at, :].astype(F32)
        full[at, :] = jnp.where(cls, 0.0, above)
        normed = normed_ref[at, :].astype(F32)
        grad_out = cot[at, :].astype(F32) * keep + jnp.where(cls, above, 0.0)
        grad = norm_grad(grad_out, normed, inv_ref[at, 0:1], vec_ref[base:base + 1, :])
        gs_ref[at, :] = grad
        gs_low_ref[at, :] = grad.astype(BF16)
        sums = add_sums(sums, grad_out, normed)
    skip_ref[...] = full[half_rows(side), :]
    put_norm_grads(norms_ref, sums)
    feed_back(gs_low_ref, slope_ref, in_ref, out_w_ref, grad_pre_ref, part_ref)


def attend_back_kernel(
    base, ids_ref, gs_ref, mine_ref, theirs_ref, normed_ref, inv_ref, vec_ref, qkv_ref, prob_ref,
    qkv_w_ref, proj_ref,
    resid_ref, low_ref, norms_ref, grad_qkv_ref, part_ref, away_ref, grad_ctx, wide,
):
    for index in range(3):
        wide[:, index * 384:(index + 1) * 384] = qkv_w_ref[index]
    sums = None
    for doc in range(DOCS):
        at = doc_rows(doc)
        grad_out = gs_ref[at, :] + mine_ref[at, :].astype(F32) + theirs_ref[at, :].astype(F32)
        normed = normed_ref[at, :].astype(F32)
        grad = norm_grad(grad_out, normed, inv_ref[at, 0:1], vec_ref[base:base + 1, :])
        resid_ref[at, :] = grad
        low_ref[at, :] = grad.astype(BF16)
        sums = add_sums(sums, grad_out, normed)
    put_norm_grads(norms_ref, sums)
    for doc in range(DOCS):
        at = doc_rows(doc)
        grad_ctx[at, :] = dot_nt(low_ref[at, :], proj_ref[...]).astype(BF16)
    left = head_masks()
    for doc in range(DOCS):
        at = doc_rows(doc)
        pairs = [slice(pair * PAIR, (pair + 1) * PAIR) for pair in range(3)]
        grad_probs = []
        for pair in range(3):
            values = qkv_ref[at, 768 + pair * PAIR:768 + (pair + 1) * PAIR]
            grad_probs.append(dot_nt(grad_ctx[at, pairs[pair]], both_heads(values, left)))
        for pair in range(3):
            prob_low = prob_ref[doc, pair]
            scored = []
            for head in range(2):
                cut = slice(head * DOC, (head + 1) * DOC)
                prob = prob_low[:, cut].astype(F32)
                grad_prob = grad_probs[pair][:, cut]
                inner = jnp.sum(grad_prob * prob, axis=-1, keepdims=True)
                scored.append((prob * (grad_prob - inner)).astype(BF16))
            grad_scores = jnp.concatenate(scored, axis=1)
            query = qkv_ref[at, pairs[pair]]
            keys = qkv_ref[at, 384 + pair * PAIR:384 + (pair + 1) * PAIR]
            grad_query = dot_nn(grad_scores, both_heads(keys, left)) * SCALE
            grad_keys = dot_tn(grad_scores, query)
            grad_values = dot_tn(prob_low, grad_ctx[at, pairs[pair]])
            grad_qkv_ref[at, pair * PAIR:(pair + 1) * PAIR] = grad_query.astype(BF16)
            for index, grad in ((1, grad_keys), (2, grad_values)):
                cut = slice(index * 384 + pair * PAIR, index * 384 + (pair + 1) * PAIR)
                grad_qkv_ref[at, cut] = jnp.where(left, grad[:DOC], grad[DOC:]).astype(BF16)
    for doc in range(DOCS):
        at = doc_rows(doc)
        part_ref[at, :] = dot_nt(grad_qkv_ref[at, :], wide[...]).astype(BF16)
    if base == 0:
        away_ref[...] = part_ref[half_rows(1 - ids_ref[0]), :]
    else:
        away_ref[...] = jnp.zeros_like(away_ref)


def rows_kernel(ids_ref, resid_ref, mine_ref, theirs_ref, back_ref, out_ref, back_out_ref, full):
    at = half_rows(ids_ref[0])
    out_ref[...] = resid_ref[at, :] + mine_ref[at, :].astype(F32) + theirs_ref[...].astype(F32)
    full[...] = back_ref[...]
    back_out_ref[...] = full[at, :]


def cut_wide(value, blocks, piece):
    for half in range(2):
        for k in range(8):
            blocks[piece, half, k] = value[k * 48:(k + 1) * 48, half * 384:(half + 1) * 384]


def cut_tall(value, blocks, piece):
    for half in range(2):
        for k in range(8):
            at = half * 384 + k * 48
            blocks[piece, half, k] = value[at:at + 48, :]


def put_blocks(ids_ref, turn, blocks, send_ref, keep_ref):
    first, second, third, outer = [ids_ref[1 + 4 * turn + i] for i in range(4)]
    for rel, ref in ((1, send_ref), (0, keep_ref)):
        for b in range(2):
            piece = 2 * (rel ^ first) + (b ^ second)
            for e in range(2):
                for k in range(8):
                    ref[16 * b + 8 * e + k] = blocks[piece, e ^ third, k ^ outer]


def out_grad_kernel(turn, ids_ref, act_ref, gs_ref, send_ref, keep_ref, blocks):
    for p in range(2):
        value = dot_tn(act_ref[:, p * 768:(p + 1) * 768], gs_ref[...]).astype(BF16)
        cut_wide(value[:384], blocks, 2 * p)
        cut_wide(value[384:], blocks, 2 * p + 1)
    put_blocks(ids_ref, turn, blocks, send_ref, keep_ref)


def in_grad_kernel(turn, ids_ref, low_ref, grad_ref, send_ref, keep_ref, blocks):
    for p in range(2):
        value = dot_tn(low_ref[...], grad_ref[:, p * 768:(p + 1) * 768]).astype(BF16)
        cut_tall(value[:, :384], blocks, 2 * p)
        cut_tall(value[:, 384:], blocks, 2 * p + 1)
    put_blocks(ids_ref, turn, blocks, send_ref, keep_ref)


def attend_grad_kernel(turn, ids_ref, x_ref, grad_ref, ctx_ref, low_ref, *refs):
    norm_refs, (send_ref, keep_ref), blocks = refs[:-3 - (len(refs) > 3)], refs[-3:-1], refs[-1]
    if norm_refs:
        send_ref, keep_ref = refs[-4:-2]
        value = jnp.concatenate([ref[0:2, :] for ref in norm_refs], axis=0)
        refs[-2][...] = value
        send_ref[32] = norm_block(value)
    value = dot_tn(x_ref[...], grad_ref[...]).astype(BF16)
    for piece in range(3):
        cut_tall(value[:, piece * 384:(piece + 1) * 384], blocks, piece)
    cut_wide(dot_tn(ctx_ref[...], low_ref[...]).astype(BF16), blocks, 3)
    put_blocks(ids_ref, turn, blocks, send_ref, keep_ref)


def vectors_kernel(*refs):
    out_ref = refs[-1]
    for i in range(8):
        out_ref[i:i + 1, :] = refs[i][...].reshape(1, D)


def plus(one, two):
    return (one.astype(F32) + two.astype(F32)).astype(BF16)


def norm_block(value):
    high = value.astype(BF16)
    low = (value - high.astype(F32)).astype(BF16)
    rows = [high[:, :PIECE], high[:, PIECE:], low[:, :PIECE], low[:, PIECE:]]
    return jnp.concatenate(rows + [jnp.zeros((16, PIECE), BF16)], axis=0)


def block_norm(block):
    high = jnp.concatenate([block[0:8], block[8:16]], axis=1)
    low = jnp.concatenate([block[16:24], block[24:32]], axis=1)
    return high.astype(F32) + low.astype(F32)


def add_norm(value, block):
    return block_norm(norm_block(value)) + block_norm(block)


def split_kernel(sizes, with_norm, *refs):
    count = len(sizes)
    ins, outs = refs[:2 * count], refs[2 * count + with_norm:]
    at = 0
    for i, m in enumerate(sizes):
        keep, got = ins[2 * i], ins[2 * i + 1]
        outs[1][at:at + m] = plus(keep[:m], got[:m])
        outs[0][at:at + m] = plus(keep[m:], got[m:2 * m])
        at += m
    if with_norm:
        value = add_norm(refs[2 * count][...], ins[1][2 * sizes[0]])
        outs[0][at] = norm_block(value)
        outs[2][...] = value


def far_kernel(with_norm, *refs):
    if with_norm:
        keep, got, norm, out, norm_out = refs
        count = keep.shape[0] - (keep.shape[0] % 8)
        value = add_norm(norm[...], got[got.shape[0] - 1])
        out[count] = norm_block(value)
        norm_out[...] = value
    else:
        keep, got, out = refs
        count = keep.shape[0]
    out[:count] = plus(keep[:count], got[:count])


def join_kernel(count, held_ref, got_ref, *outs):
    size = outs[0].shape[0] // 2
    for i in range(count):
        at = slice(i * size, (i + 1) * size)
        outs[i][:size] = held_ref[at]
        outs[i][size:] = got_ref[at]


def place_kernel(items, ids_ref, *refs):
    ins, outs, squares, sems = refs[:len(items)], refs[-6:-2], refs[-2], refs[-1]
    slots = squares.shape[0]

    def copies(index, chunk, far, b, e):
        first, second = ids_ref[1 + 4 * chunk], ids_ref[2 + 4 * chunk]
        turn = chunk % 3
        slot = index % slots
        piece = 2 * (far ^ first) + (b ^ second)
        at = pl.ds(pl.multiple_of(piece * PIECE, PIECE), PIECE)
        cut = slice(e * PIECE, (e + 1) * PIECE)

        def copy(ref):
            return pltpu.make_async_copy(squares.at[slot], ref, sems.at[slot])

        if turn == 0:
            return [(None, copy(outs[0].at[at, cut]))]
        if turn == 1:
            return [(None, copy(outs[1].at[cut, at]))]
        return [
            (piece < 3, copy(outs[2].at[jnp.minimum(piece, 2), cut, :])),
            (piece == 3, copy(outs[3].at[:, cut])),
        ]

    def each(pairs, wait):
        for when, copy in pairs:
            def act(copy=copy):
                copy.wait() if wait else copy.start()

            if when is None:
                act()
            else:
                pl.when(when)(act)

    flight = []
    for (chunk, far), from_ref in zip(items, ins):
        third, outer = ids_ref[3 + 4 * chunk], ids_ref[4 + 4 * chunk]
        for b in range(2):
            for e in range(2):
                index = len(flight)
                if index >= slots:
                    each(flight[index - slots], True)
                for k in range(8):
                    block = from_ref[16 * b + 8 * (e ^ third) + (k ^ outer)]
                    squares[index % slots, k * 48:(k + 1) * 48, :] = block.astype(F32)
                flight.append(copies(index, chunk, far, b, e))
                each(flight[index], False)
    for pairs in flight[-slots:]:
        each(pairs, True)


def sds(*shape, dtype=BF16):
    return jax.ShapeDtypeStruct(shape, dtype)


SCALARS = pl.BlockSpec(memory_space=pltpu.SMEM)
LOCAL = pl.BlockSpec(memory_space=pltpu.VMEM)
REMOTE = pl.BlockSpec(memory_space=pl.ANY)
DISTANT = pl.BlockSpec(memory_space=pltpu.HBM)


COST = pl.CostEstimate(flops=2_000_000_000, bytes_accessed=1, transcendentals=0)
HEAVY = pl.CostEstimate(flops=8_000_000_000, bytes_accessed=10_000_000, transcendentals=0)
LIGHT = ("split_kernel", "far_kernel", "join_kernel", "vectors_kernel", "rows_kernel")


LIMITS = {
    "attend_second_kernel": 8,
    "feed_back_second_kernel": 9,
    "feed_back_first_kernel": 11,
}


def run(kernel, scalars, arrays, outs, scratch, *fixed):
    name = kernel.__name__
    flat = [part for a in arrays for part in (a if isinstance(a, tuple) else (a,))]

    def grouped(*refs):
        refs = list(refs)
        ins = [refs.pop(0) for _ in scalars]
        for a in arrays:
            parts = [refs.pop(0) for _ in (a if isinstance(a, tuple) else (a,))]
            ins.append(Rows(*parts) if isinstance(a, tuple) else parts[0])
        kernel(*fixed, *ins, *refs)

    return pl.pallas_call(
        grouped,
        out_shape=list(outs),
        in_specs=[SCALARS] * len(scalars) + [LOCAL] * len(flat),
        out_specs=[LOCAL] * len(outs),
        scratch_shapes=scratch,
        compiler_params=pltpu.CompilerParams(vmem_limit_bytes=LIMITS.get(name, 6) * 2**20),
        cost_estimate=COST if name in LIGHT else HEAVY,
        name=name,
    )(*scalars, *flat)


WIDE = (D, 1152)


def attend_outs(docs):
    rows = DOC * len(docs)
    return [sds(rows, 1152), sds(len(docs), 3, DOC, 2 * DOC), sds(rows, PIECE), sds(rows, D)]


def stats(docs):
    return sds(DOC * len(docs), 128, dtype=F32)


def attend_first(ids, own, other, weights):
    docs = GROUPS[0]
    outs = [sds(ROWS, D), sds(*WIDE), sds(PIECE, D)] + attend_outs(docs)
    x, wide, proj, *one = pl.pallas_call(
        functools.partial(attend_first_kernel, docs),
        out_shape=outs,
        in_specs=[SCALARS, LOCAL] + [DISTANT] * 3,
        out_specs=[LOCAL] * len(outs),
        scratch_shapes=[pltpu.SemaphoreType.DMA((5,))],
        compiler_params=pltpu.CompilerParams(vmem_limit_bytes=44 * 2**20),
        cost_estimate=HEAVY,
        name="attend_first_kernel",
    )(ids, other, own, weights[0], weights[1])
    docs = GROUPS[1]
    two = run(attend_more_kernel, [ids], [x, wide, proj], attend_outs(docs), [], docs)
    return x, *zip(one, two)


def attend_second(ids, first, mine, theirs, vec, own, other, weights):
    results, wide = [], weights[0]
    for g, docs in enumerate(GROUPS):
        rows = DOC * len(docs)
        outs = [sds(rows, D), sds(rows, D), stats(docs), sds(rows, D)] + attend_outs(docs)
        made = run(
            attend_second_kernel, [ids],
            [first[g], mine[g], theirs[g], vec, own, other, wide, weights[1]],
            outs + ([sds(*WIDE)] if g == 0 else []), [pltpu.VMEM((ROWS, D), BF16)], docs, 2,
        )
        if g == 0:
            *made, wide = made
        results.append(made)
    return tuple(zip(*results))


def feed(base, x, mine, theirs, vec, weights):
    results = []
    for g, docs in enumerate(GROUPS):
        rows = DOC * len(docs)
        split_x = isinstance(x, tuple)
        results.append(run(
            feed_kernel, [],
            [x[g] if split_x else x, mine[g], theirs[g], vec, weights[2], weights[3]],
            [sds(rows, D, dtype=F32), sds(rows, D), sds(rows, D), stats(docs),
             sds(rows, HIDDEN), sds(rows, HIDDEN), sds(rows, D)],
            [], docs, 0 if split_x else docs[0], base,
        ))
    return tuple(zip(*results))


FEED_BACK_OUTS = [
    sds(ROWS, D, dtype=F32), sds(ROWS, D), sds(8, D, dtype=F32), sds(ROWS, HIDDEN), sds(ROWS, D),
]


def feed_back_second(ids, first, mine, theirs, vec, own, other, slope, weights):
    return run(
        feed_back_second_kernel, [ids],
        [first, mine, theirs, vec, own, other, slope, weights[2], weights[3]],
        [sds(HALF, D)] + FEED_BACK_OUTS,
        [pltpu.VMEM((ROWS, D), BF16), pltpu.VMEM((ROWS, D), BF16)], 6,
    )


def feed_back_first(ids, normed, inv, vec, own, other, resid, mine, theirs, slope, weights):
    return run(
        feed_back_first_kernel, [ids],
        [normed, inv, vec, own, other, resid, mine, theirs, slope, weights[2], weights[3]],
        [sds(HALF, D, dtype=F32)] + FEED_BACK_OUTS,
        [pltpu.VMEM((ROWS, D), BF16), pltpu.VMEM((ROWS, D), F32)], 2,
    )


def attend_back(base, ids, gs, mine, theirs, normed, inv, qkv, prob, vec, weights):
    return run(
        attend_back_kernel, [ids],
        [gs, mine, theirs, normed, inv, vec, qkv, prob, weights[0], weights[1]],
        [sds(ROWS, D, dtype=F32), sds(ROWS, D), sds(8, D, dtype=F32), sds(ROWS, 1152), sds(ROWS, D),
         sds(HALF if base == 0 else 16, D)],
        [pltpu.VMEM((ROWS, PIECE), BF16), pltpu.VMEM(WIDE, BF16)], base,
    )


SPLIT_OUTS = [sds(32, *BLOCK), sds(32, *BLOCK)]
BLOCKS = pltpu.VMEM((4, 2, 8) + BLOCK, BF16)


def out_grad(chunk, ids, act, gs_low):
    return run(out_grad_kernel, [ids], [act, gs_low], SPLIT_OUTS, [BLOCKS], chunk)


def in_grad(chunk, ids, low, grad_pre):
    return run(in_grad_kernel, [ids], [low, grad_pre], SPLIT_OUTS, [BLOCKS], chunk)


def attend_grad(chunk, ids, x, grad_qkv, ctx, low, norms=()):
    outs = SPLIT_OUTS
    if norms:
        outs = [sds(33, *BLOCK), sds(32, *BLOCK), sds(8, D, dtype=F32)]
    return run(
        attend_grad_kernel, [ids], [x, grad_qkv, ctx, low, *norms], outs, [BLOCKS], chunk
    )


def vectors(rows):
    return run(vectors_kernel, [], rows, [sds(8, D, dtype=F32)], [])[0]


def split(sources, norm=None):
    arrays = [a for pair in sources for a in pair]
    sizes = tuple(keep.shape[0] // 2 for keep, _ in sources)
    count = sum(sizes)
    outs = [sds(count + (norm is not None), *BLOCK), sds(count, *BLOCK)]
    if norm is not None:
        arrays, outs = arrays + [norm], outs + [sds(8, D, dtype=F32)]
    return run(split_kernel, [], arrays, outs, [], sizes, int(norm is not None))


def far_add(keep, got, norm=None):
    if norm is None:
        return run(far_kernel, [], [keep, got], [sds(*keep.shape)], [], 0)
    count = keep.shape[0] - keep.shape[0] % 8
    outs = [sds(count + 1, *BLOCK), sds(8, D, dtype=F32)]
    return run(far_kernel, [], [keep, got, norm], outs, [], 1)


def join(held, got, count=1):
    size = held.shape[0] // count
    return run(join_kernel, [], [held, got], [sds(2 * size, *BLOCK)] * count, [], count)


PLACED = [
    sds(HIDDEN, D, dtype=F32),
    sds(D, HIDDEN, dtype=F32),
    sds(3, D, PIECE, dtype=F32),
    sds(PIECE, D, dtype=F32),
]


def place(ids, items, values, into=()):
    return pl.pallas_call(
        functools.partial(place_kernel, tuple(items)),
        out_shape=PLACED,
        in_specs=[SCALARS] + [LOCAL] * len(values) + [REMOTE] * len(into),
        out_specs=[REMOTE] * 4,
        scratch_shapes=[pltpu.VMEM((6, PIECE, PIECE), F32), pltpu.SemaphoreType.DMA((6,))],
        input_output_aliases={1 + len(values) + i: i for i in range(len(into))},
        compiler_params=pltpu.CompilerParams(vmem_limit_bytes=6 * 2**20),
        cost_estimate=COST,
        name="place_kernel",
    )(ids, *values, *into)


def swap(value):
    if isinstance(value, tuple):
        one, two = [swap(part) for part in value]
        return lax.optimization_barrier((one, value[1]))[0], two
    return lax.ppermute(value, "tensor", SWAP)


def flip(chip, core, stage, axis):
    pos = [chip % 4, chip // 4 % 4, chip // 16]
    low = (core == 0) == (stage == 0)
    pos[axis] = pos[axis] ^ 1 if low else 3 - pos[axis]
    return pos[0] + 4 * pos[1] + 16 * pos[2]


def exchange(value, stage, axis):
    pairs = [
        (2 * chip + core, 2 * flip(chip, core, stage, axis) + core)
        for chip in range(64)
        for core in range(2)
    ]
    return lax.ppermute(value, ("dp", "tensor"), pairs)


class Order:
    def __init__(self):
        self.token = None

    def hold(self, value):
        if self.token is None:
            return value
        return lax.optimization_barrier((value, self.token))[0]


class Single:
    def __init__(self, order, axes, send, keep, norm=None):
        self.order, self.axes, self.keep, self.norm, self.round = order, axes, keep, norm, 0
        self.send(send, 0, 0)

    def send(self, value, stage, j):
        self.order.token = value
        self.got = exchange(value, stage, self.axes[j % 3])

    def next(self):
        self.round += 1
        got = self.order.hold(self.got)
        if self.round > 8:
            self.got = self.order.token = got
            return
        if self.round < 3:
            value, self.keep, *norm = split([(self.keep, got)], self.norm)
            self.send(value, 0, self.round)
        elif self.round < 6:
            self.keep, *norm = far_add(self.keep, got, self.norm)
            self.send(self.keep, 1, self.round)
        elif self.round == 6:
            self.keep, *norm = far_add(self.keep, got, self.norm)
            if norm:
                self.keep = self.keep[:8]
            self.send(self.keep, 0, 2)
        else:
            norm = ()
            self.keep = join(self.keep, got)[0]
            self.send(self.keep, 0, 8 - self.round)
        if norm:
            self.norm = norm[0]


class Pair:
    def __init__(self, order, axes):
        self.order, self.axes = order, axes
        self.keep, self.got, self.calls = [None, None], [None, None], [0, 0]
        self.both = 2

    def start(self, i, send, keep):
        self.keep[i] = keep
        self.send(i, send, 0)

    def send(self, i, value, j):
        self.order.token = value
        self.got[i] = exchange(value, 0, self.axes[i ^ j])

    def next(self, i):
        self.calls[i] += 1
        if self.calls[i] == 1:
            value, self.keep[i] = split([(self.keep[i], self.order.hold(self.got[i]))])
            self.send(i, value, 1)
        elif self.calls[i] == 2 and self.calls[1 - i] == 2:
            got = [self.order.hold(g) for g in self.got]
            value, self.held = split([(self.keep[0], got[0]), (self.keep[1], got[1])])
            self.order.token = value
            self.arrived = exchange(value, 0, self.axes[2])
        elif self.calls[i] == 3:
            self.keep[i] = join(self.keep[i], self.order.hold(self.got[i]))[0]
            self.send(i, self.keep[i], 0)
        elif self.calls[i] == 4:
            self.got[i] = self.order.token = self.order.hold(self.got[i])

    def next_both(self):
        got = self.order.hold(self.arrived)
        self.both += 1
        if self.both <= 6:
            self.held = far_add(self.held, got)[0]
            self.order.token = self.held
            if self.both < 6:
                self.arrived = exchange(self.held, 1, self.axes[self.both - 3])
            else:
                self.arrived = exchange(self.held, 0, self.axes[2])
        else:
            self.keep = list(join(self.held, got, 2))
            for i in range(2):
                self.send(i, self.keep[i], 1)


UPPER_PAIR, UPPER_LAST = (1, 0, 2), (2, 1, 0)
LOWER_PAIR, LOWER_LAST = (2, 1, 0), (0, 2, 1)
CHUNK_AXES = [
    UPPER_PAIR,
    (UPPER_PAIR[1], UPPER_PAIR[0], UPPER_PAIR[2]),
    UPPER_LAST,
    LOWER_PAIR,
    (LOWER_PAIR[1], LOWER_PAIR[0], LOWER_PAIR[2]),
    LOWER_LAST,
]
TAIL = (
    "Ub", "Lp", "Lq", "Um", "Ub", "Lb", "Lp", "Lq", "Ub", "Um", "Lb", "Ub", "Lm",
    "Lb", "Um", "Ub", "Lm", "Lb", "Ub", "Um", "Lb", "Lm", "Um", "Ub", "Lb", "Lm",
    "Up", "Uq", "Lb", "Ub", "Lm", "Lb", "Up", "Uq", "Lq", "Lp",
)


def device_table():
    rows = []
    for chip in range(64):
        pos = [chip % 4, chip // 4 % 4, chip // 16]
        low = [(p ^ (p >> 1)) & 1 for p in pos]
        high = [p >> 1 for p in pos]
        for core in range(2):
            near = low if core == 0 else high
            row = [core]
            for axes in CHUNK_AXES:
                row += [near[axis] for axis in axes] + [0]
            rows.append(row + [0] * 7)
    return np.array(rows, np.int32)


def on_device(
    tokens,
    skip_tokens,
    cot_back,
    cot_head,
    one_span,
    *params,
):
    lower = [params[i] for i in (0, 1, 4, 5)]
    upper = [params[i] for i in (8, 9, 12, 13)]
    device = lax.axis_index("dp") * 2 + lax.axis_index("tensor")
    row = lax.dynamic_index_in_dim(jnp.asarray(device_table()), device, 0, keepdims=False)
    ids = jnp.concatenate([row, one_span])
    tokens_other = swap(tokens)
    tokens, ids = lax.optimization_barrier((tokens, ids))
    vec = vectors([params[i] for i in (2, 3, 6, 7, 10, 11, 14, 15)])
    skip_other = swap(skip_tokens)
    cot_head_other = swap(cot_head)
    cot_back_other = swap(cot_back)
    order = Order()

    x_l, qkv_l, prob_l, ctx_l, part = attend_first(ids, tokens, tokens_other, lower)
    first_l, low_l, normed_al, inv_al, act_l, slope_l, part = feed(
        0, x_l, part, swap(part), vec, lower
    )
    x_u, normed_fl, inv_fl, backs, qkv_u, prob_u, ctx_u, part = attend_second(
        ids, first_l, part, swap(part), vec, skip_tokens, skip_other, upper
    )
    first_u, low_u, normed_au, inv_au, act_u, slope_u, part = feed(
        4, x_u, part, swap(part), vec, upper
    )
    head_out, gs_u, gs_low_u, norms_fu, grad_pre_u, part = feed_back_second(
        ids, first_u, part, swap(part), vec, cot_head, cot_head_other, slope_u, upper
    )
    pair_u, pair_l = Pair(order, UPPER_PAIR), Pair(order, LOWER_PAIR)
    theirs = swap(part)
    pair_u.start(0, *out_grad(0, ids, act_u, gs_low_u))
    pair_u.start(1, *in_grad(1, ids, low_u, order.hold(grad_pre_u)))
    resid_u, gr_low_u, norms_au, grad_qkv_u, part, _ = attend_back(
        4, ids, order.hold(gs_u), part, theirs, normed_au, inv_au, qkv_u, prob_u, vec=vec,
        weights=upper,
    )
    theirs = swap(part)
    at_u = Single(
        order, UPPER_LAST, *attend_grad(2, ids, x_u, grad_qkv_u, ctx_u, order.hold(gr_low_u))
    )
    pair_u.next(0)
    pair_u.next(1)
    grad_skip, gs_l, gs_low_l, norms_fl, grad_pre_l, part = feed_back_first(
        ids, normed_fl, inv_fl, vec, cot_back, cot_back_other, order.hold(resid_u), part,
        theirs, slope_l, lower,
    )
    theirs = swap(part)
    order.token = gs_low_l
    pair_u.next(0)
    pair_u.next(1)
    pair_l.start(0, *out_grad(3, ids, act_l, order.hold(gs_low_l)))
    pair_l.start(1, *in_grad(4, ids, low_l, order.hold(grad_pre_l)))
    at_u.next()
    resid_l, gr_low_l, norms_al, grad_qkv_l, part, away = attend_back(
        0, ids, order.hold(gs_l), part, theirs, normed_al, inv_al, qkv_l, prob_l, vec=vec,
        weights=lower,
    )
    at_l = Single(
        order, LOWER_LAST,
        *attend_grad(
            5, ids, x_l, grad_qkv_l, ctx_l, gr_low_l, (norms_al, norms_fl, norms_au, norms_fu)
        ),
    )
    act = {
        "Up": lambda: pair_u.next(0),
        "Uq": lambda: pair_u.next(1),
        "Um": pair_u.next_both,
        "Ub": at_u.next,
        "Lp": lambda: pair_l.next(0),
        "Lq": lambda: pair_l.next(1),
        "Lm": pair_l.next_both,
        "Lb": at_l.next,
    }
    away = swap(order.hold(away))
    for index, name in enumerate(TAIL):
        act[name]()
        if index == 2:
            grad_tokens, back_out = run(
                rows_kernel, [ids], [resid_l, part, order.hold(away), backs],
                [sds(HALF, D, dtype=F32), sds(HALF, D)], [pltpu.VMEM((ROWS, D), BF16)],
            )
            order.token = grad_tokens
    done_u = place(
        ids,
        [(0, 0), (0, 1), (1, 0), (1, 1), (2, 0), (2, 1)],
        [pair_u.keep[0], pair_u.got[0], pair_u.keep[1], pair_u.got[1], at_u.keep,
         order.hold(at_u.got)],
    )
    order.token = done_u[0]
    done_l = place(
        ids, [(3, 0), (4, 0), (5, 0)],
        [pair_l.keep[0], pair_l.keep[1], order.hold(at_l.keep)],
    )
    for chunk, got in ((5, at_l.got), (4, pair_l.got[1]), (3, pair_l.got[0])):
        done_l = place(ids, [(chunk, 1)], [got], done_l)
    norms = at_l.norm
    out_gu, in_gu, qkv_gu, proj_gu = done_u
    out_gl, in_gl, qkv_gl, proj_gl = done_l
    return (
        back_out,
        head_out,
        grad_tokens,
        grad_skip,
        qkv_gl,
        proj_gl,
        norms[0],
        norms[1],
        in_gl,
        out_gl,
        norms[2],
        norms[3],
        qkv_gu,
        proj_gu,
        norms[4],
        norms[5],
        in_gu,
        out_gu,
        norms[6],
        norms[7],
    )


def solution(mesh):
    rows = P(("dp", "tensor"), None)
    weights = (
        P(None, None, "tensor"),
        P("tensor", None),
        P(),
        P(),
        P(None, "tensor"),
        P("tensor", None),
        P(),
        P(),
    )
    return jax.shard_map(
        on_device,
        mesh=mesh,
        in_specs=(rows,) * 4 + (P("dp"),) + weights + weights,
        out_specs=(rows,) * 4 + weights + weights,
        check_vma=False,
    )
```

```python
import functools

import jax
import jax.numpy as jnp
from jax import lax
from jax.experimental import pallas as pl
from jax.experimental.pallas import tpu as pltpu
from jax.sharding import PartitionSpec as P

SPAN = 128
EPS = 1e-06
SCALE = 0.125
NEG = -1000000000.0

D = 768
ROWS = 768
HALF = ROWS // 2
HIDDEN = 1536
PIECE = 384
PAIR = 128
BLOCK = (48, 384)
F32 = jnp.float32
BF16 = jnp.bfloat16
SPANS_AT = 1

SWAP = [(0, 1), (1, 0)]


def dot_nn(left, right):
    return lax.dot_general(left, right, (((1,), (0,)), ((), ())), preferred_element_type=F32)


def dot_nt(left, right):
    return lax.dot_general(left, right, (((1,), (1,)), ((), ())), preferred_element_type=F32)


def dot_tn(left, right):
    return lax.dot_general(left, right, (((0,), (0,)), ((), ())), preferred_element_type=F32)


def normalize(resid):
    mean = jnp.mean(resid, axis=-1, keepdims=True)
    centered = resid - mean
    var = jnp.mean(centered * centered, axis=-1, keepdims=True)
    inv = lax.rsqrt(var + EPS)
    return centered * inv, inv


def norm_grad(grad_out, normed, inv, gain):
    grad = grad_out * gain
    first = jnp.mean(grad, axis=-1, keepdims=True)
    second = jnp.mean(grad * normed, axis=-1, keepdims=True)
    return inv * (grad - first - normed * second)


def fold(value):
    return jnp.sum(value.reshape(-1, 8, value.shape[-1]), axis=0)

DOC = 2 * SPAN
DOCS = ROWS // DOC


def side_of(ids_ref):
    return ids_ref[0] & 1


def chunk_bits(ids_ref, chunk):
    chip, core = ids_ref[0] >> 1, ids_ref[0] & 1
    bits = []
    for axis in CHUNK_AXES[chunk]:
        at = (chip >> (2 * axis)) & 3
        low, high = (at ^ (at >> 1)) & 1, at >> 1
        bits.append(low + core * (high - low))
    return bits


def doc_rows(doc):
    return slice(doc * DOC, (doc + 1) * DOC)


def half_rows(index):
    return pl.ds(pl.multiple_of(index * HALF, HALF), HALF)


def join_halves(side, own_ref, other_ref, full_ref):
    full_ref[half_rows(side), :] = own_ref[...]
    full_ref[half_rows(1 - side), :] = other_ref[...]


def doc_masks(ids_ref, doc):
    row = lax.broadcasted_iota(jnp.int32, (DOC, 1), 0)
    keep = jnp.where((row < SPAN) | (ids_ref[SPANS_AT + doc] == 0), 1.0, 0.0)
    return keep, (row & (SPAN - 1)) == 0


def spread(column):
    return jnp.broadcast_to(column, (column.shape[0], 128))


def head_masks():
    lane = lax.broadcasted_iota(jnp.int32, (1, PAIR), 1)
    return lane < 64


def both_heads(value, left):
    zero = jnp.zeros_like(value)
    return jnp.concatenate([jnp.where(left, value, zero), jnp.where(left, zero, value)], axis=0)


class Rows:
    def __init__(self, *refs):
        self.refs = refs

    def find(self, index):
        head = index[0] if isinstance(index, tuple) else index
        rest = index[1:] if isinstance(index, tuple) else ()
        at = head if isinstance(head, int) else head.start
        base = 0
        for ref in self.refs:
            if at < base + ref.shape[0]:
                break
            base += ref.shape[0]
        head = head - base if isinstance(head, int) else slice(at - base, head.stop - base)
        return ref, (head, *rest)

    def __getitem__(self, index):
        head = index[0] if isinstance(index, tuple) else index
        if head is Ellipsis or head == slice(None):
            return jnp.concatenate([ref[index] for ref in self.refs], axis=0)
        ref, index = self.find(index)
        return ref[index]


GROUPS = ((0, 1), (2,))


def attend(ids_ref, docs, x_ref, proj_ref, qkv_ref, prob_ref, ctx_ref, part_ref, wide, skip=0):
    for i, doc in enumerate(docs):
        at = doc_rows(i)
        out = dot_nn(x_ref[doc_rows(i + skip), :], wide[...])
        qkv_ref[at, :384] = (out[:, :384] * SCALE).astype(BF16)
        qkv_ref[at, 384:] = out[:, 384:].astype(BF16)
    left = head_masks()
    col = lax.broadcasted_iota(jnp.int32, (1, 2 * DOC), 1) & (DOC - 1)
    for i, doc in enumerate(docs):
        at = doc_rows(i)
        key_ok = (col < SPAN) | (ids_ref[SPANS_AT + doc] == 0)
        scores = []
        for pair in range(3):
            query = qkv_ref[at, pair * PAIR:(pair + 1) * PAIR]
            keys = qkv_ref[at, 384 + pair * PAIR:384 + (pair + 1) * PAIR]
            scores.append(jnp.where(key_ok, dot_nt(query, both_heads(keys, left)), NEG))
        for pair in range(3):
            probs = []
            for head in range(2):
                score = scores[pair][:, head * DOC:(head + 1) * DOC]
                raised = jnp.exp(score - jnp.max(score, axis=-1, keepdims=True))
                probs.append(
                    (raised * (1.0 / jnp.sum(raised, axis=-1, keepdims=True))).astype(BF16)
                )
            prob = jnp.concatenate(probs, axis=1)
            prob_ref[i, pair] = prob
            values = qkv_ref[at, 768 + pair * PAIR:768 + (pair + 1) * PAIR]
            mixed = dot_nn(prob, both_heads(values, left))
            ctx_ref[at, pair * PAIR:(pair + 1) * PAIR] = mixed.astype(BF16)
    for i, doc in enumerate(docs):
        at = doc_rows(i)
        part_ref[at, :] = dot_nn(ctx_ref[at, :], proj_ref[...]).astype(BF16)


def attend_first_kernel(
    docs, ids_ref, other_ref, own_ref, qkv_w_ref, proj_w_ref,
    x_ref, wide, proj, qkv_ref, prob_ref, ctx_ref, part_ref, sems,
):
    side = side_of(ids_ref)
    copies = [pltpu.make_async_copy(own_ref, x_ref.at[half_rows(side), :], sems.at[0])]
    for index in range(3):
        cut = slice(index * 384, (index + 1) * 384)
        copies.append(
            pltpu.make_async_copy(qkv_w_ref.at[index], wide.at[:, cut], sems.at[1 + index])
        )
    copies.append(pltpu.make_async_copy(proj_w_ref, proj, sems.at[4]))
    for copy in copies:
        copy.start()
    x_ref[half_rows(1 - side), :] = other_ref[...]
    for copy in copies:
        copy.wait()
    attend(ids_ref, docs, x_ref, proj, qkv_ref, prob_ref, ctx_ref, part_ref, wide)


def attend_more_kernel(
    docs, ids_ref, x_ref, wide_ref, proj_ref, qkv_ref, prob_ref, ctx_ref, part_ref,
):
    attend(
        ids_ref, docs, x_ref, proj_ref, qkv_ref, prob_ref, ctx_ref, part_ref, wide_ref, docs[0]
    )


def attend_second_kernel(
    docs, base, ids_ref, first_ref, mine_ref, theirs_ref, vec_ref, own_ref, other_ref,
    qkv_w_ref, proj_ref,
    x_ref, normed_ref, inv_ref, back_ref, qkv_ref, prob_ref, ctx_ref, part_ref, *rest,
):
    *wide_out, full = rest
    join_halves(side_of(ids_ref), own_ref, other_ref, full)
    for i, doc in enumerate(docs):
        at = doc_rows(i)
        keep, cls = doc_masks(ids_ref, doc)
        resid = first_ref[at, :] + mine_ref[at, :].astype(F32) + theirs_ref[at, :].astype(F32)
        normed, inv = normalize(resid)
        back = normed * vec_ref[base:base + 1, :] + vec_ref[base + 1:base + 2, :]
        normed_ref[at, :] = normed.astype(BF16)
        inv_ref[at, :] = spread(inv)
        x_ref[at, :] = jnp.where(cls, back, full[doc_rows(doc), :].astype(F32)).astype(BF16)
        back_ref[at, :] = (back * keep).astype(BF16)
    wide = qkv_w_ref
    if wide_out:
        wide = wide_out[0]
        for index in range(3):
            wide[:, index * 384:(index + 1) * 384] = qkv_w_ref[index]
    attend(ids_ref, docs, x_ref, proj_ref, qkv_ref, prob_ref, ctx_ref, part_ref, wide)


def feed_kernel(
    docs, skip, base, x_ref, mine_ref, theirs_ref, vec_ref, in_ref, out_w_ref,
    first_ref, low_ref, normed_ref, inv_ref, act_ref, slope_ref, part_ref,
):
    for i, doc in enumerate(docs):
        at = doc_rows(i)
        resid = x_ref[doc_rows(i + skip), :].astype(F32) + mine_ref[at, :].astype(F32)
        resid = resid + theirs_ref[at, :].astype(F32)
        normed, inv = normalize(resid)
        first = normed * vec_ref[base:base + 1, :] + vec_ref[base + 1:base + 2, :]
        normed_ref[at, :] = normed.astype(BF16)
        inv_ref[at, :] = spread(inv)
        first_ref[at, :] = first
        low_ref[at, :] = first.astype(BF16)
    for i, doc in enumerate(docs):
        at = doc_rows(i)
        for piece in range(3):
            cut = slice(piece * 512, (piece + 1) * 512)
            pre = dot_nn(low_ref[at, :], in_ref[:, cut])
            share = 0.5 * (1.0 + lax.erf(pre * 0.7071067811865476))
            density = jnp.exp(-0.5 * pre * pre) * 0.3989422804014327
            act_ref[at, cut] = (pre * share).astype(BF16)
            slope_ref[at, cut] = (share + pre * density).astype(BF16)
    for i, doc in enumerate(docs):
        at = doc_rows(i)
        part_ref[at, :] = dot_nn(act_ref[at, :], out_w_ref[...]).astype(BF16)


def feed_back(gs_low_ref, slope_ref, in_ref, out_w_ref, grad_pre_ref, part_ref):
    for doc in range(DOCS):
        at = doc_rows(doc)
        for piece in range(3):
            cut = slice(piece * 512, (piece + 1) * 512)
            grad_act = dot_nt(gs_low_ref[at, :], out_w_ref[cut, :])
            grad_pre_ref[at, cut] = (grad_act * slope_ref[at, cut].astype(F32)).astype(BF16)
    for doc in range(DOCS):
        at = doc_rows(doc)
        part_ref[at, :] = dot_nt(grad_pre_ref[at, :], in_ref[...]).astype(BF16)


def put_norm_grads(norms_ref, sums):
    gain, shift = sums
    norms_ref[...] = jnp.zeros_like(norms_ref)
    norms_ref[0:1, :] = jnp.sum(gain, axis=0, keepdims=True)
    norms_ref[1:2, :] = jnp.sum(shift, axis=0, keepdims=True)


def add_sums(sums, grad_out, normed):
    new = (fold(grad_out * normed), fold(grad_out))
    return new if sums is None else (sums[0] + new[0], sums[1] + new[1])


def feed_back_second_kernel(
    base, ids_ref, first_ref, mine_ref, theirs_ref, vec_ref, own_ref, other_ref,
    slope_ref, in_ref, out_w_ref,
    head_ref, gs_ref, gs_low_ref, norms_ref, grad_pre_ref, part_ref, cot, full,
):
    side = side_of(ids_ref)
    join_halves(side, own_ref, other_ref, cot)
    sums = None
    for doc in range(DOCS):
        at = doc_rows(doc)
        keep, _ = doc_masks(ids_ref, doc)
        resid = first_ref[at, :] + mine_ref[at, :].astype(F32) + theirs_ref[at, :].astype(F32)
        normed, inv = normalize(resid)
        head = normed * vec_ref[base:base + 1, :] + vec_ref[base + 1:base + 2, :]
        full[at, :] = (head * keep).astype(BF16)
        grad_out = cot[at, :].astype(F32) * keep
        grad = norm_grad(grad_out, normed, inv, vec_ref[base:base + 1, :])
        gs_ref[at, :] = grad
        gs_low_ref[at, :] = grad.astype(BF16)
        sums = add_sums(sums, grad_out, normed)
    head_ref[...] = full[half_rows(side), :]
    put_norm_grads(norms_ref, sums)
    feed_back(gs_low_ref, slope_ref, in_ref, out_w_ref, grad_pre_ref, part_ref)


def feed_back_first_kernel(
    base, ids_ref, normed_ref, inv_ref, vec_ref, own_ref, other_ref,
    resid_ref, mine_ref, theirs_ref, slope_ref, in_ref, out_w_ref,
    skip_ref, gs_ref, gs_low_ref, norms_ref, grad_pre_ref, part_ref, cot, full,
):
    side = side_of(ids_ref)
    join_halves(side, own_ref, other_ref, cot)
    sums = None
    for doc in range(DOCS):
        at = doc_rows(doc)
        keep, cls = doc_masks(ids_ref, doc)
        above = resid_ref[at, :] + mine_ref[at, :].astype(F32) + theirs_ref[at, :].astype(F32)
        full[at, :] = jnp.where(cls, 0.0, above)
        normed = normed_ref[at, :].astype(F32)
        grad_out = cot[at, :].astype(F32) * keep + jnp.where(cls, above, 0.0)
        grad = norm_grad(grad_out, normed, inv_ref[at, 0:1], vec_ref[base:base + 1, :])
        gs_ref[at, :] = grad
        gs_low_ref[at, :] = grad.astype(BF16)
        sums = add_sums(sums, grad_out, normed)
    skip_ref[...] = full[half_rows(side), :]
    put_norm_grads(norms_ref, sums)
    feed_back(gs_low_ref, slope_ref, in_ref, out_w_ref, grad_pre_ref, part_ref)


def attend_back_kernel(
    base, ids_ref, gs_ref, mine_ref, theirs_ref, normed_ref, inv_ref, vec_ref, qkv_ref, prob_ref,
    qkv_w_ref, proj_ref,
    resid_ref, low_ref, norms_ref, grad_qkv_ref, part_ref, away_ref, grad_ctx, wide,
):
    for index in range(3):
        wide[:, index * 384:(index + 1) * 384] = qkv_w_ref[index]
    sums = None
    for doc in range(DOCS):
        at = doc_rows(doc)
        grad_out = gs_ref[at, :] + mine_ref[at, :].astype(F32) + theirs_ref[at, :].astype(F32)
        normed = normed_ref[at, :].astype(F32)
        grad = norm_grad(grad_out, normed, inv_ref[at, 0:1], vec_ref[base:base + 1, :])
        resid_ref[at, :] = grad
        low_ref[at, :] = grad.astype(BF16)
        sums = add_sums(sums, grad_out, normed)
    put_norm_grads(norms_ref, sums)
    for doc in range(DOCS):
        at = doc_rows(doc)
        grad_ctx[at, :] = dot_nt(low_ref[at, :], proj_ref[...]).astype(BF16)
    left = head_masks()
    for doc in range(DOCS):
        at = doc_rows(doc)
        pairs = [slice(pair * PAIR, (pair + 1) * PAIR) for pair in range(3)]
        grad_probs = []
        for pair in range(3):
            values = qkv_ref[at, 768 + pair * PAIR:768 + (pair + 1) * PAIR]
            grad_probs.append(dot_nt(grad_ctx[at, pairs[pair]], both_heads(values, left)))
        for pair in range(3):
            prob_low = prob_ref[doc, pair]
            scored = []
            for head in range(2):
                cut = slice(head * DOC, (head + 1) * DOC)
                prob = prob_low[:, cut].astype(F32)
                grad_prob = grad_probs[pair][:, cut]
                inner = jnp.sum(grad_prob * prob, axis=-1, keepdims=True)
                scored.append((prob * (grad_prob - inner)).astype(BF16))
            grad_scores = jnp.concatenate(scored, axis=1)
            query = qkv_ref[at, pairs[pair]]
            keys = qkv_ref[at, 384 + pair * PAIR:384 + (pair + 1) * PAIR]
            grad_query = dot_nn(grad_scores, both_heads(keys, left)) * SCALE
            grad_keys = dot_tn(grad_scores, query)
            grad_values = dot_tn(prob_low, grad_ctx[at, pairs[pair]])
            grad_qkv_ref[at, pair * PAIR:(pair + 1) * PAIR] = grad_query.astype(BF16)
            for index, grad in ((1, grad_keys), (2, grad_values)):
                cut = slice(index * 384 + pair * PAIR, index * 384 + (pair + 1) * PAIR)
                grad_qkv_ref[at, cut] = jnp.where(left, grad[:DOC], grad[DOC:]).astype(BF16)
    for doc in range(DOCS):
        at = doc_rows(doc)
        part_ref[at, :] = dot_nt(grad_qkv_ref[at, :], wide[...]).astype(BF16)
    if base == 0:
        away_ref[...] = part_ref[half_rows(1 - side_of(ids_ref)), :]
    else:
        away_ref[...] = jnp.zeros_like(away_ref)


def rows_kernel(ids_ref, resid_ref, mine_ref, theirs_ref, back_ref, out_ref, back_out_ref, full):
    at = half_rows(side_of(ids_ref))
    out_ref[...] = resid_ref[at, :] + mine_ref[at, :].astype(F32) + theirs_ref[...].astype(F32)
    full[...] = back_ref[...]
    back_out_ref[...] = full[at, :]


def cut_wide(value, blocks, piece):
    for half in range(2):
        for k in range(8):
            blocks[piece, half, k] = value[k * 48:(k + 1) * 48, half * 384:(half + 1) * 384]


def cut_tall(value, blocks, piece):
    for half in range(2):
        for k in range(8):
            at = half * 384 + k * 48
            blocks[piece, half, k] = value[at:at + 48, :]


def put_blocks(ids_ref, turn, blocks, send_ref, keep_ref):
    first, second, third = chunk_bits(ids_ref, turn)
    for rel, ref in ((1, send_ref), (0, keep_ref)):
        for b in range(2):
            piece = 2 * (rel ^ first) + (b ^ second)
            for e in range(2):
                for k in range(8):
                    ref[16 * b + 8 * e + k] = blocks[piece, e ^ third, k]


def out_grad_kernel(turn, ids_ref, act_ref, gs_ref, send_ref, keep_ref, blocks):
    for p in range(2):
        value = dot_tn(act_ref[:, p * 768:(p + 1) * 768], gs_ref[...]).astype(BF16)
        cut_wide(value[:384], blocks, 2 * p)
        cut_wide(value[384:], blocks, 2 * p + 1)
    put_blocks(ids_ref, turn, blocks, send_ref, keep_ref)


def in_grad_kernel(turn, ids_ref, low_ref, grad_ref, send_ref, keep_ref, blocks):
    for p in range(2):
        value = dot_tn(low_ref[...], grad_ref[:, p * 768:(p + 1) * 768]).astype(BF16)
        cut_tall(value[:, :384], blocks, 2 * p)
        cut_tall(value[:, 384:], blocks, 2 * p + 1)
    put_blocks(ids_ref, turn, blocks, send_ref, keep_ref)


def attend_grad_kernel(turn, ids_ref, x_ref, grad_ref, ctx_ref, low_ref, *refs):
    norm_refs, (send_ref, keep_ref), blocks = refs[:-3 - (len(refs) > 3)], refs[-3:-1], refs[-1]
    if norm_refs:
        send_ref, keep_ref = refs[-4:-2]
        value = jnp.concatenate([ref[0:2, :] for ref in norm_refs], axis=0)
        refs[-2][...] = value
        send_ref[32] = norm_block(value)
    value = dot_tn(x_ref[...], grad_ref[...]).astype(BF16)
    for piece in range(3):
        cut_tall(value[:, piece * 384:(piece + 1) * 384], blocks, piece)
    cut_wide(dot_tn(ctx_ref[...], low_ref[...]).astype(BF16), blocks, 3)
    put_blocks(ids_ref, turn, blocks, send_ref, keep_ref)


def vectors_kernel(*refs):
    out_ref = refs[-1]
    for i in range(8):
        out_ref[i:i + 1, :] = refs[i][...].reshape(1, D)


def plus(one, two):
    return (one.astype(F32) + two.astype(F32)).astype(BF16)


def norm_block(value):
    high = value.astype(BF16)
    low = (value - high.astype(F32)).astype(BF16)
    rows = [high[:, :PIECE], high[:, PIECE:], low[:, :PIECE], low[:, PIECE:]]
    return jnp.concatenate(rows + [jnp.zeros((16, PIECE), BF16)], axis=0)


def block_norm(block):
    high = jnp.concatenate([block[0:8], block[8:16]], axis=1)
    low = jnp.concatenate([block[16:24], block[24:32]], axis=1)
    return high.astype(F32) + low.astype(F32)


def add_norm(value, block):
    return block_norm(norm_block(value)) + block_norm(block)


def split_kernel(sizes, with_norm, *refs):
    count = len(sizes)
    ins, outs = refs[:2 * count], refs[2 * count + with_norm:]
    at = 0
    for i, m in enumerate(sizes):
        keep, got = ins[2 * i], ins[2 * i + 1]
        outs[1][at:at + m] = plus(keep[:m], got[:m])
        outs[0][at:at + m] = plus(keep[m:], got[m:2 * m])
        at += m
    if with_norm:
        value = add_norm(refs[2 * count][...], ins[1][2 * sizes[0]])
        outs[0][at] = norm_block(value)
        outs[2][...] = value


def far_kernel(with_norm, *refs):
    if with_norm:
        keep, got, norm, out, norm_out = refs
        count = keep.shape[0] - (keep.shape[0] % 8)
        value = add_norm(norm[...], got[got.shape[0] - 1])
        out[count] = norm_block(value)
        norm_out[...] = value
    else:
        keep, got, out = refs
        count = keep.shape[0]
    out[:count] = plus(keep[:count], got[:count])


def join_kernel(count, held_ref, got_ref, *outs):
    size = outs[0].shape[0] // 2
    for i in range(count):
        at = slice(i * size, (i + 1) * size)
        outs[i][:size] = held_ref[at]
        outs[i][size:] = got_ref[at]


def place_kernel(items, ids_ref, *refs):
    ins, outs, squares, sems = refs[:len(items)], refs[-6:-2], refs[-2], refs[-1]
    slots = squares.shape[0]

    def copies(index, chunk, far, b, e):
        first, second, _ = chunk_bits(ids_ref, chunk)
        turn = chunk % 3
        slot = index % slots
        piece = 2 * (far ^ first) + (b ^ second)
        at = pl.ds(pl.multiple_of(piece * PIECE, PIECE), PIECE)
        cut = slice(e * PIECE, (e + 1) * PIECE)

        def copy(ref):
            return pltpu.make_async_copy(squares.at[slot], ref, sems.at[slot])

        if turn == 0:
            return [(None, copy(outs[0].at[at, cut]))]
        if turn == 1:
            return [(None, copy(outs[1].at[cut, at]))]
        return [
            (piece < 3, copy(outs[2].at[jnp.minimum(piece, 2), cut, :])),
            (piece == 3, copy(outs[3].at[:, cut])),
        ]

    def each(pairs, wait):
        for when, copy in pairs:
            def act(copy=copy):
                copy.wait() if wait else copy.start()

            if when is None:
                act()
            else:
                pl.when(when)(act)

    flight = []
    for (chunk, far), from_ref in zip(items, ins):
        third = chunk_bits(ids_ref, chunk)[2]
        for b in range(2):
            for e in range(2):
                index = len(flight)
                if index >= slots:
                    each(flight[index - slots], True)
                for k in range(8):
                    block = from_ref[16 * b + 8 * (e ^ third) + k]
                    squares[index % slots, k * 48:(k + 1) * 48, :] = block.astype(F32)
                flight.append(copies(index, chunk, far, b, e))
                each(flight[index], False)
    for pairs in flight[-slots:]:
        each(pairs, True)


def sds(*shape, dtype=BF16):
    return jax.ShapeDtypeStruct(shape, dtype)


SCALARS = pl.BlockSpec(memory_space=pltpu.SMEM)
LOCAL = pl.BlockSpec(memory_space=pltpu.VMEM)
REMOTE = pl.BlockSpec(memory_space=pl.ANY)
DISTANT = pl.BlockSpec(memory_space=pltpu.HBM)


COST = pl.CostEstimate(flops=2_000_000_000, bytes_accessed=1, transcendentals=0)
HEAVY = pl.CostEstimate(flops=8_000_000_000, bytes_accessed=10_000_000, transcendentals=0)
LIGHT = ("split_kernel", "far_kernel", "join_kernel", "vectors_kernel", "rows_kernel")


LIMITS = {
    "attend_second_kernel": 8,
    "feed_back_second_kernel": 9,
    "feed_back_first_kernel": 11,
}


def run(kernel, scalars, arrays, outs, scratch, *fixed):
    name = kernel.__name__
    flat = [part for a in arrays for part in (a if isinstance(a, tuple) else (a,))]

    def grouped(*refs):
        refs = list(refs)
        ins = [refs.pop(0) for _ in scalars]
        for a in arrays:
            parts = [refs.pop(0) for _ in (a if isinstance(a, tuple) else (a,))]
            ins.append(Rows(*parts) if isinstance(a, tuple) else parts[0])
        kernel(*fixed, *ins, *refs)

    return pl.pallas_call(
        grouped,
        out_shape=list(outs),
        in_specs=[SCALARS] * len(scalars) + [LOCAL] * len(flat),
        out_specs=[LOCAL] * len(outs),
        scratch_shapes=scratch,
        compiler_params=pltpu.CompilerParams(vmem_limit_bytes=LIMITS.get(name, 6) * 2**20),
        cost_estimate=COST if name in LIGHT else HEAVY,
        name=name,
    )(*scalars, *flat)


WIDE = (D, 1152)


def attend_outs(docs):
    rows = DOC * len(docs)
    return [sds(rows, 1152), sds(len(docs), 3, DOC, 2 * DOC), sds(rows, PIECE), sds(rows, D)]


def stats(docs):
    return sds(DOC * len(docs), 128, dtype=F32)


def attend_first(ids, own, other, weights):
    docs = GROUPS[0]
    outs = [sds(ROWS, D), sds(*WIDE), sds(PIECE, D)] + attend_outs(docs)
    x, wide, proj, *one = pl.pallas_call(
        functools.partial(attend_first_kernel, docs),
        out_shape=outs,
        in_specs=[SCALARS, LOCAL] + [DISTANT] * 3,
        out_specs=[LOCAL] * len(outs),
        scratch_shapes=[pltpu.SemaphoreType.DMA((5,))],
        compiler_params=pltpu.CompilerParams(vmem_limit_bytes=44 * 2**20),
        cost_estimate=HEAVY,
        name="attend_first_kernel",
    )(ids, other, own, weights[0], weights[1])
    docs = GROUPS[1]
    two = run(attend_more_kernel, [ids], [x, wide, proj], attend_outs(docs), [], docs)
    return x, *zip(one, two)


def attend_second(ids, first, mine, theirs, vec, own, other, weights):
    results, wide = [], weights[0]
    for g, docs in enumerate(GROUPS):
        rows = DOC * len(docs)
        outs = [sds(rows, D), sds(rows, D), stats(docs), sds(rows, D)] + attend_outs(docs)
        made = run(
            attend_second_kernel, [ids],
            [first[g], mine[g], theirs[g], vec, own, other, wide, weights[1]],
            outs + ([sds(*WIDE)] if g == 0 else []), [pltpu.VMEM((ROWS, D), BF16)], docs, 2,
        )
        if g == 0:
            *made, wide = made
        results.append(made)
    return tuple(zip(*results))


def feed(base, x, mine, theirs, vec, weights):
    results = []
    for g, docs in enumerate(GROUPS):
        rows = DOC * len(docs)
        split_x = isinstance(x, tuple)
        results.append(run(
            feed_kernel, [],
            [x[g] if split_x else x, mine[g], theirs[g], vec, weights[2], weights[3]],
            [sds(rows, D, dtype=F32), sds(rows, D), sds(rows, D), stats(docs),
             sds(rows, HIDDEN), sds(rows, HIDDEN), sds(rows, D)],
            [], docs, 0 if split_x else docs[0], base,
        ))
    return tuple(zip(*results))


FEED_BACK_OUTS = [
    sds(ROWS, D, dtype=F32), sds(ROWS, D), sds(8, D, dtype=F32), sds(ROWS, HIDDEN), sds(ROWS, D),
]


def feed_back_second(ids, first, mine, theirs, vec, own, other, slope, weights):
    return run(
        feed_back_second_kernel, [ids],
        [first, mine, theirs, vec, own, other, slope, weights[2], weights[3]],
        [sds(HALF, D)] + FEED_BACK_OUTS,
        [pltpu.VMEM((ROWS, D), BF16), pltpu.VMEM((ROWS, D), BF16)], 6,
    )


def feed_back_first(ids, normed, inv, vec, own, other, resid, mine, theirs, slope, weights):
    return run(
        feed_back_first_kernel, [ids],
        [normed, inv, vec, own, other, resid, mine, theirs, slope, weights[2], weights[3]],
        [sds(HALF, D, dtype=F32)] + FEED_BACK_OUTS,
        [pltpu.VMEM((ROWS, D), BF16), pltpu.VMEM((ROWS, D), F32)], 2,
    )


def attend_back(base, ids, gs, mine, theirs, normed, inv, qkv, prob, vec, weights):
    return run(
        attend_back_kernel, [ids],
        [gs, mine, theirs, normed, inv, vec, qkv, prob, weights[0], weights[1]],
        [sds(ROWS, D, dtype=F32), sds(ROWS, D), sds(8, D, dtype=F32), sds(ROWS, 1152), sds(ROWS, D),
         sds(HALF if base == 0 else 16, D)],
        [pltpu.VMEM((ROWS, PIECE), BF16), pltpu.VMEM(WIDE, BF16)], base,
    )


SPLIT_OUTS = [sds(32, *BLOCK), sds(32, *BLOCK)]
BLOCKS = pltpu.VMEM((4, 2, 8) + BLOCK, BF16)


def out_grad(chunk, ids, act, gs_low):
    return run(out_grad_kernel, [ids], [act, gs_low], SPLIT_OUTS, [BLOCKS], chunk)


def in_grad(chunk, ids, low, grad_pre):
    return run(in_grad_kernel, [ids], [low, grad_pre], SPLIT_OUTS, [BLOCKS], chunk)


def attend_grad(chunk, ids, x, grad_qkv, ctx, low, norms=()):
    outs = SPLIT_OUTS
    if norms:
        outs = [sds(33, *BLOCK), sds(32, *BLOCK), sds(8, D, dtype=F32)]
    return run(
        attend_grad_kernel, [ids], [x, grad_qkv, ctx, low, *norms], outs, [BLOCKS], chunk
    )


def vectors(rows):
    return run(vectors_kernel, [], rows, [sds(8, D, dtype=F32)], [])[0]


def split(sources, norm=None):
    arrays = [a for pair in sources for a in pair]
    sizes = tuple(keep.shape[0] // 2 for keep, _ in sources)
    count = sum(sizes)
    outs = [sds(count + (norm is not None), *BLOCK), sds(count, *BLOCK)]
    if norm is not None:
        arrays, outs = arrays + [norm], outs + [sds(8, D, dtype=F32)]
    return run(split_kernel, [], arrays, outs, [], sizes, int(norm is not None))


def far_add(keep, got, norm=None):
    if norm is None:
        return run(far_kernel, [], [keep, got], [sds(*keep.shape)], [], 0)
    count = keep.shape[0] - keep.shape[0] % 8
    outs = [sds(count + 1, *BLOCK), sds(8, D, dtype=F32)]
    return run(far_kernel, [], [keep, got, norm], outs, [], 1)


def join(held, got, count=1):
    size = held.shape[0] // count
    return run(join_kernel, [], [held, got], [sds(2 * size, *BLOCK)] * count, [], count)


PLACED = [
    sds(HIDDEN, D, dtype=F32),
    sds(D, HIDDEN, dtype=F32),
    sds(3, D, PIECE, dtype=F32),
    sds(PIECE, D, dtype=F32),
]


def place(ids, items, values, into=()):
    return pl.pallas_call(
        functools.partial(place_kernel, tuple(items)),
        out_shape=PLACED,
        in_specs=[SCALARS] + [LOCAL] * len(values) + [REMOTE] * len(into),
        out_specs=[REMOTE] * 4,
        scratch_shapes=[pltpu.VMEM((6, PIECE, PIECE), F32), pltpu.SemaphoreType.DMA((6,))],
        input_output_aliases={1 + len(values) + i: i for i in range(len(into))},
        compiler_params=pltpu.CompilerParams(vmem_limit_bytes=6 * 2**20),
        cost_estimate=COST,
        name="place_kernel",
    )(ids, *values, *into)


def swap(value):
    if isinstance(value, tuple):
        one, two = [swap(part) for part in value]
        return lax.optimization_barrier((one, value[1]))[0], two
    return lax.ppermute(value, "tensor", SWAP)


def flip(chip, core, stage, axis):
    pos = [chip % 4, chip // 4 % 4, chip // 16]
    low = (core == 0) == (stage == 0)
    pos[axis] = pos[axis] ^ 1 if low else 3 - pos[axis]
    return pos[0] + 4 * pos[1] + 16 * pos[2]


def exchange(value, stage, axis):
    pairs = [
        (2 * chip + core, 2 * flip(chip, core, stage, axis) + core)
        for chip in range(64)
        for core in range(2)
    ]
    return lax.ppermute(value, ("dp", "tensor"), pairs)


class Order:
    def __init__(self):
        self.token = None

    def hold(self, value):
        if self.token is None:
            return value
        return lax.optimization_barrier((value, self.token))[0]


class Single:
    def __init__(self, order, axes, send, keep, norm=None):
        self.order, self.axes, self.keep, self.norm, self.round = order, axes, keep, norm, 0
        self.send(send, 0, 0)

    def send(self, value, stage, j):
        self.order.token = value
        self.got = exchange(value, stage, self.axes[j % 3])

    def next(self):
        self.round += 1
        got = self.order.hold(self.got)
        if self.round > 8:
            self.got = self.order.token = got
            return
        if self.round < 3:
            value, self.keep, *norm = split([(self.keep, got)], self.norm)
            self.send(value, 0, self.round)
        elif self.round < 6:
            self.keep, *norm = far_add(self.keep, got, self.norm)
            self.send(self.keep, 1, self.round)
        elif self.round == 6:
            self.keep, *norm = far_add(self.keep, got, self.norm)
            if norm:
                self.keep = self.keep[:8]
            self.send(self.keep, 0, 2)
        else:
            norm = ()
            self.keep = join(self.keep, got)[0]
            self.send(self.keep, 0, 8 - self.round)
        if norm:
            self.norm = norm[0]


class Pair:
    def __init__(self, order, axes):
        self.order, self.axes = order, axes
        self.keep, self.got, self.calls = [None, None], [None, None], [0, 0]
        self.both = 2

    def start(self, i, send, keep):
        self.keep[i] = keep
        self.send(i, send, 0)

    def send(self, i, value, j):
        self.order.token = value
        self.got[i] = exchange(value, 0, self.axes[i ^ j])

    def next(self, i):
        self.calls[i] += 1
        if self.calls[i] == 1:
            value, self.keep[i] = split([(self.keep[i], self.order.hold(self.got[i]))])
            self.send(i, value, 1)
        elif self.calls[i] == 2 and self.calls[1 - i] == 2:
            got = [self.order.hold(g) for g in self.got]
            value, self.held = split([(self.keep[0], got[0]), (self.keep[1], got[1])])
            self.order.token = value
            self.arrived = exchange(value, 0, self.axes[2])
        elif self.calls[i] == 3:
            self.keep[i] = join(self.keep[i], self.order.hold(self.got[i]))[0]
            self.send(i, self.keep[i], 0)
        elif self.calls[i] == 4:
            self.got[i] = self.order.token = self.order.hold(self.got[i])

    def next_both(self):
        got = self.order.hold(self.arrived)
        self.both += 1
        if self.both <= 6:
            self.held = far_add(self.held, got)[0]
            self.order.token = self.held
            if self.both < 6:
                self.arrived = exchange(self.held, 1, self.axes[self.both - 3])
            else:
                self.arrived = exchange(self.held, 0, self.axes[2])
        else:
            self.keep = list(join(self.held, got, 2))
            for i in range(2):
                self.send(i, self.keep[i], 1)


UPPER_PAIR, UPPER_LAST = (0, 2, 1), (1, 2, 0)
LOWER_PAIR, LOWER_LAST = (2, 1, 0), (0, 2, 1)
CHUNK_AXES = [
    UPPER_PAIR,
    (UPPER_PAIR[1], UPPER_PAIR[0], UPPER_PAIR[2]),
    UPPER_LAST,
    LOWER_PAIR,
    (LOWER_PAIR[1], LOWER_PAIR[0], LOWER_PAIR[2]),
    LOWER_LAST,
]
TAIL = (
    "Um", "Lq", "Lp", "Ub", "Lb", "Lq", "Um", "Ub", "Lp", "Lb", "Ub", "Um", "Lb",
    "Lm", "Ub", "Up", "Lb", "Lm", "Uq", "Ub", "Lb", "Lm", "Up", "Lb", "Ub", "Lm",
    "Lb", "Uq", "Lm", "Lb", "Ub", "Lq", "Lp", "Lb",
)


def on_device(
    tokens,
    skip_tokens,
    cot_back,
    cot_head,
    one_span,
    *params,
):
    lower = [params[i] for i in (0, 1, 4, 5)]
    upper = [params[i] for i in (8, 9, 12, 13)]
    device = lax.axis_index("dp") * 2 + lax.axis_index("tensor")
    ids = jnp.concatenate([device.astype(jnp.int32).reshape(1), one_span])
    tokens_other = swap(tokens)
    tokens, ids = lax.optimization_barrier((tokens, ids))
    vec = vectors([params[i] for i in (2, 3, 6, 7, 10, 11, 14, 15)])
    skip_other = swap(skip_tokens)
    cot_head_other = swap(cot_head)
    cot_back_other = swap(cot_back)
    order = Order()

    x_l, qkv_l, prob_l, ctx_l, part = attend_first(ids, tokens, tokens_other, lower)
    first_l, low_l, normed_al, inv_al, act_l, slope_l, part = feed(
        0, x_l, part, swap(part), vec, lower
    )
    x_u, normed_fl, inv_fl, backs, qkv_u, prob_u, ctx_u, part = attend_second(
        ids, first_l, part, swap(part), vec, skip_tokens, skip_other, upper
    )
    first_u, low_u, normed_au, inv_au, act_u, slope_u, part = feed(
        4, x_u, part, swap(part), vec, upper
    )
    head_out, gs_u, gs_low_u, norms_fu, grad_pre_u, part = feed_back_second(
        ids, first_u, part, swap(part), vec, cot_head, cot_head_other, slope_u, upper
    )
    pair_u, pair_l = Pair(order, UPPER_PAIR), Pair(order, LOWER_PAIR)
    theirs = swap(part)
    pair_u.start(0, *out_grad(0, ids, act_u, gs_low_u))
    pair_u.start(1, *in_grad(1, ids, low_u, order.hold(grad_pre_u)))
    resid_u, gr_low_u, norms_au, grad_qkv_u, part, _ = attend_back(
        4, ids, order.hold(gs_u), part, theirs, normed_au, inv_au, qkv_u, prob_u, vec=vec,
        weights=upper,
    )
    theirs = swap(part)
    at_u = Single(
        order, UPPER_LAST, *attend_grad(2, ids, x_u, grad_qkv_u, ctx_u, order.hold(gr_low_u))
    )
    pair_u.next(0)
    pair_u.next(1)
    grad_skip, gs_l, gs_low_l, norms_fl, grad_pre_l, part = feed_back_first(
        ids, normed_fl, inv_fl, vec, cot_back, cot_back_other, order.hold(resid_u), part,
        theirs, slope_l, lower,
    )
    theirs = swap(part)
    order.token = gs_low_l
    pair_u.next(0)
    pair_u.next(1)
    pair_l.start(0, *out_grad(3, ids, act_l, order.hold(gs_low_l)))
    pair_l.start(1, *in_grad(4, ids, low_l, order.hold(grad_pre_l)))
    at_u.next()
    pair_u.next_both()
    resid_l, gr_low_l, norms_al, grad_qkv_l, part, away = attend_back(
        0, ids, order.hold(gs_l), part, theirs, normed_al, inv_al, qkv_l, prob_l, vec=vec,
        weights=lower,
    )
    order.token = gr_low_l
    pair_u.next_both()
    at_u.next()
    at_l = Single(
        order, LOWER_LAST,
        *attend_grad(
            5, ids, x_l, grad_qkv_l, ctx_l, order.hold(gr_low_l), (norms_al, norms_fl, norms_au, norms_fu)
        ),
    )
    act = {
        "Up": lambda: pair_u.next(0),
        "Uq": lambda: pair_u.next(1),
        "Um": pair_u.next_both,
        "Ub": at_u.next,
        "Lp": lambda: pair_l.next(0),
        "Lq": lambda: pair_l.next(1),
        "Lm": pair_l.next_both,
        "Lb": at_l.next,
    }
    for name in TAIL:
        act[name]()
    away = swap(order.hold(away))
    done_u = place(
        ids,
        [(0, 0), (0, 1), (1, 0), (1, 1), (2, 0), (2, 1)],
        [pair_u.keep[0], pair_u.got[0], pair_u.keep[1], pair_u.got[1], at_u.keep,
         order.hold(at_u.got)],
    )
    order.token = done_u[0]
    done_l = place(
        ids, [(3, 0), (4, 0), (5, 0)],
        [pair_l.keep[0], pair_l.keep[1], order.hold(at_l.keep)],
    )
    grad_tokens, back_out = run(
        rows_kernel, [ids], [resid_l, part, lax.optimization_barrier((away, done_l[0]))[0], backs],
        [sds(HALF, D, dtype=F32), sds(HALF, D)], [pltpu.VMEM((ROWS, D), BF16)],
    )
    for chunk, got in ((5, at_l.got), (4, pair_l.got[1]), (3, pair_l.got[0])):
        done_l = place(ids, [(chunk, 1)], [got], done_l)
    norms = at_l.norm
    out_gu, in_gu, qkv_gu, proj_gu = done_u
    out_gl, in_gl, qkv_gl, proj_gl = done_l
    return (
        back_out,
        head_out,
        grad_tokens,
        grad_skip,
        qkv_gl,
        proj_gl,
        norms[0],
        norms[1],
        in_gl,
        out_gl,
        norms[2],
        norms[3],
        qkv_gu,
        proj_gu,
        norms[4],
        norms[5],
        in_gu,
        out_gu,
        norms[6],
        norms[7],
    )


def solution(mesh):
    rows = P(("dp", "tensor"), None)
    weights = (
        P(None, None, "tensor"),
        P("tensor", None),
        P(),
        P(),
        P(None, "tensor"),
        P("tensor", None),
        P(),
        P(),
    )
    return jax.shard_map(
        on_device,
        mesh=mesh,
        in_specs=(rows,) * 4 + (P("dp"),) + weights + weights,
        out_specs=(rows,) * 4 + weights + weights,
        check_vma=False,
    )
```

```python
import functools

import jax
import jax.numpy as jnp
from jax import lax
from jax.experimental import pallas as pl
from jax.experimental.pallas import tpu as pltpu
from jax.sharding import PartitionSpec as P

SPAN = 128
EPS = 1e-06
SCALE = 0.125
NEG = -1000000000.0

D = 768
ROWS = 768
HALF = ROWS // 2
HIDDEN = 1536
PIECE = 384
PAIR = 128
BLOCK = (48, 384)
F32 = jnp.float32
BF16 = jnp.bfloat16
SPANS_AT = 1

SWAP = [(0, 1), (1, 0)]


def dot_nn(left, right):
    return lax.dot_general(left, right, (((1,), (0,)), ((), ())), preferred_element_type=F32)


def dot_nt(left, right):
    return lax.dot_general(left, right, (((1,), (1,)), ((), ())), preferred_element_type=F32)


def dot_tn(left, right):
    return lax.dot_general(left, right, (((0,), (0,)), ((), ())), preferred_element_type=F32)


def normalize(resid):
    mean = jnp.mean(resid, axis=-1, keepdims=True)
    centered = resid - mean
    var = jnp.mean(centered * centered, axis=-1, keepdims=True)
    inv = lax.rsqrt(var + EPS)
    return centered * inv, inv


def norm_grad(grad_out, normed, inv, gain):
    grad = grad_out * gain
    first = jnp.mean(grad, axis=-1, keepdims=True)
    second = jnp.mean(grad * normed, axis=-1, keepdims=True)
    return inv * (grad - first - normed * second)


def fold(value):
    return jnp.sum(value.reshape(-1, 8, value.shape[-1]), axis=0)

DOC = 2 * SPAN
DOCS = ROWS // DOC


def side_of(ids_ref):
    return ids_ref[0] & 1


def chunk_bits(ids_ref, chunk):
    chip, core = ids_ref[0] >> 1, ids_ref[0] & 1
    bits = []
    for axis in CHUNK_AXES[chunk]:
        at = (chip >> (2 * axis)) & 3
        low, high = (at ^ (at >> 1)) & 1, at >> 1
        bits.append(low + core * (high - low))
    return bits


def doc_rows(doc):
    return slice(doc * DOC, (doc + 1) * DOC)


def half_rows(index):
    return pl.ds(pl.multiple_of(index * HALF, HALF), HALF)


def join_halves(side, own_ref, other_ref, full_ref):
    full_ref[half_rows(side), :] = own_ref[...]
    full_ref[half_rows(1 - side), :] = other_ref[...]


def doc_masks(ids_ref, doc):
    row = lax.broadcasted_iota(jnp.int32, (DOC, 1), 0)
    keep = jnp.where((row < SPAN) | (ids_ref[SPANS_AT + doc] == 0), 1.0, 0.0)
    return keep, (row & (SPAN - 1)) == 0


def spread(column):
    return jnp.broadcast_to(column, (column.shape[0], 128))


def head_masks():
    lane = lax.broadcasted_iota(jnp.int32, (1, PAIR), 1)
    return lane < 64


def both_heads(value, left):
    zero = jnp.zeros_like(value)
    return jnp.concatenate([jnp.where(left, value, zero), jnp.where(left, zero, value)], axis=0)


class Rows:
    def __init__(self, *refs):
        self.refs = refs

    def find(self, index):
        head = index[0] if isinstance(index, tuple) else index
        rest = index[1:] if isinstance(index, tuple) else ()
        at = head if isinstance(head, int) else head.start
        base = 0
        for ref in self.refs:
            if at < base + ref.shape[0]:
                break
            base += ref.shape[0]
        head = head - base if isinstance(head, int) else slice(at - base, head.stop - base)
        return ref, (head, *rest)

    def __getitem__(self, index):
        head = index[0] if isinstance(index, tuple) else index
        if head is Ellipsis or head == slice(None):
            return jnp.concatenate([ref[index] for ref in self.refs], axis=0)
        ref, index = self.find(index)
        return ref[index]


GROUPS = ((0, 1), (2,))


def attend(ids_ref, docs, x_ref, proj_ref, qkv_ref, prob_ref, ctx_ref, part_ref, wide, skip=0):
    for i, doc in enumerate(docs):
        at = doc_rows(i)
        out = dot_nn(x_ref[doc_rows(i + skip), :], wide[...])
        qkv_ref[at, :384] = (out[:, :384] * SCALE).astype(BF16)
        qkv_ref[at, 384:] = out[:, 384:].astype(BF16)
    left = head_masks()
    col = lax.broadcasted_iota(jnp.int32, (1, 2 * DOC), 1) & (DOC - 1)
    for i, doc in enumerate(docs):
        at = doc_rows(i)
        key_ok = (col < SPAN) | (ids_ref[SPANS_AT + doc] == 0)
        scores = []
        for pair in range(3):
            query = qkv_ref[at, pair * PAIR:(pair + 1) * PAIR]
            keys = qkv_ref[at, 384 + pair * PAIR:384 + (pair + 1) * PAIR]
            scores.append(jnp.where(key_ok, dot_nt(query, both_heads(keys, left)), NEG))
        for pair in range(3):
            probs = []
            for head in range(2):
                score = scores[pair][:, head * DOC:(head + 1) * DOC]
                raised = jnp.exp(score - jnp.max(score, axis=-1, keepdims=True))
                probs.append(
                    (raised * (1.0 / jnp.sum(raised, axis=-1, keepdims=True))).astype(BF16)
                )
            prob = jnp.concatenate(probs, axis=1)
            prob_ref[i, pair] = prob
            values = qkv_ref[at, 768 + pair * PAIR:768 + (pair + 1) * PAIR]
            mixed = dot_nn(prob, both_heads(values, left))
            ctx_ref[at, pair * PAIR:(pair + 1) * PAIR] = mixed.astype(BF16)
    for i, doc in enumerate(docs):
        at = doc_rows(i)
        part_ref[at, :] = dot_nn(ctx_ref[at, :], proj_ref[...]).astype(BF16)


def attend_first_kernel(
    docs, ids_ref, other_ref, own_ref, qkv_w_ref, proj_w_ref,
    x_ref, wide, proj, qkv_ref, prob_ref, ctx_ref, part_ref, sems,
):
    side = side_of(ids_ref)
    copies = [pltpu.make_async_copy(own_ref, x_ref.at[half_rows(side), :], sems.at[0])]
    for index in range(3):
        cut = slice(index * 384, (index + 1) * 384)
        copies.append(
            pltpu.make_async_copy(qkv_w_ref.at[index], wide.at[:, cut], sems.at[1 + index])
        )
    copies.append(pltpu.make_async_copy(proj_w_ref, proj, sems.at[4]))
    for copy in copies:
        copy.start()
    x_ref[half_rows(1 - side), :] = other_ref[...]
    for copy in copies:
        copy.wait()
    attend(ids_ref, docs, x_ref, proj, qkv_ref, prob_ref, ctx_ref, part_ref, wide)


def attend_more_kernel(
    docs, ids_ref, x_ref, wide_ref, proj_ref, qkv_ref, prob_ref, ctx_ref, part_ref,
):
    attend(
        ids_ref, docs, x_ref, proj_ref, qkv_ref, prob_ref, ctx_ref, part_ref, wide_ref, docs[0]
    )


def attend_second_kernel(
    docs, base, ids_ref, first_ref, mine_ref, theirs_ref, vec_ref, own_ref, other_ref,
    qkv_w_ref, proj_ref,
    x_ref, normed_ref, inv_ref, back_ref, qkv_ref, prob_ref, ctx_ref, part_ref, *rest,
):
    *wide_out, full = rest
    join_halves(side_of(ids_ref), own_ref, other_ref, full)
    for i, doc in enumerate(docs):
        at = doc_rows(i)
        keep, cls = doc_masks(ids_ref, doc)
        resid = first_ref[at, :] + mine_ref[at, :].astype(F32) + theirs_ref[at, :].astype(F32)
        normed, inv = normalize(resid)
        back = normed * vec_ref[base:base + 1, :] + vec_ref[base + 1:base + 2, :]
        normed_ref[at, :] = normed.astype(BF16)
        inv_ref[at, :] = spread(inv)
        x_ref[at, :] = jnp.where(cls, back, full[doc_rows(doc), :].astype(F32)).astype(BF16)
        back_ref[at, :] = (back * keep).astype(BF16)
    wide = qkv_w_ref
    if wide_out:
        wide = wide_out[0]
        for index in range(3):
            wide[:, index * 384:(index + 1) * 384] = qkv_w_ref[index]
    attend(ids_ref, docs, x_ref, proj_ref, qkv_ref, prob_ref, ctx_ref, part_ref, wide)


def feed_kernel(
    docs, skip, base, x_ref, mine_ref, theirs_ref, vec_ref, in_ref, out_w_ref,
    first_ref, low_ref, normed_ref, inv_ref, act_ref, slope_ref, part_ref,
):
    for i, doc in enumerate(docs):
        at = doc_rows(i)
        resid = x_ref[doc_rows(i + skip), :].astype(F32) + mine_ref[at, :].astype(F32)
        resid = resid + theirs_ref[at, :].astype(F32)
        normed, inv = normalize(resid)
        first = normed * vec_ref[base:base + 1, :] + vec_ref[base + 1:base + 2, :]
        normed_ref[at, :] = normed.astype(BF16)
        inv_ref[at, :] = spread(inv)
        first_ref[at, :] = first
        low_ref[at, :] = first.astype(BF16)
    for i, doc in enumerate(docs):
        at = doc_rows(i)
        for piece in range(3):
            cut = slice(piece * 512, (piece + 1) * 512)
            pre = dot_nn(low_ref[at, :], in_ref[:, cut])
            share = 0.5 * (1.0 + lax.erf(pre * 0.7071067811865476))
            density = jnp.exp(-0.5 * pre * pre) * 0.3989422804014327
            act_ref[at, cut] = (pre * share).astype(BF16)
            slope_ref[at, cut] = (share + pre * density).astype(BF16)
    for i, doc in enumerate(docs):
        at = doc_rows(i)
        part_ref[at, :] = dot_nn(act_ref[at, :], out_w_ref[...]).astype(BF16)


def feed_back(gs_low_ref, slope_ref, in_ref, out_w_ref, grad_pre_ref, part_ref):
    for doc in range(DOCS):
        at = doc_rows(doc)
        for piece in range(3):
            cut = slice(piece * 512, (piece + 1) * 512)
            grad_act = dot_nt(gs_low_ref[at, :], out_w_ref[cut, :])
            grad_pre_ref[at, cut] = (grad_act * slope_ref[at, cut].astype(F32)).astype(BF16)
    for doc in range(DOCS):
        at = doc_rows(doc)
        part_ref[at, :] = dot_nt(grad_pre_ref[at, :], in_ref[...]).astype(BF16)


def put_norm_grads(norms_ref, sums):
    gain, shift = sums
    norms_ref[...] = jnp.zeros_like(norms_ref)
    norms_ref[0:1, :] = jnp.sum(gain, axis=0, keepdims=True)
    norms_ref[1:2, :] = jnp.sum(shift, axis=0, keepdims=True)


def add_sums(sums, grad_out, normed):
    new = (fold(grad_out * normed), fold(grad_out))
    return new if sums is None else (sums[0] + new[0], sums[1] + new[1])


def feed_back_second_kernel(
    base, ids_ref, first_ref, mine_ref, theirs_ref, vec_ref, own_ref, other_ref,
    slope_ref, in_ref, out_w_ref,
    head_ref, gs_ref, gs_low_ref, norms_ref, grad_pre_ref, part_ref, cot, full,
):
    side = side_of(ids_ref)
    join_halves(side, own_ref, other_ref, cot)
    sums = None
    for doc in range(DOCS):
        at = doc_rows(doc)
        keep, _ = doc_masks(ids_ref, doc)
        resid = first_ref[at, :] + mine_ref[at, :].astype(F32) + theirs_ref[at, :].astype(F32)
        normed, inv = normalize(resid)
        head = normed * vec_ref[base:base + 1, :] + vec_ref[base + 1:base + 2, :]
        full[at, :] = (head * keep).astype(BF16)
        grad_out = cot[at, :].astype(F32) * keep
        grad = norm_grad(grad_out, normed, inv, vec_ref[base:base + 1, :])
        gs_ref[at, :] = grad
        gs_low_ref[at, :] = grad.astype(BF16)
        sums = add_sums(sums, grad_out, normed)
    head_ref[...] = full[half_rows(side), :]
    put_norm_grads(norms_ref, sums)
    feed_back(gs_low_ref, slope_ref, in_ref, out_w_ref, grad_pre_ref, part_ref)


def feed_back_first_kernel(
    base, ids_ref, normed_ref, inv_ref, vec_ref, own_ref, other_ref,
    resid_ref, mine_ref, theirs_ref, slope_ref, in_ref, out_w_ref,
    skip_ref, gs_ref, gs_low_ref, norms_ref, grad_pre_ref, part_ref, cot, full,
):
    side = side_of(ids_ref)
    join_halves(side, own_ref, other_ref, cot)
    sums = None
    for doc in range(DOCS):
        at = doc_rows(doc)
        keep, cls = doc_masks(ids_ref, doc)
        above = resid_ref[at, :] + mine_ref[at, :].astype(F32) + theirs_ref[at, :].astype(F32)
        full[at, :] = jnp.where(cls, 0.0, above)
        normed = normed_ref[at, :].astype(F32)
        grad_out = cot[at, :].astype(F32) * keep + jnp.where(cls, above, 0.0)
        grad = norm_grad(grad_out, normed, inv_ref[at, 0:1], vec_ref[base:base + 1, :])
        gs_ref[at, :] = grad
        gs_low_ref[at, :] = grad.astype(BF16)
        sums = add_sums(sums, grad_out, normed)
    skip_ref[...] = full[half_rows(side), :]
    put_norm_grads(norms_ref, sums)
    feed_back(gs_low_ref, slope_ref, in_ref, out_w_ref, grad_pre_ref, part_ref)


def attend_back_kernel(
    base, ids_ref, gs_ref, mine_ref, theirs_ref, normed_ref, inv_ref, vec_ref, qkv_ref, prob_ref,
    qkv_w_ref, proj_ref,
    resid_ref, low_ref, norms_ref, grad_qkv_ref, part_ref, away_ref, grad_ctx, wide,
):
    for index in range(3):
        wide[:, index * 384:(index + 1) * 384] = qkv_w_ref[index]
    sums = None
    for doc in range(DOCS):
        at = doc_rows(doc)
        grad_out = gs_ref[at, :] + mine_ref[at, :].astype(F32) + theirs_ref[at, :].astype(F32)
        normed = normed_ref[at, :].astype(F32)
        grad = norm_grad(grad_out, normed, inv_ref[at, 0:1], vec_ref[base:base + 1, :])
        resid_ref[at, :] = grad
        low_ref[at, :] = grad.astype(BF16)
        sums = add_sums(sums, grad_out, normed)
    put_norm_grads(norms_ref, sums)
    for doc in range(DOCS):
        at = doc_rows(doc)
        grad_ctx[at, :] = dot_nt(low_ref[at, :], proj_ref[...]).astype(BF16)
    left = head_masks()
    for doc in range(DOCS):
        at = doc_rows(doc)
        pairs = [slice(pair * PAIR, (pair + 1) * PAIR) for pair in range(3)]
        grad_probs = []
        for pair in range(3):
            values = qkv_ref[at, 768 + pair * PAIR:768 + (pair + 1) * PAIR]
            grad_probs.append(dot_nt(grad_ctx[at, pairs[pair]], both_heads(values, left)))
        for pair in range(3):
            prob_low = prob_ref[doc, pair]
            scored = []
            for head in range(2):
                cut = slice(head * DOC, (head + 1) * DOC)
                prob = prob_low[:, cut].astype(F32)
                grad_prob = grad_probs[pair][:, cut]
                inner = jnp.sum(grad_prob * prob, axis=-1, keepdims=True)
                scored.append((prob * (grad_prob - inner)).astype(BF16))
            grad_scores = jnp.concatenate(scored, axis=1)
            query = qkv_ref[at, pairs[pair]]
            keys = qkv_ref[at, 384 + pair * PAIR:384 + (pair + 1) * PAIR]
            grad_query = dot_nn(grad_scores, both_heads(keys, left)) * SCALE
            grad_keys = dot_tn(grad_scores, query)
            grad_values = dot_tn(prob_low, grad_ctx[at, pairs[pair]])
            grad_qkv_ref[at, pair * PAIR:(pair + 1) * PAIR] = grad_query.astype(BF16)
            for index, grad in ((1, grad_keys), (2, grad_values)):
                cut = slice(index * 384 + pair * PAIR, index * 384 + (pair + 1) * PAIR)
                grad_qkv_ref[at, cut] = jnp.where(left, grad[:DOC], grad[DOC:]).astype(BF16)
    for doc in range(DOCS):
        at = doc_rows(doc)
        part_ref[at, :] = dot_nt(grad_qkv_ref[at, :], wide[...]).astype(BF16)
    if base == 0:
        away_ref[...] = part_ref[half_rows(1 - side_of(ids_ref)), :]
    else:
        away_ref[...] = jnp.zeros_like(away_ref)


def rows_kernel(ids_ref, resid_ref, mine_ref, theirs_ref, back_ref, out_ref, back_out_ref, full):
    at = half_rows(side_of(ids_ref))
    out_ref[...] = resid_ref[at, :] + mine_ref[at, :].astype(F32) + theirs_ref[...].astype(F32)
    full[...] = back_ref[...]
    back_out_ref[...] = full[at, :]


def cut_wide(value, blocks, piece):
    for half in range(2):
        for k in range(8):
            blocks[piece, half, k] = value[k * 48:(k + 1) * 48, half * 384:(half + 1) * 384]


def cut_tall(value, blocks, piece):
    for half in range(2):
        for k in range(8):
            at = half * 384 + k * 48
            blocks[piece, half, k] = value[at:at + 48, :]


def put_blocks(ids_ref, turn, blocks, send_ref, keep_ref):
    first, second, third = chunk_bits(ids_ref, turn)
    for rel, ref in ((1, send_ref), (0, keep_ref)):
        for b in range(2):
            piece = 2 * (rel ^ first) + (b ^ second)
            for e in range(2):
                for k in range(8):
                    ref[16 * b + 8 * e + k] = blocks[piece, e ^ third, k]


def out_grad_kernel(turn, ids_ref, act_ref, gs_ref, send_ref, keep_ref, blocks):
    for p in range(2):
        value = dot_tn(act_ref[:, p * 768:(p + 1) * 768], gs_ref[...]).astype(BF16)
        cut_wide(value[:384], blocks, 2 * p)
        cut_wide(value[384:], blocks, 2 * p + 1)
    put_blocks(ids_ref, turn, blocks, send_ref, keep_ref)


def in_grad_kernel(turn, ids_ref, low_ref, grad_ref, send_ref, keep_ref, blocks):
    for p in range(2):
        value = dot_tn(low_ref[...], grad_ref[:, p * 768:(p + 1) * 768]).astype(BF16)
        cut_tall(value[:, :384], blocks, 2 * p)
        cut_tall(value[:, 384:], blocks, 2 * p + 1)
    put_blocks(ids_ref, turn, blocks, send_ref, keep_ref)


def attend_grad_kernel(turn, ids_ref, x_ref, grad_ref, ctx_ref, low_ref, *refs):
    norm_refs, (send_ref, keep_ref), blocks = refs[:-3 - (len(refs) > 3)], refs[-3:-1], refs[-1]
    if norm_refs:
        send_ref, keep_ref = refs[-4:-2]
        value = jnp.concatenate([ref[0:2, :] for ref in norm_refs], axis=0)
        refs[-2][...] = value
        send_ref[32] = norm_block(value)
    value = dot_tn(x_ref[...], grad_ref[...]).astype(BF16)
    for piece in range(3):
        cut_tall(value[:, piece * 384:(piece + 1) * 384], blocks, piece)
    cut_wide(dot_tn(ctx_ref[...], low_ref[...]).astype(BF16), blocks, 3)
    put_blocks(ids_ref, turn, blocks, send_ref, keep_ref)


def vectors_kernel(*refs):
    out_ref = refs[-1]
    for i in range(8):
        out_ref[i:i + 1, :] = refs[i][...].reshape(1, D)


def plus(one, two):
    return (one.astype(F32) + two.astype(F32)).astype(BF16)


def norm_block(value):
    high = value.astype(BF16)
    low = (value - high.astype(F32)).astype(BF16)
    rows = [high[:, :PIECE], high[:, PIECE:], low[:, :PIECE], low[:, PIECE:]]
    return jnp.concatenate(rows + [jnp.zeros((16, PIECE), BF16)], axis=0)


def block_norm(block):
    high = jnp.concatenate([block[0:8], block[8:16]], axis=1)
    low = jnp.concatenate([block[16:24], block[24:32]], axis=1)
    return high.astype(F32) + low.astype(F32)


def add_norm(value, block):
    return block_norm(norm_block(value)) + block_norm(block)


def split_kernel(sizes, with_norm, *refs):
    count = len(sizes)
    ins, outs = refs[:2 * count], refs[2 * count + with_norm:]
    at = 0
    for i, m in enumerate(sizes):
        keep, got = ins[2 * i], ins[2 * i + 1]
        outs[1][at:at + m] = plus(keep[:m], got[:m])
        outs[0][at:at + m] = plus(keep[m:], got[m:2 * m])
        at += m
    if with_norm:
        value = add_norm(refs[2 * count][...], ins[1][2 * sizes[0]])
        outs[0][at] = norm_block(value)
        outs[2][...] = value


def far_kernel(with_norm, *refs):
    if with_norm:
        keep, got, norm, out, norm_out = refs
        count = keep.shape[0] - (keep.shape[0] % 8)
        value = add_norm(norm[...], got[got.shape[0] - 1])
        out[count] = norm_block(value)
        norm_out[...] = value
    else:
        keep, got, out = refs
        count = keep.shape[0]
    out[:count] = plus(keep[:count], got[:count])


def join_kernel(count, held_ref, got_ref, *outs):
    size = outs[0].shape[0] // 2
    for i in range(count):
        at = slice(i * size, (i + 1) * size)
        outs[i][:size] = held_ref[at]
        outs[i][size:] = got_ref[at]


def place_kernel(items, ids_ref, *refs):
    ins, outs, squares, sems = refs[:len(items)], refs[-6:-2], refs[-2], refs[-1]
    slots = squares.shape[0]

    def copies(index, chunk, far, b, e):
        first, second, _ = chunk_bits(ids_ref, chunk)
        turn = chunk % 3
        slot = index % slots
        piece = 2 * (far ^ first) + (b ^ second)
        at = pl.ds(pl.multiple_of(piece * PIECE, PIECE), PIECE)
        cut = slice(e * PIECE, (e + 1) * PIECE)

        def copy(ref):
            return pltpu.make_async_copy(squares.at[slot], ref, sems.at[slot])

        if turn == 0:
            return [(None, copy(outs[0].at[at, cut]))]
        if turn == 1:
            return [(None, copy(outs[1].at[cut, at]))]
        return [
            (piece < 3, copy(outs[2].at[jnp.minimum(piece, 2), cut, :])),
            (piece == 3, copy(outs[3].at[:, cut])),
        ]

    def each(pairs, wait):
        for when, copy in pairs:
            def act(copy=copy):
                copy.wait() if wait else copy.start()

            if when is None:
                act()
            else:
                pl.when(when)(act)

    flight = []
    for (chunk, far), from_ref in zip(items, ins):
        third = chunk_bits(ids_ref, chunk)[2]
        for b in range(2):
            for e in range(2):
                index = len(flight)
                if index >= slots:
                    each(flight[index - slots], True)
                for k in range(8):
                    block = from_ref[16 * b + 8 * (e ^ third) + k]
                    squares[index % slots, k * 48:(k + 1) * 48, :] = block.astype(F32)
                flight.append(copies(index, chunk, far, b, e))
                each(flight[index], False)
    for pairs in flight[-slots:]:
        each(pairs, True)


def sds(*shape, dtype=BF16):
    return jax.ShapeDtypeStruct(shape, dtype)


SCALARS = pl.BlockSpec(memory_space=pltpu.SMEM)
LOCAL = pl.BlockSpec(memory_space=pltpu.VMEM)
REMOTE = pl.BlockSpec(memory_space=pl.ANY)
DISTANT = pl.BlockSpec(memory_space=pltpu.HBM)


COST = pl.CostEstimate(flops=2_000_000_000, bytes_accessed=1, transcendentals=0)
HEAVY = pl.CostEstimate(flops=8_000_000_000, bytes_accessed=10_000_000, transcendentals=0)
LIGHT = ("split_kernel", "far_kernel", "join_kernel", "vectors_kernel", "rows_kernel")


LIMITS = {
    "attend_second_kernel": 6,
    "feed_back_second_kernel": 7,
    "feed_back_first_kernel": 9,
    "attend_back_kernel": 6,
    "rows_kernel": 6,
}


def run(kernel, scalars, arrays, outs, scratch, *fixed):
    name = kernel.__name__
    flat = [part for a in arrays for part in (a if isinstance(a, tuple) else (a,))]

    def grouped(*refs):
        refs = list(refs)
        ins = [refs.pop(0) for _ in scalars]
        for a in arrays:
            parts = [refs.pop(0) for _ in (a if isinstance(a, tuple) else (a,))]
            ins.append(Rows(*parts) if isinstance(a, tuple) else parts[0])
        kernel(*fixed, *ins, *refs)

    return pl.pallas_call(
        grouped,
        out_shape=list(outs),
        in_specs=[SCALARS] * len(scalars) + [LOCAL] * len(flat),
        out_specs=[LOCAL] * len(outs),
        scratch_shapes=scratch,
        compiler_params=pltpu.CompilerParams(vmem_limit_bytes=LIMITS.get(name, 5) * 2**20),
        cost_estimate=COST if name in LIGHT else HEAVY,
        name=name,
    )(*scalars, *flat)


WIDE = (D, 1152)


def attend_outs(docs):
    rows = DOC * len(docs)
    return [sds(rows, 1152), sds(len(docs), 3, DOC, 2 * DOC), sds(rows, PIECE), sds(rows, D)]


def stats(docs):
    return sds(DOC * len(docs), 128, dtype=F32)


def attend_first(ids, own, other, weights):
    docs = GROUPS[0]
    outs = [sds(ROWS, D), sds(*WIDE), sds(PIECE, D)] + attend_outs(docs)
    x, wide, proj, *one = pl.pallas_call(
        functools.partial(attend_first_kernel, docs),
        out_shape=outs,
        in_specs=[SCALARS, LOCAL] + [DISTANT] * 3,
        out_specs=[LOCAL] * len(outs),
        scratch_shapes=[pltpu.SemaphoreType.DMA((5,))],
        compiler_params=pltpu.CompilerParams(vmem_limit_bytes=44 * 2**20),
        cost_estimate=HEAVY,
        name="attend_first_kernel",
    )(ids, other, own, weights[0], weights[1])
    docs = GROUPS[1]
    two = run(attend_more_kernel, [ids], [x, wide, proj], attend_outs(docs), [], docs)
    return x, *zip(one, two)


def attend_second(ids, first, mine, theirs, vec, own, other, weights):
    results, wide = [], weights[0]
    for g, docs in enumerate(GROUPS):
        rows = DOC * len(docs)
        outs = [sds(rows, D), sds(rows, D), stats(docs), sds(rows, D)] + attend_outs(docs)
        made = run(
            attend_second_kernel, [ids],
            [first[g], mine[g], theirs[g], vec, own, other, wide, weights[1]],
            outs + ([sds(*WIDE)] if g == 0 else []), [pltpu.VMEM((ROWS, D), BF16)], docs, 2,
        )
        if g == 0:
            *made, wide = made
        results.append(made)
    return tuple(zip(*results))


def feed(base, x, mine, theirs, vec, weights):
    results = []
    for g, docs in enumerate(GROUPS):
        rows = DOC * len(docs)
        split_x = isinstance(x, tuple)
        results.append(run(
            feed_kernel, [],
            [x[g] if split_x else x, mine[g], theirs[g], vec, weights[2], weights[3]],
            [sds(rows, D, dtype=F32), sds(rows, D), sds(rows, D), stats(docs),
             sds(rows, HIDDEN), sds(rows, HIDDEN), sds(rows, D)],
            [], docs, 0 if split_x else docs[0], base,
        ))
    return tuple(zip(*results))


FEED_BACK_OUTS = [
    sds(ROWS, D, dtype=F32), sds(ROWS, D), sds(8, D, dtype=F32), sds(ROWS, HIDDEN), sds(ROWS, D),
]


def feed_back_second(ids, first, mine, theirs, vec, own, other, slope, weights):
    return run(
        feed_back_second_kernel, [ids],
        [first, mine, theirs, vec, own, other, slope, weights[2], weights[3]],
        [sds(HALF, D)] + FEED_BACK_OUTS,
        [pltpu.VMEM((ROWS, D), BF16), pltpu.VMEM((ROWS, D), BF16)], 6,
    )


def feed_back_first(ids, normed, inv, vec, own, other, resid, mine, theirs, slope, weights):
    return run(
        feed_back_first_kernel, [ids],
        [normed, inv, vec, own, other, resid, mine, theirs, slope, weights[2], weights[3]],
        [sds(HALF, D, dtype=F32)] + FEED_BACK_OUTS,
        [pltpu.VMEM((ROWS, D), BF16), pltpu.VMEM((ROWS, D), F32)], 2,
    )


def attend_back(base, ids, gs, mine, theirs, normed, inv, qkv, prob, vec, weights):
    return run(
        attend_back_kernel, [ids],
        [gs, mine, theirs, normed, inv, vec, qkv, prob, weights[0], weights[1]],
        [sds(ROWS, D, dtype=F32), sds(ROWS, D), sds(8, D, dtype=F32), sds(ROWS, 1152), sds(ROWS, D),
         sds(HALF if base == 0 else 16, D)],
        [pltpu.VMEM((ROWS, PIECE), BF16), pltpu.VMEM(WIDE, BF16)], base,
    )


SPLIT_OUTS = [sds(32, *BLOCK), sds(32, *BLOCK)]
BLOCKS = pltpu.VMEM((4, 2, 8) + BLOCK, BF16)


def out_grad(chunk, ids, act, gs_low):
    return run(out_grad_kernel, [ids], [act, gs_low], SPLIT_OUTS, [BLOCKS], chunk)


def in_grad(chunk, ids, low, grad_pre):
    return run(in_grad_kernel, [ids], [low, grad_pre], SPLIT_OUTS, [BLOCKS], chunk)


def attend_grad(chunk, ids, x, grad_qkv, ctx, low, norms=()):
    outs = SPLIT_OUTS
    if norms:
        outs = [sds(33, *BLOCK), sds(32, *BLOCK), sds(8, D, dtype=F32)]
    return run(
        attend_grad_kernel, [ids], [x, grad_qkv, ctx, low, *norms], outs, [BLOCKS], chunk
    )


def vectors(rows):
    return run(vectors_kernel, [], rows, [sds(8, D, dtype=F32)], [])[0]


def split(sources, norm=None):
    arrays = [a for pair in sources for a in pair]
    sizes = tuple(keep.shape[0] // 2 for keep, _ in sources)
    count = sum(sizes)
    outs = [sds(count + (norm is not None), *BLOCK), sds(count, *BLOCK)]
    if norm is not None:
        arrays, outs = arrays + [norm], outs + [sds(8, D, dtype=F32)]
    return run(split_kernel, [], arrays, outs, [], sizes, int(norm is not None))


def far_add(keep, got, norm=None):
    if norm is None:
        return run(far_kernel, [], [keep, got], [sds(*keep.shape)], [], 0)
    count = keep.shape[0] - keep.shape[0] % 8
    outs = [sds(count + 1, *BLOCK), sds(8, D, dtype=F32)]
    return run(far_kernel, [], [keep, got, norm], outs, [], 1)


def join(held, got, count=1):
    size = held.shape[0] // count
    return run(join_kernel, [], [held, got], [sds(2 * size, *BLOCK)] * count, [], count)


PLACED = [
    sds(HIDDEN, D, dtype=F32),
    sds(D, HIDDEN, dtype=F32),
    sds(3, D, PIECE, dtype=F32),
    sds(PIECE, D, dtype=F32),
]


def place(ids, items, values, into=()):
    return pl.pallas_call(
        functools.partial(place_kernel, tuple(items)),
        out_shape=PLACED,
        in_specs=[SCALARS] + [LOCAL] * len(values) + [REMOTE] * len(into),
        out_specs=[REMOTE] * 4,
        scratch_shapes=[pltpu.VMEM((6, PIECE, PIECE), F32), pltpu.SemaphoreType.DMA((6,))],
        input_output_aliases={1 + len(values) + i: i for i in range(len(into))},
        compiler_params=pltpu.CompilerParams(vmem_limit_bytes=6 * 2**20),
        cost_estimate=COST,
        name="place_kernel",
    )(ids, *values, *into)


def swap(value):
    if isinstance(value, tuple):
        one, two = [swap(part) for part in value]
        return lax.optimization_barrier((one, value[1]))[0], two
    return lax.ppermute(value, "tensor", SWAP)


def flip(chip, core, stage, axis):
    pos = [chip % 4, chip // 4 % 4, chip // 16]
    low = (core == 0) == (stage == 0)
    pos[axis] = pos[axis] ^ 1 if low else 3 - pos[axis]
    return pos[0] + 4 * pos[1] + 16 * pos[2]


def exchange(value, stage, axis):
    pairs = [
        (2 * chip + core, 2 * flip(chip, core, stage, axis) + core)
        for chip in range(64)
        for core in range(2)
    ]
    return lax.ppermute(value, ("dp", "tensor"), pairs)


class Order:
    def __init__(self):
        self.token = None

    def hold(self, value):
        if self.token is None:
            return value
        return lax.optimization_barrier((value, self.token))[0]


class Single:
    def __init__(self, order, axes, send, keep, norm=None):
        self.order, self.axes, self.keep, self.norm, self.round = order, axes, keep, norm, 0
        self.send(send, 0, 0)

    def send(self, value, stage, j):
        self.order.token = value
        self.got = exchange(value, stage, self.axes[j % 3])

    def next(self):
        self.round += 1
        got = self.order.hold(self.got)
        if self.round > 8:
            self.got = self.order.token = got
            return
        if self.round < 3:
            value, self.keep, *norm = split([(self.keep, got)], self.norm)
            self.send(value, 0, self.round)
        elif self.round < 6:
            self.keep, *norm = far_add(self.keep, got, self.norm)
            self.send(self.keep, 1, self.round)
        elif self.round == 6:
            self.keep, *norm = far_add(self.keep, got, self.norm)
            if norm:
                self.keep = self.keep[:8]
            self.send(self.keep, 0, 2)
        else:
            norm = ()
            self.keep = join(self.keep, got)[0]
            self.send(self.keep, 0, 8 - self.round)
        if norm:
            self.norm = norm[0]


class Pair:
    def __init__(self, order, axes):
        self.order, self.axes = order, axes
        self.keep, self.got, self.calls = [None, None], [None, None], [0, 0]
        self.both = 2

    def start(self, i, send, keep):
        self.keep[i] = keep
        self.send(i, send, 0)

    def send(self, i, value, j):
        self.order.token = value
        self.got[i] = exchange(value, 0, self.axes[i ^ j])

    def next(self, i):
        self.calls[i] += 1
        if self.calls[i] == 1:
            value, self.keep[i] = split([(self.keep[i], self.order.hold(self.got[i]))])
            self.send(i, value, 1)
        elif self.calls[i] == 2 and self.calls[1 - i] == 2:
            got = [self.order.hold(g) for g in self.got]
            value, self.held = split([(self.keep[0], got[0]), (self.keep[1], got[1])])
            self.order.token = value
            self.arrived = exchange(value, 0, self.axes[2])
        elif self.calls[i] == 3:
            self.keep[i] = join(self.keep[i], self.order.hold(self.got[i]))[0]
            self.send(i, self.keep[i], 0)
        elif self.calls[i] == 4:
            self.got[i] = self.order.token = self.order.hold(self.got[i])

    def next_both(self):
        got = self.order.hold(self.arrived)
        self.both += 1
        if self.both <= 6:
            self.held = far_add(self.held, got)[0]
            self.order.token = self.held
            if self.both < 6:
                self.arrived = exchange(self.held, 1, self.axes[self.both - 3])
            else:
                self.arrived = exchange(self.held, 0, self.axes[2])
        else:
            self.keep = list(join(self.held, got, 2))
            for i in range(2):
                self.send(i, self.keep[i], 1)


UPPER_PAIR, UPPER_LAST = (1, 0, 2), (2, 1, 0)
LOWER_PAIR, LOWER_LAST = (2, 1, 0), (0, 2, 1)
CHUNK_AXES = [
    UPPER_PAIR,
    (UPPER_PAIR[1], UPPER_PAIR[0], UPPER_PAIR[2]),
    UPPER_LAST,
    LOWER_PAIR,
    (LOWER_PAIR[1], LOWER_PAIR[0], LOWER_PAIR[2]),
    LOWER_LAST,
]
TAIL = (
    "Ub", "Lp", "Lq", "Um", "Ub", "Lb", "Lp", "Lq", "Ub", "Um", "Lb", "Ub", "Lm",
    "Lb", "Um", "Ub", "Lm", "Lb", "Ub", "Um", "Lb", "Lm", "Um", "Ub", "Lb", "Lm",
    "Up", "Uq", "Lb", "Ub", "Lm", "Lb", "Up", "Uq", "Lq", "Lp",
)


def on_device(
    tokens,
    skip_tokens,
    cot_back,
    cot_head,
    one_span,
    *params,
):
    lower = [params[i] for i in (0, 1, 4, 5)]
    upper = [params[i] for i in (8, 9, 12, 13)]
    device = lax.axis_index("dp") * 2 + lax.axis_index("tensor")
    ids = jnp.concatenate([device.astype(jnp.int32).reshape(1), one_span])
    tokens_other = swap(tokens)
    tokens, ids = lax.optimization_barrier((tokens, ids))
    vec = vectors([params[i] for i in (2, 3, 6, 7, 10, 11, 14, 15)])
    skip_other = swap(skip_tokens)
    cot_head_other = swap(cot_head)
    cot_back_other = swap(cot_back)
    order = Order()

    x_l, qkv_l, prob_l, ctx_l, part = attend_first(ids, tokens, tokens_other, lower)
    first_l, low_l, normed_al, inv_al, act_l, slope_l, part = feed(
        0, x_l, part, swap(part), vec, lower
    )
    x_u, normed_fl, inv_fl, backs, qkv_u, prob_u, ctx_u, part = attend_second(
        ids, first_l, part, swap(part), vec, skip_tokens, skip_other, upper
    )
    first_u, low_u, normed_au, inv_au, act_u, slope_u, part = feed(
        4, x_u, part, swap(part), vec, upper
    )
    head_out, gs_u, gs_low_u, norms_fu, grad_pre_u, part = feed_back_second(
        ids, first_u, part, swap(part), vec, cot_head, cot_head_other, slope_u, upper
    )
    pair_u, pair_l = Pair(order, UPPER_PAIR), Pair(order, LOWER_PAIR)
    theirs = swap(part)
    pair_u.start(0, *out_grad(0, ids, act_u, gs_low_u))
    pair_u.start(1, *in_grad(1, ids, low_u, order.hold(grad_pre_u)))
    resid_u, gr_low_u, norms_au, grad_qkv_u, part, _ = attend_back(
        4, ids, order.hold(gs_u), part, theirs, normed_au, inv_au, qkv_u, prob_u, vec=vec,
        weights=upper,
    )
    theirs = swap(part)
    at_u = Single(
        order, UPPER_LAST, *attend_grad(2, ids, x_u, grad_qkv_u, ctx_u, order.hold(gr_low_u))
    )
    pair_u.next(0)
    pair_u.next(1)
    grad_skip, gs_l, gs_low_l, norms_fl, grad_pre_l, part = feed_back_first(
        ids, normed_fl, inv_fl, vec, cot_back, cot_back_other, order.hold(resid_u), part,
        theirs, slope_l, lower,
    )
    theirs = swap(part)
    order.token = gs_low_l
    pair_u.next(0)
    pair_u.next(1)
    pair_l.start(0, *out_grad(3, ids, act_l, order.hold(gs_low_l)))
    pair_l.start(1, *in_grad(4, ids, low_l, order.hold(grad_pre_l)))
    at_u.next()
    resid_l, gr_low_l, norms_al, grad_qkv_l, part, away = attend_back(
        0, ids, order.hold(gs_l), part, theirs, normed_al, inv_al, qkv_l, prob_l, vec=vec,
        weights=lower,
    )
    at_l = Single(
        order, LOWER_LAST,
        *attend_grad(
            5, ids, x_l, grad_qkv_l, ctx_l, gr_low_l, (norms_al, norms_fl, norms_au, norms_fu)
        ),
    )
    act = {
        "Up": lambda: pair_u.next(0),
        "Uq": lambda: pair_u.next(1),
        "Um": pair_u.next_both,
        "Ub": at_u.next,
        "Lp": lambda: pair_l.next(0),
        "Lq": lambda: pair_l.next(1),
        "Lm": pair_l.next_both,
        "Lb": at_l.next,
    }
    for index, name in enumerate(TAIL):
        act[name]()
        if index == 16:
            away = swap(order.hold(away))
        if index == 21:
            grad_tokens, back_out = run(
                rows_kernel, [ids], [resid_l, part, order.hold(away), backs],
                [sds(HALF, D, dtype=F32), sds(HALF, D)], [pltpu.VMEM((ROWS, D), BF16)],
            )
            order.token = grad_tokens
    done_u = place(
        ids,
        [(0, 0), (0, 1), (1, 0), (1, 1), (2, 0), (2, 1)],
        [pair_u.keep[0], pair_u.got[0], pair_u.keep[1], pair_u.got[1], at_u.keep,
         order.hold(at_u.got)],
    )
    order.token = done_u[0]
    done_l = place(
        ids, [(3, 0), (4, 0), (5, 0)],
        [pair_l.keep[0], pair_l.keep[1], order.hold(at_l.keep)],
    )
    for chunk, got in ((5, at_l.got), (4, pair_l.got[1]), (3, pair_l.got[0])):
        done_l = place(ids, [(chunk, 1)], [got], done_l)
    norms = at_l.norm
    out_gu, in_gu, qkv_gu, proj_gu = done_u
    out_gl, in_gl, qkv_gl, proj_gl = done_l
    return (
        back_out,
        head_out,
        grad_tokens,
        grad_skip,
        qkv_gl,
        proj_gl,
        norms[0],
        norms[1],
        in_gl,
        out_gl,
        norms[2],
        norms[3],
        qkv_gu,
        proj_gu,
        norms[4],
        norms[5],
        in_gu,
        out_gu,
        norms[6],
        norms[7],
    )


def solution(mesh):
    rows = P(("dp", "tensor"), None)
    weights = (
        P(None, None, "tensor"),
        P("tensor", None),
        P(),
        P(),
        P(None, "tensor"),
        P("tensor", None),
        P(),
        P(),
    )
    return jax.shard_map(
        on_device,
        mesh=mesh,
        in_specs=(rows,) * 4 + (P("dp"),) + weights + weights,
        out_specs=(rows,) * 4 + weights + weights,
        check_vma=False,
    )
```

```python
import functools

import jax
import jax.numpy as jnp
from jax import lax
from jax.experimental import pallas as pl
from jax.experimental.pallas import tpu as pltpu
from jax.sharding import PartitionSpec as P

SPAN = 128
EPS = 1e-06
SCALE = 0.125
NEG = -1000000000.0

D = 768
ROWS = 768
HALF = ROWS // 2
HIDDEN = 1536
PIECE = 384
PAIR = 128
BLOCK = (48, 384)
F32 = jnp.float32
BF16 = jnp.bfloat16
SPANS_AT = 1

SWAP = [(0, 1), (1, 0)]


def dot_nn(left, right):
    return lax.dot_general(left, right, (((1,), (0,)), ((), ())), preferred_element_type=F32)


def dot_nt(left, right):
    return lax.dot_general(left, right, (((1,), (1,)), ((), ())), preferred_element_type=F32)


def dot_tn(left, right):
    return lax.dot_general(left, right, (((0,), (0,)), ((), ())), preferred_element_type=F32)


def normalize(resid):
    mean = jnp.mean(resid, axis=-1, keepdims=True)
    centered = resid - mean
    var = jnp.mean(centered * centered, axis=-1, keepdims=True)
    inv = lax.rsqrt(var + EPS)
    return centered * inv, inv


def norm_grad(grad_out, normed, inv, gain):
    grad = grad_out * gain
    first = jnp.mean(grad, axis=-1, keepdims=True)
    second = jnp.mean(grad * normed, axis=-1, keepdims=True)
    return inv * (grad - first - normed * second)


def fold(value):
    return jnp.sum(value.reshape(-1, 8, value.shape[-1]), axis=0)

DOC = 2 * SPAN
DOCS = ROWS // DOC


def side_of(ids_ref):
    return ids_ref[0] & 1


def chunk_bits(ids_ref, chunk):
    chip, core = ids_ref[0] >> 1, ids_ref[0] & 1
    bits = []
    for axis in CHUNK_AXES[chunk]:
        at = (chip >> (2 * axis)) & 3
        low, high = (at ^ (at >> 1)) & 1, at >> 1
        bits.append(low + core * (high - low))
    return bits


def doc_rows(doc):
    return slice(doc * DOC, (doc + 1) * DOC)


def half_rows(index):
    return pl.ds(pl.multiple_of(index * HALF, HALF), HALF)


def join_halves(side, own_ref, other_ref, full_ref):
    full_ref[half_rows(side), :] = own_ref[...]
    full_ref[half_rows(1 - side), :] = other_ref[...]


def doc_masks(ids_ref, doc):
    row = lax.broadcasted_iota(jnp.int32, (DOC, 1), 0)
    keep = jnp.where((row < SPAN) | (ids_ref[SPANS_AT + doc] == 0), 1.0, 0.0)
    return keep, (row & (SPAN - 1)) == 0


def spread(column):
    return jnp.broadcast_to(column, (column.shape[0], 128))


def head_masks():
    lane = lax.broadcasted_iota(jnp.int32, (1, PAIR), 1)
    return lane < 64


def both_heads(value, left):
    zero = jnp.zeros_like(value)
    return jnp.concatenate([jnp.where(left, value, zero), jnp.where(left, zero, value)], axis=0)


class Rows:
    def __init__(self, *refs):
        self.refs = refs

    def find(self, index):
        head = index[0] if isinstance(index, tuple) else index
        rest = index[1:] if isinstance(index, tuple) else ()
        at = head if isinstance(head, int) else head.start
        base = 0
        for ref in self.refs:
            if at < base + ref.shape[0]:
                break
            base += ref.shape[0]
        head = head - base if isinstance(head, int) else slice(at - base, head.stop - base)
        return ref, (head, *rest)

    def __getitem__(self, index):
        head = index[0] if isinstance(index, tuple) else index
        if head is Ellipsis or head == slice(None):
            return jnp.concatenate([ref[index] for ref in self.refs], axis=0)
        ref, index = self.find(index)
        return ref[index]


GROUPS = ((0, 1), (2,))


def attend(ids_ref, docs, x_ref, proj_ref, qkv_ref, prob_ref, ctx_ref, part_ref, wide, skip=0):
    for i, doc in enumerate(docs):
        at = doc_rows(i)
        out = dot_nn(x_ref[doc_rows(i + skip), :], wide[...])
        qkv_ref[at, :384] = (out[:, :384] * SCALE).astype(BF16)
        qkv_ref[at, 384:] = out[:, 384:].astype(BF16)
    left = head_masks()
    col = lax.broadcasted_iota(jnp.int32, (1, 2 * DOC), 1) & (DOC - 1)
    for i, doc in enumerate(docs):
        at = doc_rows(i)
        key_ok = (col < SPAN) | (ids_ref[SPANS_AT + doc] == 0)
        scores = []
        for pair in range(3):
            query = qkv_ref[at, pair * PAIR:(pair + 1) * PAIR]
            keys = qkv_ref[at, 384 + pair * PAIR:384 + (pair + 1) * PAIR]
            scores.append(jnp.where(key_ok, dot_nt(query, both_heads(keys, left)), NEG))
        for pair in range(3):
            probs = []
            for head in range(2):
                score = scores[pair][:, head * DOC:(head + 1) * DOC]
                raised = jnp.exp(score - jnp.max(score, axis=-1, keepdims=True))
                probs.append(
                    (raised * (1.0 / jnp.sum(raised, axis=-1, keepdims=True))).astype(BF16)
                )
            prob = jnp.concatenate(probs, axis=1)
            prob_ref[i, pair] = prob
            values = qkv_ref[at, 768 + pair * PAIR:768 + (pair + 1) * PAIR]
            mixed = dot_nn(prob, both_heads(values, left))
            ctx_ref[at, pair * PAIR:(pair + 1) * PAIR] = mixed.astype(BF16)
    for i, doc in enumerate(docs):
        at = doc_rows(i)
        part_ref[at, :] = dot_nn(ctx_ref[at, :], proj_ref[...]).astype(BF16)


def attend_first_kernel(
    docs, ids_ref, other_ref, own_ref, qkv_w_ref, proj_w_ref,
    x_ref, wide, proj, qkv_ref, prob_ref, ctx_ref, part_ref, sems,
):
    side = side_of(ids_ref)
    copies = [pltpu.make_async_copy(own_ref, x_ref.at[half_rows(side), :], sems.at[0])]
    for index in range(3):
        cut = slice(index * 384, (index + 1) * 384)
        copies.append(
            pltpu.make_async_copy(qkv_w_ref.at[index], wide.at[:, cut], sems.at[1 + index])
        )
    copies.append(pltpu.make_async_copy(proj_w_ref, proj, sems.at[4]))
    for copy in copies:
        copy.start()
    x_ref[half_rows(1 - side), :] = other_ref[...]
    for copy in copies:
        copy.wait()
    attend(ids_ref, docs, x_ref, proj, qkv_ref, prob_ref, ctx_ref, part_ref, wide)


def attend_more_kernel(
    docs, ids_ref, x_ref, wide_ref, proj_ref, qkv_ref, prob_ref, ctx_ref, part_ref,
):
    attend(
        ids_ref, docs, x_ref, proj_ref, qkv_ref, prob_ref, ctx_ref, part_ref, wide_ref, docs[0]
    )


def attend_second_kernel(
    docs, base, ids_ref, first_ref, mine_ref, theirs_ref, vec_ref, own_ref, other_ref,
    qkv_w_ref, proj_ref,
    x_ref, normed_ref, inv_ref, back_ref, qkv_ref, prob_ref, ctx_ref, part_ref, *rest,
):
    *wide_out, full = rest
    join_halves(side_of(ids_ref), own_ref, other_ref, full)
    for i, doc in enumerate(docs):
        at = doc_rows(i)
        keep, cls = doc_masks(ids_ref, doc)
        resid = first_ref[at, :] + mine_ref[at, :].astype(F32) + theirs_ref[at, :].astype(F32)
        normed, inv = normalize(resid)
        back = normed * vec_ref[base:base + 1, :] + vec_ref[base + 1:base + 2, :]
        normed_ref[at, :] = normed.astype(BF16)
        inv_ref[at, :] = spread(inv)
        x_ref[at, :] = jnp.where(cls, back, full[doc_rows(doc), :].astype(F32)).astype(BF16)
        back_ref[at, :] = (back * keep).astype(BF16)
    wide = qkv_w_ref
    if wide_out:
        wide = wide_out[0]
        for index in range(3):
            wide[:, index * 384:(index + 1) * 384] = qkv_w_ref[index]
    attend(ids_ref, docs, x_ref, proj_ref, qkv_ref, prob_ref, ctx_ref, part_ref, wide)


def feed_kernel(
    docs, skip, base, x_ref, mine_ref, theirs_ref, vec_ref, in_ref, out_w_ref,
    first_ref, low_ref, normed_ref, inv_ref, act_ref, slope_ref, part_ref,
):
    for i, doc in enumerate(docs):
        at = doc_rows(i)
        resid = x_ref[doc_rows(i + skip), :].astype(F32) + mine_ref[at, :].astype(F32)
        resid = resid + theirs_ref[at, :].astype(F32)
        normed, inv = normalize(resid)
        first = normed * vec_ref[base:base + 1, :] + vec_ref[base + 1:base + 2, :]
        normed_ref[at, :] = normed.astype(BF16)
        inv_ref[at, :] = spread(inv)
        first_ref[at, :] = first
        low_ref[at, :] = first.astype(BF16)
    for i, doc in enumerate(docs):
        at = doc_rows(i)
        for piece in range(3):
            cut = slice(piece * 512, (piece + 1) * 512)
            pre = dot_nn(low_ref[at, :], in_ref[:, cut])
            share = 0.5 * (1.0 + lax.erf(pre * 0.7071067811865476))
            density = jnp.exp(-0.5 * pre * pre) * 0.3989422804014327
            act_ref[at, cut] = (pre * share).astype(BF16)
            slope_ref[at, cut] = (share + pre * density).astype(BF16)
    for i, doc in enumerate(docs):
        at = doc_rows(i)
        part_ref[at, :] = dot_nn(act_ref[at, :], out_w_ref[...]).astype(BF16)


def feed_back(gs_low_ref, slope_ref, in_ref, out_w_ref, grad_pre_ref, part_ref):
    for doc in range(DOCS):
        at = doc_rows(doc)
        for piece in range(3):
            cut = slice(piece * 512, (piece + 1) * 512)
            grad_act = dot_nt(gs_low_ref[at, :], out_w_ref[cut, :])
            grad_pre_ref[at, cut] = (grad_act * slope_ref[at, cut].astype(F32)).astype(BF16)
    for doc in range(DOCS):
        at = doc_rows(doc)
        part_ref[at, :] = dot_nt(grad_pre_ref[at, :], in_ref[...]).astype(BF16)


def put_norm_grads(norms_ref, sums):
    gain, shift = sums
    norms_ref[...] = jnp.zeros_like(norms_ref)
    norms_ref[0:1, :] = jnp.sum(gain, axis=0, keepdims=True)
    norms_ref[1:2, :] = jnp.sum(shift, axis=0, keepdims=True)


def add_sums(sums, grad_out, normed):
    new = (fold(grad_out * normed), fold(grad_out))
    return new if sums is None else (sums[0] + new[0], sums[1] + new[1])


def feed_back_second_kernel(
    base, ids_ref, first_ref, mine_ref, theirs_ref, vec_ref, own_ref, other_ref,
    slope_ref, in_ref, out_w_ref,
    head_ref, gs_ref, gs_low_ref, norms_ref, grad_pre_ref, part_ref, cot, full,
):
    side = side_of(ids_ref)
    join_halves(side, own_ref, other_ref, cot)
    sums = None
    for doc in range(DOCS):
        at = doc_rows(doc)
        keep, _ = doc_masks(ids_ref, doc)
        resid = first_ref[at, :] + mine_ref[at, :].astype(F32) + theirs_ref[at, :].astype(F32)
        normed, inv = normalize(resid)
        head = normed * vec_ref[base:base + 1, :] + vec_ref[base + 1:base + 2, :]
        full[at, :] = (head * keep).astype(BF16)
        grad_out = cot[at, :].astype(F32) * keep
        grad = norm_grad(grad_out, normed, inv, vec_ref[base:base + 1, :])
        gs_ref[at, :] = grad
        gs_low_ref[at, :] = grad.astype(BF16)
        sums = add_sums(sums, grad_out, normed)
    head_ref[...] = full[half_rows(side), :]
    put_norm_grads(norms_ref, sums)
    feed_back(gs_low_ref, slope_ref, in_ref, out_w_ref, grad_pre_ref, part_ref)


def feed_back_first_kernel(
    base, ids_ref, normed_ref, inv_ref, vec_ref, own_ref, other_ref,
    resid_ref, mine_ref, theirs_ref, slope_ref, in_ref, out_w_ref,
    skip_ref, gs_ref, gs_low_ref, norms_ref, grad_pre_ref, part_ref, cot, full,
):
    side = side_of(ids_ref)
    join_halves(side, own_ref, other_ref, cot)
    sums = None
    for doc in range(DOCS):
        at = doc_rows(doc)
        keep, cls = doc_masks(ids_ref, doc)
        above = resid_ref[at, :] + mine_ref[at, :].astype(F32) + theirs_ref[at, :].astype(F32)
        full[at, :] = jnp.where(cls, 0.0, above)
        normed = normed_ref[at, :].astype(F32)
        grad_out = cot[at, :].astype(F32) * keep + jnp.where(cls, above, 0.0)
        grad = norm_grad(grad_out, normed, inv_ref[at, 0:1], vec_ref[base:base + 1, :])
        gs_ref[at, :] = grad
        gs_low_ref[at, :] = grad.astype(BF16)
        sums = add_sums(sums, grad_out, normed)
    skip_ref[...] = full[half_rows(side), :]
    put_norm_grads(norms_ref, sums)
    feed_back(gs_low_ref, slope_ref, in_ref, out_w_ref, grad_pre_ref, part_ref)


def attend_back_kernel(
    base, ids_ref, gs_ref, mine_ref, theirs_ref, normed_ref, inv_ref, vec_ref, qkv_ref, prob_ref,
    qkv_w_ref, proj_ref,
    resid_ref, low_ref, norms_ref, grad_qkv_ref, part_ref, away_ref, grad_ctx, wide,
):
    for index in range(3):
        wide[:, index * 384:(index + 1) * 384] = qkv_w_ref[index]
    sums = None
    for doc in range(DOCS):
        at = doc_rows(doc)
        grad_out = gs_ref[at, :] + mine_ref[at, :].astype(F32) + theirs_ref[at, :].astype(F32)
        normed = normed_ref[at, :].astype(F32)
        grad = norm_grad(grad_out, normed, inv_ref[at, 0:1], vec_ref[base:base + 1, :])
        resid_ref[at, :] = grad
        low_ref[at, :] = grad.astype(BF16)
        sums = add_sums(sums, grad_out, normed)
    put_norm_grads(norms_ref, sums)
    for doc in range(DOCS):
        at = doc_rows(doc)
        grad_ctx[at, :] = dot_nt(low_ref[at, :], proj_ref[...]).astype(BF16)
    left = head_masks()
    for doc in range(DOCS):
        at = doc_rows(doc)
        pairs = [slice(pair * PAIR, (pair + 1) * PAIR) for pair in range(3)]
        grad_probs = []
        for pair in range(3):
            values = qkv_ref[at, 768 + pair * PAIR:768 + (pair + 1) * PAIR]
            grad_probs.append(dot_nt(grad_ctx[at, pairs[pair]], both_heads(values, left)))
        for pair in range(3):
            prob_low = prob_ref[doc, pair]
            scored = []
            for head in range(2):
                cut = slice(head * DOC, (head + 1) * DOC)
                prob = prob_low[:, cut].astype(F32)
                grad_prob = grad_probs[pair][:, cut]
                inner = jnp.sum(grad_prob * prob, axis=-1, keepdims=True)
                scored.append((prob * (grad_prob - inner)).astype(BF16))
            grad_scores = jnp.concatenate(scored, axis=1)
            query = qkv_ref[at, pairs[pair]]
            keys = qkv_ref[at, 384 + pair * PAIR:384 + (pair + 1) * PAIR]
            grad_query = dot_nn(grad_scores, both_heads(keys, left)) * SCALE
            grad_keys = dot_tn(grad_scores, query)
            grad_values = dot_tn(prob_low, grad_ctx[at, pairs[pair]])
            grad_qkv_ref[at, pair * PAIR:(pair + 1) * PAIR] = grad_query.astype(BF16)
            for index, grad in ((1, grad_keys), (2, grad_values)):
                cut = slice(index * 384 + pair * PAIR, index * 384 + (pair + 1) * PAIR)
                grad_qkv_ref[at, cut] = jnp.where(left, grad[:DOC], grad[DOC:]).astype(BF16)
    for doc in range(DOCS):
        at = doc_rows(doc)
        part_ref[at, :] = dot_nt(grad_qkv_ref[at, :], wide[...]).astype(BF16)
    if base == 0:
        away_ref[...] = part_ref[half_rows(1 - side_of(ids_ref)), :]
    else:
        away_ref[...] = jnp.zeros_like(away_ref)


def rows_kernel(ids_ref, resid_ref, mine_ref, theirs_ref, back_ref, out_ref, back_out_ref, full):
    at = half_rows(side_of(ids_ref))
    out_ref[...] = resid_ref[at, :] + mine_ref[at, :].astype(F32) + theirs_ref[...].astype(F32)
    full[...] = back_ref[...]
    back_out_ref[...] = full[at, :]


def cut_wide(value, blocks, piece):
    for half in range(2):
        for k in range(8):
            blocks[piece, half, k] = value[k * 48:(k + 1) * 48, half * 384:(half + 1) * 384]


def cut_tall(value, blocks, piece):
    for half in range(2):
        for k in range(8):
            at = half * 384 + k * 48
            blocks[piece, half, k] = value[at:at + 48, :]


def put_blocks(ids_ref, turn, blocks, send_ref, keep_ref):
    first, second, third = chunk_bits(ids_ref, turn)
    for rel, ref in ((1, send_ref), (0, keep_ref)):
        for b in range(2):
            piece = 2 * (rel ^ first) + (b ^ second)
            for e in range(2):
                for k in range(8):
                    ref[16 * b + 8 * e + k] = blocks[piece, e ^ third, k]


def out_grad_kernel(turn, ids_ref, act_ref, gs_ref, send_ref, keep_ref, blocks):
    for p in range(2):
        value = dot_tn(act_ref[:, p * 768:(p + 1) * 768], gs_ref[...]).astype(BF16)
        cut_wide(value[:384], blocks, 2 * p)
        cut_wide(value[384:], blocks, 2 * p + 1)
    put_blocks(ids_ref, turn, blocks, send_ref, keep_ref)


def in_grad_kernel(turn, ids_ref, low_ref, grad_ref, send_ref, keep_ref, blocks):
    for p in range(2):
        value = dot_tn(low_ref[...], grad_ref[:, p * 768:(p + 1) * 768]).astype(BF16)
        cut_tall(value[:, :384], blocks, 2 * p)
        cut_tall(value[:, 384:], blocks, 2 * p + 1)
    put_blocks(ids_ref, turn, blocks, send_ref, keep_ref)


def attend_grad_kernel(turn, ids_ref, x_ref, grad_ref, ctx_ref, low_ref, *refs):
    norm_refs, (send_ref, keep_ref), blocks = refs[:-3 - (len(refs) > 3)], refs[-3:-1], refs[-1]
    if norm_refs:
        send_ref, keep_ref = refs[-4:-2]
        value = jnp.concatenate([ref[0:2, :] for ref in norm_refs], axis=0)
        refs[-2][...] = value
        send_ref[32] = norm_block(value)
    value = dot_tn(x_ref[...], grad_ref[...]).astype(BF16)
    for piece in range(3):
        cut_tall(value[:, piece * 384:(piece + 1) * 384], blocks, piece)
    cut_wide(dot_tn(ctx_ref[...], low_ref[...]).astype(BF16), blocks, 3)
    put_blocks(ids_ref, turn, blocks, send_ref, keep_ref)


def vectors_kernel(*refs):
    out_ref = refs[-1]
    for i in range(8):
        out_ref[i:i + 1, :] = refs[i][...].reshape(1, D)


def plus(one, two):
    return (one.astype(F32) + two.astype(F32)).astype(BF16)


def norm_block(value):
    high = value.astype(BF16)
    low = (value - high.astype(F32)).astype(BF16)
    rows = [high[:, :PIECE], high[:, PIECE:], low[:, :PIECE], low[:, PIECE:]]
    return jnp.concatenate(rows + [jnp.zeros((16, PIECE), BF16)], axis=0)


def block_norm(block):
    high = jnp.concatenate([block[0:8], block[8:16]], axis=1)
    low = jnp.concatenate([block[16:24], block[24:32]], axis=1)
    return high.astype(F32) + low.astype(F32)


def add_norm(value, block):
    return block_norm(norm_block(value)) + block_norm(block)


def split_kernel(sizes, with_norm, *refs):
    count = len(sizes)
    ins, outs = refs[:2 * count], refs[2 * count + with_norm:]
    at = 0
    for i, m in enumerate(sizes):
        keep, got = ins[2 * i], ins[2 * i + 1]
        outs[1][at:at + m] = plus(keep[:m], got[:m])
        outs[0][at:at + m] = plus(keep[m:], got[m:2 * m])
        at += m
    if with_norm:
        value = add_norm(refs[2 * count][...], ins[1][2 * sizes[0]])
        outs[0][at] = norm_block(value)
        outs[2][...] = value


def far_kernel(with_norm, *refs):
    if with_norm:
        keep, got, norm, out, norm_out = refs
        count = keep.shape[0] - (keep.shape[0] % 8)
        value = add_norm(norm[...], got[got.shape[0] - 1])
        out[count] = norm_block(value)
        norm_out[...] = value
    else:
        keep, got, out = refs
        count = keep.shape[0]
    out[:count] = plus(keep[:count], got[:count])


def join_kernel(count, held_ref, got_ref, *outs):
    size = outs[0].shape[0] // 2
    for i in range(count):
        at = slice(i * size, (i + 1) * size)
        outs[i][:size] = held_ref[at]
        outs[i][size:] = got_ref[at]


def place_kernel(items, ids_ref, *refs):
    ins, outs, squares, sems = refs[:len(items)], refs[-6:-2], refs[-2], refs[-1]
    slots = squares.shape[0]

    def copies(index, chunk, far, b, e):
        first, second, _ = chunk_bits(ids_ref, chunk)
        turn = chunk % 3
        slot = index % slots
        piece = 2 * (far ^ first) + (b ^ second)
        at = pl.ds(pl.multiple_of(piece * PIECE, PIECE), PIECE)
        cut = slice(e * PIECE, (e + 1) * PIECE)

        def copy(ref):
            return pltpu.make_async_copy(squares.at[slot], ref, sems.at[slot])

        if turn == 0:
            return [(None, copy(outs[0].at[at, cut]))]
        if turn == 1:
            return [(None, copy(outs[1].at[cut, at]))]
        return [
            (piece < 3, copy(outs[2].at[jnp.minimum(piece, 2), cut, :])),
            (piece == 3, copy(outs[3].at[:, cut])),
        ]

    def each(pairs, wait):
        for when, copy in pairs:
            def act(copy=copy):
                copy.wait() if wait else copy.start()

            if when is None:
                act()
            else:
                pl.when(when)(act)

    flight = []
    for (chunk, far), from_ref in zip(items, ins):
        third = chunk_bits(ids_ref, chunk)[2]
        for b in range(2):
            for e in range(2):
                index = len(flight)
                if index >= slots:
                    each(flight[index - slots], True)
                for k in range(8):
                    block = from_ref[16 * b + 8 * (e ^ third) + k]
                    squares[index % slots, k * 48:(k + 1) * 48, :] = block.astype(F32)
                flight.append(copies(index, chunk, far, b, e))
                each(flight[index], False)
    for pairs in flight[-slots:]:
        each(pairs, True)


def sds(*shape, dtype=BF16):
    return jax.ShapeDtypeStruct(shape, dtype)


SCALARS = pl.BlockSpec(memory_space=pltpu.SMEM)
LOCAL = pl.BlockSpec(memory_space=pltpu.VMEM)
REMOTE = pl.BlockSpec(memory_space=pl.ANY)
DISTANT = pl.BlockSpec(memory_space=pltpu.HBM)


COST = pl.CostEstimate(flops=2_000_000_000, bytes_accessed=1, transcendentals=0)
HEAVY = pl.CostEstimate(flops=8_000_000_000, bytes_accessed=10_000_000, transcendentals=0)
LIGHT = ("split_kernel", "far_kernel", "join_kernel", "vectors_kernel", "rows_kernel")


LIMITS = {
    "feed_back_second_kernel": 6,
    "feed_back_first_kernel": 8,
    "attend_back_kernel": 6,
    "rows_kernel": 6,
    "out_grad_kernel": 5,
    "in_grad_kernel": 5,
    "attend_grad_kernel": 5,
}


def run(kernel, scalars, arrays, outs, scratch, *fixed):
    name = kernel.__name__
    flat = [part for a in arrays for part in (a if isinstance(a, tuple) else (a,))]

    def grouped(*refs):
        refs = list(refs)
        ins = [refs.pop(0) for _ in scalars]
        for a in arrays:
            parts = [refs.pop(0) for _ in (a if isinstance(a, tuple) else (a,))]
            ins.append(Rows(*parts) if isinstance(a, tuple) else parts[0])
        kernel(*fixed, *ins, *refs)

    return pl.pallas_call(
        grouped,
        out_shape=list(outs),
        in_specs=[SCALARS] * len(scalars) + [LOCAL] * len(flat),
        out_specs=[LOCAL] * len(outs),
        scratch_shapes=scratch,
        compiler_params=pltpu.CompilerParams(vmem_limit_bytes=LIMITS.get(name, 4) * 2**20),
        cost_estimate=COST if name in LIGHT else HEAVY,
        name=name,
    )(*scalars, *flat)


WIDE = (D, 1152)


def attend_outs(docs):
    rows = DOC * len(docs)
    return [sds(rows, 1152), sds(len(docs), 3, DOC, 2 * DOC), sds(rows, PIECE), sds(rows, D)]


def stats(docs):
    return sds(DOC * len(docs), 128, dtype=F32)


def attend_first(ids, own, other, weights):
    docs = GROUPS[0]
    outs = [sds(ROWS, D), sds(*WIDE), sds(PIECE, D)] + attend_outs(docs)
    x, wide, proj, *one = pl.pallas_call(
        functools.partial(attend_first_kernel, docs),
        out_shape=outs,
        in_specs=[SCALARS, LOCAL] + [DISTANT] * 3,
        out_specs=[LOCAL] * len(outs),
        scratch_shapes=[pltpu.SemaphoreType.DMA((5,))],
        compiler_params=pltpu.CompilerParams(vmem_limit_bytes=44 * 2**20),
        cost_estimate=HEAVY,
        name="attend_first_kernel",
    )(ids, other, own, weights[0], weights[1])
    docs = GROUPS[1]
    two = run(attend_more_kernel, [ids], [x, wide, proj], attend_outs(docs), [], docs)
    return x, *zip(one, two)


def attend_second(ids, first, mine, theirs, vec, own, other, weights):
    results, wide = [], weights[0]
    for g, docs in enumerate(GROUPS):
        rows = DOC * len(docs)
        outs = [sds(rows, D), sds(rows, D), stats(docs), sds(rows, D)] + attend_outs(docs)
        made = run(
            attend_second_kernel, [ids],
            [first[g], mine[g], theirs[g], vec, own, other, wide, weights[1]],
            outs + ([sds(*WIDE)] if g == 0 else []), [pltpu.VMEM((ROWS, D), BF16)], docs, 2,
        )
        if g == 0:
            *made, wide = made
        results.append(made)
    return tuple(zip(*results))


def feed(base, x, mine, theirs, vec, weights):
    results = []
    for g, docs in enumerate(GROUPS):
        rows = DOC * len(docs)
        split_x = isinstance(x, tuple)
        results.append(run(
            feed_kernel, [],
            [x[g] if split_x else x, mine[g], theirs[g], vec, weights[2], weights[3]],
            [sds(rows, D, dtype=F32), sds(rows, D), sds(rows, D), stats(docs),
             sds(rows, HIDDEN), sds(rows, HIDDEN), sds(rows, D)],
            [], docs, 0 if split_x else docs[0], base,
        ))
    return tuple(zip(*results))


FEED_BACK_OUTS = [
    sds(ROWS, D, dtype=F32), sds(ROWS, D), sds(8, D, dtype=F32), sds(ROWS, HIDDEN), sds(ROWS, D),
]


def feed_back_second(ids, first, mine, theirs, vec, own, other, slope, weights):
    return run(
        feed_back_second_kernel, [ids],
        [first, mine, theirs, vec, own, other, slope, weights[2], weights[3]],
        [sds(HALF, D)] + FEED_BACK_OUTS,
        [pltpu.VMEM((ROWS, D), BF16), pltpu.VMEM((ROWS, D), BF16)], 6,
    )


def feed_back_first(ids, normed, inv, vec, own, other, resid, mine, theirs, slope, weights):
    return run(
        feed_back_first_kernel, [ids],
        [normed, inv, vec, own, other, resid, mine, theirs, slope, weights[2], weights[3]],
        [sds(HALF, D, dtype=F32)] + FEED_BACK_OUTS,
        [pltpu.VMEM((ROWS, D), BF16), pltpu.VMEM((ROWS, D), F32)], 2,
    )


def attend_back(base, ids, gs, mine, theirs, normed, inv, qkv, prob, vec, weights):
    return run(
        attend_back_kernel, [ids],
        [gs, mine, theirs, normed, inv, vec, qkv, prob, weights[0], weights[1]],
        [sds(ROWS, D, dtype=F32), sds(ROWS, D), sds(8, D, dtype=F32), sds(ROWS, 1152), sds(ROWS, D),
         sds(HALF if base == 0 else 16, D)],
        [pltpu.VMEM((ROWS, PIECE), BF16), pltpu.VMEM(WIDE, BF16)], base,
    )


SPLIT_OUTS = [sds(32, *BLOCK), sds(32, *BLOCK)]
BLOCKS = pltpu.VMEM((4, 2, 8) + BLOCK, BF16)


def out_grad(chunk, ids, act, gs_low):
    return run(out_grad_kernel, [ids], [act, gs_low], SPLIT_OUTS, [BLOCKS], chunk)


def in_grad(chunk, ids, low, grad_pre):
    return run(in_grad_kernel, [ids], [low, grad_pre], SPLIT_OUTS, [BLOCKS], chunk)


def attend_grad(chunk, ids, x, grad_qkv, ctx, low, norms=()):
    outs = SPLIT_OUTS
    if norms:
        outs = [sds(33, *BLOCK), sds(32, *BLOCK), sds(8, D, dtype=F32)]
    return run(
        attend_grad_kernel, [ids], [x, grad_qkv, ctx, low, *norms], outs, [BLOCKS], chunk
    )


def vectors(rows):
    return run(vectors_kernel, [], rows, [sds(8, D, dtype=F32)], [])[0]


def split(sources, norm=None):
    arrays = [a for pair in sources for a in pair]
    sizes = tuple(keep.shape[0] // 2 for keep, _ in sources)
    count = sum(sizes)
    outs = [sds(count + (norm is not None), *BLOCK), sds(count, *BLOCK)]
    if norm is not None:
        arrays, outs = arrays + [norm], outs + [sds(8, D, dtype=F32)]
    return run(split_kernel, [], arrays, outs, [], sizes, int(norm is not None))


def far_add(keep, got, norm=None):
    if norm is None:
        return run(far_kernel, [], [keep, got], [sds(*keep.shape)], [], 0)
    count = keep.shape[0] - keep.shape[0] % 8
    outs = [sds(count + 1, *BLOCK), sds(8, D, dtype=F32)]
    return run(far_kernel, [], [keep, got, norm], outs, [], 1)


def join(held, got, count=1):
    size = held.shape[0] // count
    return run(join_kernel, [], [held, got], [sds(2 * size, *BLOCK)] * count, [], count)


PLACED = [
    sds(HIDDEN, D, dtype=F32),
    sds(D, HIDDEN, dtype=F32),
    sds(3, D, PIECE, dtype=F32),
    sds(PIECE, D, dtype=F32),
]


def place(ids, items, values, into=()):
    return pl.pallas_call(
        functools.partial(place_kernel, tuple(items)),
        out_shape=PLACED,
        in_specs=[SCALARS] + [LOCAL] * len(values) + [REMOTE] * len(into),
        out_specs=[REMOTE] * 4,
        scratch_shapes=[pltpu.VMEM((6, PIECE, PIECE), F32), pltpu.SemaphoreType.DMA((6,))],
        input_output_aliases={1 + len(values) + i: i for i in range(len(into))},
        compiler_params=pltpu.CompilerParams(vmem_limit_bytes=6 * 2**20),
        cost_estimate=COST,
        name="place_kernel",
    )(ids, *values, *into)


def swap(value):
    if isinstance(value, tuple):
        one, two = [swap(part) for part in value]
        return lax.optimization_barrier((one, value[1]))[0], two
    return lax.ppermute(value, "tensor", SWAP)


def flip(chip, core, stage, axis):
    pos = [chip % 4, chip // 4 % 4, chip // 16]
    low = (core == 0) == (stage == 0)
    pos[axis] = pos[axis] ^ 1 if low else 3 - pos[axis]
    return pos[0] + 4 * pos[1] + 16 * pos[2]


def exchange(value, stage, axis):
    pairs = [
        (2 * chip + core, 2 * flip(chip, core, stage, axis) + core)
        for chip in range(64)
        for core in range(2)
    ]
    return lax.ppermute(value, ("dp", "tensor"), pairs)


class Order:
    def __init__(self):
        self.token = None

    def hold(self, value):
        if self.token is None:
            return value
        return lax.optimization_barrier((value, self.token))[0]


class Single:
    def __init__(self, order, axes, send, keep, norm=None):
        self.order, self.axes, self.keep, self.norm, self.round = order, axes, keep, norm, 0
        self.send(send, 0, 0)

    def send(self, value, stage, j):
        self.order.token = value
        self.got = exchange(value, stage, self.axes[j % 3])

    def next(self):
        self.round += 1
        got = self.order.hold(self.got)
        if self.round > 8:
            self.got = self.order.token = got
            return
        if self.round < 3:
            value, self.keep, *norm = split([(self.keep, got)], self.norm)
            self.send(value, 0, self.round)
        elif self.round < 6:
            self.keep, *norm = far_add(self.keep, got, self.norm)
            self.send(self.keep, 1, self.round)
        elif self.round == 6:
            self.keep, *norm = far_add(self.keep, got, self.norm)
            if norm:
                self.keep = self.keep[:8]
            self.send(self.keep, 0, 2)
        else:
            norm = ()
            self.keep = join(self.keep, got)[0]
            self.send(self.keep, 0, 8 - self.round)
        if norm:
            self.norm = norm[0]


class Pair:
    def __init__(self, order, axes):
        self.order, self.axes = order, axes
        self.keep, self.got, self.calls = [None, None], [None, None], [0, 0]
        self.both = 2

    def start(self, i, send, keep):
        self.keep[i] = keep
        self.send(i, send, 0)

    def send(self, i, value, j):
        self.order.token = value
        self.got[i] = exchange(value, 0, self.axes[i ^ j])

    def next(self, i):
        self.calls[i] += 1
        if self.calls[i] == 1:
            value, self.keep[i] = split([(self.keep[i], self.order.hold(self.got[i]))])
            self.send(i, value, 1)
        elif self.calls[i] == 2 and self.calls[1 - i] == 2:
            got = [self.order.hold(g) for g in self.got]
            value, self.held = split([(self.keep[0], got[0]), (self.keep[1], got[1])])
            self.order.token = value
            self.arrived = exchange(value, 0, self.axes[2])
        elif self.calls[i] == 3:
            self.keep[i] = join(self.keep[i], self.order.hold(self.got[i]))[0]
            self.send(i, self.keep[i], 0)
        elif self.calls[i] == 4:
            self.got[i] = self.order.token = self.order.hold(self.got[i])

    def next_both(self):
        got = self.order.hold(self.arrived)
        self.both += 1
        if self.both <= 6:
            self.held = far_add(self.held, got)[0]
            self.order.token = self.held
            if self.both < 6:
                self.arrived = exchange(self.held, 1, self.axes[self.both - 3])
            else:
                self.arrived = exchange(self.held, 0, self.axes[2])
        else:
            self.keep = list(join(self.held, got, 2))
            for i in range(2):
                self.send(i, self.keep[i], 1)


UPPER_PAIR, UPPER_LAST = (1, 0, 2), (2, 1, 0)
LOWER_PAIR, LOWER_LAST = (2, 1, 0), (0, 2, 1)
CHUNK_AXES = [
    UPPER_PAIR,
    (UPPER_PAIR[1], UPPER_PAIR[0], UPPER_PAIR[2]),
    UPPER_LAST,
    LOWER_PAIR,
    (LOWER_PAIR[1], LOWER_PAIR[0], LOWER_PAIR[2]),
    LOWER_LAST,
]
TAIL = (
    "Ub", "Lp", "Lq", "Um", "Ub", "Lb", "Lp", "Lq", "Ub", "Um", "Lb", "Ub", "Lm",
    "Lb", "Um", "Ub", "Lm", "Lb", "Ub", "Um", "Lb", "Lm", "Um", "Ub", "Lb", "Lm",
    "Up", "Uq", "Lb", "Ub", "Lm", "Lb", "Up", "Uq", "Lq", "Lp",
)


def on_device(
    tokens,
    skip_tokens,
    cot_back,
    cot_head,
    one_span,
    *params,
):
    lower = [params[i] for i in (0, 1, 4, 5)]
    upper = [params[i] for i in (8, 9, 12, 13)]
    device = lax.axis_index("dp") * 2 + lax.axis_index("tensor")
    ids = jnp.concatenate([device.astype(jnp.int32).reshape(1), one_span])
    tokens_other = swap(tokens)
    tokens, ids = lax.optimization_barrier((tokens, ids))
    vec = vectors([params[i] for i in (2, 3, 6, 7, 10, 11, 14, 15)])
    skip_other = swap(skip_tokens)
    cot_head_other = swap(cot_head)
    cot_back_other = swap(cot_back)
    order = Order()

    x_l, qkv_l, prob_l, ctx_l, part = attend_first(ids, tokens, tokens_other, lower)
    first_l, low_l, normed_al, inv_al, act_l, slope_l, part = feed(
        0, x_l, part, swap(part), vec, lower
    )
    x_u, normed_fl, inv_fl, backs, qkv_u, prob_u, ctx_u, part = attend_second(
        ids, first_l, part, swap(part), vec, skip_tokens, skip_other, upper
    )
    first_u, low_u, normed_au, inv_au, act_u, slope_u, part = feed(
        4, x_u, part, swap(part), vec, upper
    )
    head_out, gs_u, gs_low_u, norms_fu, grad_pre_u, part = feed_back_second(
        ids, first_u, part, swap(part), vec, cot_head, cot_head_other, slope_u, upper
    )
    pair_u, pair_l = Pair(order, UPPER_PAIR), Pair(order, LOWER_PAIR)
    theirs = swap(part)
    pair_u.start(0, *out_grad(0, ids, act_u, gs_low_u))
    pair_u.start(1, *in_grad(1, ids, low_u, order.hold(grad_pre_u)))
    resid_u, gr_low_u, norms_au, grad_qkv_u, part, _ = attend_back(
        4, ids, order.hold(gs_u), part, theirs, normed_au, inv_au, qkv_u, prob_u, vec=vec,
        weights=upper,
    )
    theirs = swap(part)
    at_u = Single(
        order, UPPER_LAST, *attend_grad(2, ids, x_u, grad_qkv_u, ctx_u, order.hold(gr_low_u))
    )
    pair_u.next(0)
    pair_u.next(1)
    grad_skip, gs_l, gs_low_l, norms_fl, grad_pre_l, part = feed_back_first(
        ids, normed_fl, inv_fl, vec, cot_back, cot_back_other, order.hold(resid_u), part,
        theirs, slope_l, lower,
    )
    theirs = swap(part)
    order.token = gs_low_l
    pair_u.next(0)
    pair_u.next(1)
    pair_l.start(0, *out_grad(3, ids, act_l, order.hold(gs_low_l)))
    pair_l.start(1, *in_grad(4, ids, low_l, order.hold(grad_pre_l)))
    at_u.next()
    resid_l, gr_low_l, norms_al, grad_qkv_l, part, away = attend_back(
        0, ids, order.hold(gs_l), part, theirs, normed_al, inv_al, qkv_l, prob_l, vec=vec,
        weights=lower,
    )
    at_l = Single(
        order, LOWER_LAST,
        *attend_grad(
            5, ids, x_l, grad_qkv_l, ctx_l, gr_low_l, (norms_al, norms_fl, norms_au, norms_fu)
        ),
    )
    act = {
        "Up": lambda: pair_u.next(0),
        "Uq": lambda: pair_u.next(1),
        "Um": pair_u.next_both,
        "Ub": at_u.next,
        "Lp": lambda: pair_l.next(0),
        "Lq": lambda: pair_l.next(1),
        "Lm": pair_l.next_both,
        "Lb": at_l.next,
    }
    for index, name in enumerate(TAIL):
        act[name]()
        if index == 16:
            away = swap(order.hold(away))
        if index == 21:
            grad_tokens, back_out = run(
                rows_kernel, [ids], [resid_l, part, order.hold(away), backs],
                [sds(HALF, D, dtype=F32), sds(HALF, D)], [pltpu.VMEM((ROWS, D), BF16)],
            )
            order.token = grad_tokens
    done_u = place(
        ids,
        [(0, 0), (0, 1), (1, 0), (1, 1), (2, 0), (2, 1)],
        [pair_u.keep[0], pair_u.got[0], pair_u.keep[1], pair_u.got[1], at_u.keep,
         order.hold(at_u.got)],
    )
    order.token = done_u[0]
    done_l = place(
        ids, [(3, 0), (4, 0), (5, 0)],
        [pair_l.keep[0], pair_l.keep[1], order.hold(at_l.keep)],
    )
    for chunk, got in ((5, at_l.got), (4, pair_l.got[1]), (3, pair_l.got[0])):
        done_l = place(ids, [(chunk, 1)], [got], done_l)
    norms = at_l.norm
    out_gu, in_gu, qkv_gu, proj_gu = done_u
    out_gl, in_gl, qkv_gl, proj_gl = done_l
    return (
        back_out,
        head_out,
        grad_tokens,
        grad_skip,
        qkv_gl,
        proj_gl,
        norms[0],
        norms[1],
        in_gl,
        out_gl,
        norms[2],
        norms[3],
        qkv_gu,
        proj_gu,
        norms[4],
        norms[5],
        in_gu,
        out_gu,
        norms[6],
        norms[7],
    )


def solution(mesh):
    rows = P(("dp", "tensor"), None)
    weights = (
        P(None, None, "tensor"),
        P("tensor", None),
        P(),
        P(),
        P(None, "tensor"),
        P("tensor", None),
        P(),
        P(),
    )
    return jax.shard_map(
        on_device,
        mesh=mesh,
        in_specs=(rows,) * 4 + (P("dp"),) + weights + weights,
        out_specs=(rows,) * 4 + weights + weights,
        check_vma=False,
    )
```
